32 devices in a mesh: face: 4 (over z), strip: 8 (over y, x, core).
Axes of the slice: x: 2, y: 2, z: 4, core: 2. Of those that a mesh axis runs over, the one named last changes fastest.
Arguments:
- pixels_in: bfloat16 [4, 8, 64, 1024], P('face', 'strip'), may hold values from -6 to 6
- w_qkv: bfloat16 [1024, 3072], P(None, 'face'), may hold values from -0.1875 to 0.1875
- w_gate: bfloat16 [1024, 32], P(None, 'face'), may hold values from -0.1875 to 0.1875
- decay_rate: float32 [16], replicated, may hold values from 0.0005859375 to 0.05
- beta_bias: float32 [16], replicated, may hold values from -4 to 1
Outputs:
- mixed: bfloat16 [4, 8, 64, 1024], P('face', 'strip')
The draws below stay inside these ranges and needn't reach their ends.
All inputs are finite; a program needn't handle non-finite values.
Results may differ from the reference program's by a relative error of at most 0.0069.
Values may be sent and summed in bfloat16 or wider, within the bound.
A program may use at most 192 MiB of HBM per device.

```python
import math
import jax
import jax.numpy as jnp
from jax import lax

D = 1024
H = 16
DK = 64
FACE_ROWS = 8
FACE_COLS = 64
FACES = 4
HV = 1024


def shard_levels(rng, shape, shards, low, top_value):
    gain, own = 1.0, jax.random.fold_in(rng, 6)
    for dim, blocks in shards:
        heights = jnp.exp(jax.random.uniform(jax.random.fold_in(own, dim), (blocks,), jnp.float32, low / len(shards), top_value / len(shards)))
        gain = gain * jnp.repeat(heights, shape[dim] // blocks).reshape([-1 if axis == dim else 1 for axis in range(len(shape))])
    return gain


def gaussian(key, dims, scale, most, split=(), kind=jnp.bfloat16):
    values = scale * jax.random.normal(key, dims, jnp.float32)
    if split:
        values = values * shard_levels(key, dims, split, -0.22, 0.18)
    return jnp.clip(values, -most, most).astype(kind)


def setup_inputs(seed: int = 0) -> dict:
    key_of = jax.random.split(jax.random.key(seed), 6)
    pixels_in = gaussian(key_of[0], (FACES, FACE_ROWS, FACE_COLS, D), 1.0, 6.0, ((0, 4), (1, 8)))
    w_qkv = gaussian(key_of[1], (D, 3 * H * DK), D ** -0.5, 0.1875, ((1, 4),))
    w_gate = gaussian(key_of[2], (D, 2 * H), D ** -0.5, 0.1875, ((1, 4),))
    decay_rate = jnp.clip(jnp.exp(jax.random.uniform(key_of[3], (H,), jnp.float32, math.log(0.0005859375), math.log(0.05))), 0.0005859375, 0.05)
    beta_bias = jnp.clip(jax.random.uniform(key_of[4], (H,), jnp.float32, -4.0, 1.0), -4.0, 1.0)
    return dict(pixels_in=pixels_in, w_qkv=w_qkv, w_gate=w_gate, decay_rate=decay_rate, beta_bias=beta_bias)


highest = lax.Precision.HIGHEST

def unit_rows(tensor):
    return tensor / jnp.sqrt(lax.optimization_barrier(jnp.sum(tensor * tensor, axis=-1, keepdims=True)) + 1e-06)

def head_norm(tensor):
    normed = tensor / jnp.sqrt(lax.optimization_barrier(jnp.mean(tensor * tensor, axis=-1, keepdims=True)) + 1e-06)
    return normed.reshape(tensor.shape[0], -1)

def project(flat_px, w_qkv, w_gate):
    projected = jnp.dot(flat_px.astype(jnp.float32), w_qkv.astype(jnp.float32), preferred_element_type=jnp.float32).astype(jnp.bfloat16)
    gate_logits = jnp.dot(flat_px.astype(jnp.float32), w_gate.astype(jnp.float32), preferred_element_type=jnp.float32).astype(jnp.bfloat16)
    return (projected, gate_logits)

def unpack(projected, gate_logits, decay_rate, beta_bias):
    heads = decay_rate.shape[0]
    count = projected.shape[0]
    parts = projected.astype(jnp.float32).reshape(count, 3, heads, -1)
    logits = gate_logits.astype(jnp.float32)
    log_decay = -decay_rate[None, :] * jnp.exp(logits[:, :heads])
    strength = jax.nn.sigmoid(logits[:, heads:] + beta_bias[None, :])
    return (unit_rows(parts[:, 0]), unit_rows(parts[:, 1]), parts[:, 2], log_decay, strength)

def group_terms(queries, key_rows, val_rows, log_decay, strength):
    span = queries.shape[1]
    width = queries.shape[2]
    cumulative = jnp.cumsum(log_decay, axis=1)
    gap_log = cumulative[:, :, None] - cumulative[:, None, :]
    row_ids = lax.broadcasted_iota(jnp.int32, (span, span), 0)
    col_ids = lax.broadcasted_iota(jnp.int32, (span, span), 1)
    inclusive = row_ids >= col_ids
    strict = row_ids > col_ids
    within = jnp.where(inclusive, jnp.exp(jnp.where(inclusive, gap_log, 0.0)), 0.0)
    key_dot = jnp.einsum('hck,hjk->hcj', key_rows, key_rows, precision=highest)
    lower_part = jnp.where(strict, within * key_dot, 0.0) * strength[:, :, None]
    system = lower_part + jnp.eye(span, dtype=queries.dtype)
    scale_all = jnp.exp(cumulative)
    rhs_values = val_rows * strength[:, :, None]
    rhs_keys = key_rows * (strength * scale_all)[:, :, None]
    solved = lax.linalg.triangular_solve(system, jnp.concatenate([rhs_values, rhs_keys], axis=-1), left_side=True, lower=True, unit_diagonal=True)
    new_values = solved[..., :width]
    mixing = solved[..., width:]
    scores = jnp.where(inclusive, within * jnp.einsum('hck,hjk->hcj', queries, key_rows, precision=highest), 0.0)
    tail_decay = jnp.exp(cumulative[:, -1:] - cumulative)
    weighted_keys = key_rows * tail_decay[:, :, None]
    end_scale = jnp.exp(cumulative[:, -1])
    transition = end_scale[:, None, None] * jnp.eye(width, dtype=queries.dtype) - jnp.einsum('hck,hcj->hkj', mixing, weighted_keys, precision=highest)
    writes = jnp.einsum('hcv,hck->hvk', new_values, weighted_keys, precision=highest)
    effective_query = queries * scale_all[:, :, None] - jnp.einsum('hcj,hjk->hck', scores, mixing, precision=highest)
    local_out = jnp.einsum('hcj,hjv->hcv', scores, new_values, precision=highest)
    return (local_out, effective_query, transition, writes)

def to_blocks(queries, key_rows, val_rows, log_decay, strength):
    count = queries.shape[0] // 64

    def shape_four(tensor):
        return tensor.reshape(count, 64, tensor.shape[1], tensor.shape[2]).transpose(0, 2, 1, 3)

    def shape_three(tensor):
        return tensor.reshape(count, 64, tensor.shape[1]).transpose(0, 2, 1)
    return (shape_four(queries), shape_four(key_rows), shape_four(val_rows), shape_three(log_decay), shape_three(strength))

def from_blocks(outputs):
    count, heads, span, width = outputs.shape
    return outputs.transpose(0, 2, 1, 3).reshape(count * span, heads, width)

def sequence_scan(queries, key_rows, val_rows, log_decay, strength):
    blocks = to_blocks(queries, key_rows, val_rows, log_decay, strength)
    heads = queries.shape[1]
    width = queries.shape[2]

    def advance(carry_state, block_in):
        local_out, effective_query, transition, writes = group_terms(*block_in)
        outputs = local_out + jnp.einsum('hck,hvk->hcv', effective_query, carry_state, precision=highest)
        carry_state = jnp.einsum('hvk,hkj->hvj', carry_state, transition, precision=highest) + writes
        return (carry_state, outputs)
    start = jnp.zeros((heads, width, width), queries.dtype)
    _, outputs = lax.scan(advance, start, blocks)
    return from_blocks(outputs)

def reference(pixels_in, w_qkv, w_gate, decay_rate, beta_bias):

    def column_order(tensor):
        rest = tensor.shape[1:]
        return tensor.reshape((FACE_ROWS, FACE_COLS) + rest).swapaxes(0, 1).reshape((FACE_ROWS * FACE_COLS,) + rest)

    def one_face(face_px):
        flat_px = face_px.reshape(FACE_ROWS * FACE_COLS, D)
        projected, gate_logits = project(flat_px, w_qkv, w_gate)
        unpacked = unpack(projected, gate_logits, decay_rate, beta_bias)
        row_out = sequence_scan(*unpacked)
        col_out = sequence_scan(*[column_order(tensor) for tensor in unpacked])
        col_mixed = head_norm(col_out).astype(jnp.bfloat16)
        col_rowwise = col_mixed.reshape(FACE_COLS, FACE_ROWS, HV).swapaxes(0, 1).reshape(FACE_ROWS * FACE_COLS, HV)
        mixed = (head_norm(row_out) + col_rowwise.astype(jnp.float32)).astype(jnp.bfloat16)
        return mixed.reshape(FACE_ROWS, FACE_COLS, HV)
    return lax.map(one_face, pixels_in)
```

```python
import functools

import jax
import jax.numpy as jnp
from jax import lax
from jax.experimental import pallas as pl
from jax.experimental.pallas import tpu as pltpu
from jax.sharding import PartitionSpec as P

MESH = pl.DeviceIdType.MESH
f32 = jnp.float32
bf16 = jnp.bfloat16


def group_of(place, strips, groups):
    rep = strips // groups
    if rep > 1 or groups % 2:
        return place // rep
    return jnp.where(lax.rem(place, 2) == 0, place // 2, groups - 1 - place // 2)


def project_kernel(
    cfg, px_ref, wq_ref, wg_ref, slabs_ref, gates_ref,
    px_all, wbuf, wg_own, wg_all, acc, px_send, px_fwd, px_recv, w_send, w_recv, g_send, g_recv,
):
    faces, strips, groups, n_slab, pieces = cfg
    me_f, me_s = lax.axis_index("face"), lax.axis_index("strip")
    block, features = px_ref.shape
    count = strips * block
    width = wbuf.shape[2]
    chips = strips // 2
    core, chip = lax.rem(me_s, 2), me_s // 2
    partner = chip * 2 + (1 - core)
    group = group_of(me_s, strips, groups)
    depth = features // pieces

    def chip_at(step):
        return lax.rem(chip + step, chips) * 2 + core

    barrier = pltpu.get_barrier_semaphore()

    def greet(face, strip):
        pl.semaphore_signal(barrier, inc=1, device_id=(face, strip), device_id_type=MESH)

    greet(me_f, partner)
    for step in range(1, chips):
        greet(me_f, chip_at(step))
    for step in range(1, faces):
        greet(lax.rem(me_f + step, faces), me_s)

    wg_own[...] = wg_ref[...].astype(f32)

    def rows_of(strip):
        return px_all.at[pl.ds(pl.multiple_of(strip * block, block), block)]

    own_px = pltpu.make_async_copy(px_ref, rows_of(me_s), px_recv.at[me_s])
    own_px.start()
    pl.semaphore_wait(barrier, 1 + chips - 1 + faces - 1)

    def weight_from(kind):
        slab = kind * groups + group
        return slab // n_slab, lax.rem(slab, n_slab)

    def weight_src(j, p):
        rows = pl.ds(p * depth, depth)
        if len(wq_ref.shape) == 3:
            return wq_ref.at[j, rows]
        return wq_ref.at[rows, pl.ds(pl.multiple_of(j * width, width), width)]

    def weight_copy(kind, p, src, side):
        return pltpu.make_async_remote_copy(
            src_ref=src,
            dst_ref=wbuf.at[kind, pl.ds(p * depth, depth)],
            send_sem=w_send.at[kind, p, side],
            recv_sem=w_recv.at[kind, p],
            device_id=(me_f + (1 if side else -1), me_s),
            device_id_type=MESH,
        )

    def own_weight(kind, p, j):
        return pltpu.make_async_copy(
            weight_src(j, p), wbuf.at[kind, pl.ds(p * depth, depth)], w_recv.at[kind, p]
        )

    for p in range(pieces):
        for kind in range(3):
            owner, j = weight_from(kind)

            @pl.when(owner == me_f)
            def _(kind=kind, p=p, j=j):
                pl.when(me_f + 1 < faces)(weight_copy(kind, p, weight_src(j, p), 1).start)
                pl.when(me_f > 0)(weight_copy(kind, p, weight_src(j, p), 0).start)
                own_weight(kind, p, j).start()

    def px_copy(dest, sem, source, src):
        return pltpu.make_async_remote_copy(
            src_ref=src,
            dst_ref=rows_of(source),
            send_sem=sem,
            recv_sem=px_recv.at[source],
            device_id=(me_f, dest),
            device_id_type=MESH,
        )

    def px_out(step):
        return px_copy(chip_at(step), px_send.at[step], me_s, px_ref)

    def px_pass(step):
        source = chip_at(step)
        return px_copy(partner, px_fwd.at[step], source, rows_of(source))

    to_partner = px_copy(partner, px_send.at[0], me_s, px_ref)
    for step in range(1, chips):
        px_out(step).start()
    to_partner.start()

    def gate_copy(step):
        return pltpu.make_async_remote_copy(
            src_ref=wg_own,
            dst_ref=wg_all.at[me_f],
            send_sem=g_send.at[step],
            recv_sem=g_recv.at[me_f],
            device_id=(lax.rem(me_f + step, faces), me_s),
            device_id_type=MESH,
        )

    for step in range(1, faces):
        gate_copy(step).start()
    own_gate = pltpu.make_async_copy(wg_own, wg_all.at[me_f], g_recv.at[me_f])
    own_gate.start()

    def px_wait(strip):
        pltpu.make_async_copy(px_ref, rows_of(strip), px_recv.at[strip]).wait()

    def pass_pixels(step):
        px_wait(chip_at(step))
        px_pass(step).start()

    def pass_weights(p):
        for kind in range(3):
            owner, _ = weight_from(kind)
            here = wbuf.at[kind, pl.ds(p * depth, depth)]
            pltpu.make_async_copy(here, here, w_recv.at[kind, p]).wait()
            pl.when((owner < me_f) & (me_f + 1 < faces))(weight_copy(kind, p, here, 1).start)
            pl.when((owner > me_f) & (me_f > 0))(weight_copy(kind, p, here, 0).start)

    tile = min(512, count)

    def each_tile(body):
        if count == tile:
            body(pl.ds(0, tile), 0)
        else:

            def one(i, carry):
                body(pl.ds(pl.multiple_of(i * tile, tile), tile), i)
                return carry

            lax.fori_loop(0, count // tile, one, 0)

    def multiply(p):
        rows = pl.ds(p * depth, depth)
        weights = jnp.concatenate([wbuf[kind, rows, :] for kind in range(3)], axis=1)

        def body(at, _):
            term = jnp.dot(px_all[at, rows], weights, preferred_element_type=f32)
            if p > 0:
                term = term + acc[at, :]
            if p < pieces - 1:
                acc[at, :] = term
            else:
                for kind in range(3):
                    slabs_ref[kind, at, :] = term[
                        :, kind * width : (kind + 1) * width
                    ].astype(bf16)

        each_tile(body)

    for turn in range(max(pieces - 1, chips - 1)):
        if turn < pieces - 1:
            pass_weights(turn)
        if turn < chips - 1:
            pass_pixels(turn + 1)
    px_wait(me_s)
    px_wait(partner)
    for step in range(1, chips):
        px_wait(lax.rem(chip + step, chips) * 2 + (1 - core))
    for face in range(faces):
        pltpu.make_async_copy(wg_own, wg_all.at[face], g_recv.at[face]).wait()
    gate_w = jnp.concatenate([wg_all[face] for face in range(faces)], axis=0).astype(bf16)

    chunk = gates_ref.shape[2]

    def gate_body(at, i):
        logits = lax.dot_general(
            gate_w, px_all[at, :], (((1,), (1,)), ((), ())), preferred_element_type=f32
        )
        logits = logits.astype(bf16).astype(f32)
        for c in range(tile // chunk):
            gates_ref[i * (tile // chunk) + c] = logits[:, c * chunk : (c + 1) * chunk]

    each_tile(gate_body)
    for p in range(pieces - 1):
        multiply(p)
    pass_weights(pieces - 1)
    multiply(pieces - 1)

    to_partner.wait_send()
    for step in range(1, chips):
        px_out(step).wait_send()
        px_pass(step).wait_send()
    for step in range(1, faces):
        gate_copy(step).wait_send()
    for p in range(pieces):
        for kind in range(3):
            owner, _ = weight_from(kind)
            here = wbuf.at[kind, pl.ds(p * depth, depth)]
            pl.when((owner <= me_f) & (me_f + 1 < faces))(
                weight_copy(kind, p, here, 1).wait_send
            )
            pl.when((owner >= me_f) & (me_f > 0))(weight_copy(kind, p, here, 0).wait_send)


def mm(a, b, dims=((1,), (0,))):
    return lax.dot_general(
        a.astype(bf16), b.astype(bf16), (dims, ((), ())), preferred_element_type=f32
    )


def split_mm(exact, wide, pieces):
    exact = exact.astype(bf16)
    total, rest = None, wide
    for _ in range(pieces):
        piece = rest.astype(bf16)
        rest = rest - piece.astype(f32)
        term = jnp.dot(exact, piece, preferred_element_type=f32)
        total = term if total is None else total + term
    return total


def mm_split(wide, exact, pieces):
    exact = exact.astype(bf16)
    total, rest = None, wide
    for _ in range(pieces):
        piece = rest.astype(bf16)
        rest = rest - piece.astype(f32)
        term = jnp.dot(piece, exact, preferred_element_type=f32)
        total = term if total is None else total + term
    return total


def scan_kernel(
    cfg, first_ref, slabs_ref, gates_ref, rate_ref, bias_ref, out_ref,
    feats, gates, row_buf, col_buf, states,
):
    chunk, per_group, tall, wide, dk = cfg
    count, width = slabs_ref.shape[1:]
    strips, block, _ = out_ref.shape
    heads = gates_ref.shape[1] // 2
    first = first_ref[0]

    lane = lax.broadcasted_iota(jnp.int32, (width, width), 1)
    sub = lax.broadcasted_iota(jnp.int32, (width, width), 0)
    same_head = (lane // dk) == (sub // dk)
    head_ones = same_head.astype(f32)
    ti = lax.broadcasted_iota(jnp.int32, (chunk, chunk), 0)
    tj = lax.broadcasted_iota(jnp.int32, (chunk, chunk), 1)
    inclusive = ti >= tj
    tri = inclusive.astype(f32)
    eye = (ti == tj).astype(f32)

    def prepare(i, carry):
        at = pl.ds(pl.multiple_of(i * chunk, chunk), chunk)
        for kind in range(3):
            x = slabs_ref[kind, at, :].astype(f32)
            if kind < 2:
                x = x * lax.rsqrt(mm_split(x * x, head_ones, 2) + 1e-06)
            feats[kind, at, :] = x
        for a in range(per_group):
            head = first + a
            decay = -rate_ref[head] * jnp.exp(gates_ref[i, pl.ds(head, 1), :])
            strength = jax.nn.sigmoid(gates_ref[i, pl.ds(heads + head, 1), :] + bias_ref[head])
            gates[a, at, :] = jnp.broadcast_to(decay, (chunk, chunk)).T
            gates[per_group + a, at, :] = jnp.broadcast_to(strength, (chunk, chunk)).T
        return carry

    lax.fori_loop(0, count // chunk, prepare, 0, unroll=count // chunk <= 4)

    columns = chunk // tall
    flane = lax.broadcasted_iota(jnp.int32, (chunk, width), 1) // dk

    def lanes_of(parts):
        out = parts[0][:, :width]
        for a in range(1, per_group):
            out = jnp.where(flane == a, parts[a][:, :width], out)
        return out

    def stacked(x):
        if per_group == 1:
            return x
        return jnp.concatenate(
            [jnp.where(flane == a, x, jnp.zeros_like(x)) for a in range(per_group)], axis=0
        )

    def side_by_side(parts):
        return parts[0] if per_group == 1 else jnp.concatenate(parts, axis=1)

    def load(ref, which, i, by_column):
        if not by_column:
            return ref[which, pl.ds(pl.multiple_of(i * chunk, chunk), chunk), :]
        return jnp.concatenate(
            [ref[which, pl.ds(i * columns + c, tall, stride=wide), :] for c in range(columns)],
            axis=0,
        )

    states[...] = jnp.zeros_like(states)

    def advance(i, carry):
        work = []
        for order in range(2):
            q, k, v = (load(feats, kind, i, order) for kind in range(3))
            cums, betas, systems, scores = [], [], [], []
            for a in range(per_group):
                cum = split_mm(tri, load(gates, a, i, order), 3)
                beta = load(gates, per_group + a, i, order)
                gap = cum - cum.T
                within = jnp.where(inclusive, jnp.exp(jnp.where(inclusive, gap, 0.0)), 0.0)
                k_a = k if per_group == 1 else jnp.where(flane == a, k, 0.0)
                q_a = q if per_group == 1 else jnp.where(flane == a, q, 0.0)
                dots = mm(jnp.concatenate([k_a, q_a], axis=0), k, ((1,), (1,)))
                systems.append(within * dots[:chunk] * beta)
                scores.append(within * dots[chunk:])
                cums.append(cum)
                betas.append(beta)
            work.append((q, k, v, cums, betas, systems, scores))

        inverses = [[None] * per_group for _ in range(2)]
        half = 1
        while half < chunk:
            here = ((ti // (2 * half)) == (tj // (2 * half))) & (
                (lax.rem(ti, 2 * half) >= half) & (lax.rem(tj, 2 * half) < half)
            )
            lows = [
                [jnp.where(here, work[o][5][a], 0.0) for a in range(per_group)] for o in range(2)
            ]
            if half == 1:
                inverses = [[eye - low for low in row] for row in lows]
            else:
                firsts = [
                    [mm(lows[o][a], inverses[o][a]) for a in range(per_group)] for o in range(2)
                ]
                inverses = [
                    [inverses[o][a] - mm(inverses[o][a], firsts[o][a]) for a in range(per_group)]
                    for o in range(2)
                ]
            half *= 2

        for order in range(2):
            q, k, v, cums, betas, _, scores = work[order]
            beta = lanes_of(betas)
            cum = lanes_of(cums)
            scale = jnp.exp(cum)
            last = cum[chunk - 1 : chunk, :]
            tail = jnp.exp(last - cum)
            both = side_by_side(inverses[order])
            u = mm(both, stacked(v * beta))
            w = mm(both, stacked(k * (beta * scale)))
            state = states[order]
            fresh = u - mm(w, state)
            out = mm(q * scale, state) + mm(side_by_side(scores), stacked(fresh))
            grown = mm(k * tail, fresh, ((0,), (0,)))
            decayed = state * jnp.exp(last)
            states[order] = decayed + jnp.where(same_head, grown, 0.0)
            normed = out * lax.rsqrt(mm_split(out * out, head_ones, 2) * (1.0 / dk) + 1e-06)
            if order == 0:
                row_buf[pl.ds(pl.multiple_of(i * chunk, chunk), chunk), :] = normed
            else:
                normed = normed.astype(bf16).astype(f32)
                for c in range(columns):
                    col_buf[pl.ds(i * columns + c, tall, stride=wide), :] = normed[
                        c * tall : (c + 1) * tall
                    ]
        return carry

    lax.fori_loop(0, count // chunk, advance, 0)

    def finish(s, carry):
        at = pl.ds(s * block, block)
        out_ref[s] = (row_buf[at, :] + col_buf[at, :]).astype(bf16)
        return carry

    lax.fori_loop(0, strips, finish, 0)


def return_kernel(strips, groups, mixed_ref, out_ref, send_sem, recv_sem):
    me_f, me_s = lax.axis_index("face"), lax.axis_index("strip")
    rep = strips // groups
    barrier = pltpu.get_barrier_semaphore()
    for step in range(1, strips):
        pl.semaphore_signal(
            barrier, inc=1, device_id=(me_f, lax.rem(me_s + step, strips)), device_id_type=MESH
        )
    pl.semaphore_wait(barrier, strips - 1)
    mine = group_of(me_s, strips, groups)
    sends = lax.rem(me_s, rep) == 0

    def copy(step):
        dest = lax.rem(me_s + step, strips)
        return pltpu.make_async_remote_copy(
            src_ref=mixed_ref.at[dest],
            dst_ref=out_ref.at[mine],
            send_sem=send_sem.at[step],
            recv_sem=recv_sem.at[mine],
            device_id=(me_f, dest),
            device_id_type=MESH,
        )

    @pl.when(sends)
    def _():
        for step in range(1, strips):
            copy(step).start()
        pltpu.make_async_copy(mixed_ref.at[me_s], out_ref.at[mine], recv_sem.at[mine]).start()
        for step in range(1, strips):
            copy(step).wait_send()

    for group in range(groups):
        pltpu.make_async_copy(mixed_ref.at[0], out_ref.at[group], recv_sem.at[group]).wait()


def scan_call(
    first, slabs, gates, decay_rate, beta_bias, strips, per_group, tall, wide, dk
):
    count, width = slabs.shape[1:]
    block = count // strips
    chunk = min(128, count)
    vmem = pl.BlockSpec(memory_space=pltpu.VMEM)
    smem = pl.BlockSpec(memory_space=pltpu.SMEM)
    return pl.pallas_call(
        functools.partial(scan_kernel, (chunk, per_group, tall, wide, dk)),
        out_shape=jax.ShapeDtypeStruct((strips, block, width), bf16),
        in_specs=[smem, vmem, vmem, smem, smem],
        out_specs=vmem,
        scratch_shapes=[
            pltpu.VMEM((3, count, width), f32),
            pltpu.VMEM((2 * per_group, count, chunk), f32),
            pltpu.VMEM((count, width), f32),
            pltpu.VMEM((count, width), f32),
            pltpu.VMEM((2, width, width), f32),
        ],
        name="scans",
    )(first, slabs, gates, decay_rate, beta_bias)


LEVELS = 6
SPAN = 1 << LEVELS


def fused_kernel(
    cfg, px_ref, wq_ref, wg_ref, rate_ref, bias_ref, out_ref,
    px_all, wbuf, wg_own, g_out, g_in, g_rows, masks, flat, ordered, cums, sides,
    inv, into, trans, keyed, reads, asks, states, outs, mixed,
    px_send, px_fwd, px_recv, w_send, w_recv, g_send, g_recv, wg_sem, r_send, r_recv,
):
    faces, strips, n_slab, pieces, tall, wide = cfg
    me_f, me_s = lax.axis_index("face"), lax.axis_index("strip")
    block, features = px_ref.shape
    count = strips * block
    width = wbuf.shape[2]
    dk = width // 2
    heads = rate_ref.shape[0]
    gate_cols = wg_ref.shape[0]
    chips = strips // 2
    core, chip = lax.rem(me_s, 2), me_s // 2
    partner = chip * 2 + (1 - core)
    group = group_of(me_s, strips, strips)
    depth = features // pieces
    spans = count // SPAN
    columns = SPAN // tall

    barrier = pltpu.get_barrier_semaphore()
    for step in range(1, strips):
        pl.semaphore_signal(
            barrier, inc=1, device_id=(me_f, lax.rem(me_s + step, strips)), device_id_type=MESH
        )
    for step in range(1, faces):
        pl.semaphore_signal(
            barrier, inc=1, device_id=(lax.rem(me_f + step, faces), me_s), device_id_type=MESH
        )

    def chip_at(step):
        return lax.rem(chip + step, chips) * 2 + core

    def rows_of(strip):
        return px_all.at[pl.ds(pl.multiple_of(strip * block, block), block)]

    def weight_from(kind):
        slab = kind * strips + group
        return slab // n_slab, lax.rem(slab, n_slab)

    def weight_src(j, p):
        return wq_ref.at[pl.ds(p * depth, depth), pl.ds(pl.multiple_of(j * width, width), width)]

    def weight_at(kind, p):
        return wbuf.at[kind, pl.ds(p * depth, depth)]

    def weight_copy(kind, p, src, dest):
        return pltpu.make_async_remote_copy(
            src_ref=src,
            dst_ref=weight_at(kind, p),
            send_sem=w_send.at[kind, p, dest],
            recv_sem=w_recv.at[kind, p],
            device_id=(dest, me_s),
            device_id_type=MESH,
        )

    def own_weight(kind, p, j):
        return pltpu.make_async_copy(weight_src(j, p), weight_at(kind, p), w_recv.at[kind, p])

    def weight_wait(kind, p):
        here = weight_at(kind, p)
        pltpu.make_async_copy(here, here, w_recv.at[kind, p]).wait()

    def away(owner, dest):
        out = (dest == me_f + 1) & (owner <= me_f)
        return out | ((dest == me_f - 1) & (owner >= me_f))

    own_px = pltpu.make_async_copy(px_ref, rows_of(me_s), px_recv.at[me_s])
    own_px.start()
    own_gate = pltpu.make_async_copy(wg_ref, wg_own, wg_sem.at[0])
    own_gate.start()
    order = (1, 0, 2)
    pl.semaphore_wait(barrier, strips - 1 + faces - 1)

    for p in range(pieces):
        for kind in order:
            owner, j = weight_from(kind)

            @pl.when(owner == me_f)
            def _(kind=kind, p=p, j=j, owner=owner):
                for dest in range(faces):
                    pl.when(away(owner, dest))(weight_copy(kind, p, weight_src(j, p), dest).start)

    def px_copy(dest, sem, source, src):
        return pltpu.make_async_remote_copy(
            src_ref=src,
            dst_ref=rows_of(source),
            send_sem=sem,
            recv_sem=px_recv.at[source],
            device_id=(me_f, dest),
            device_id_type=MESH,
        )

    def px_out(step):
        return px_copy(chip_at(step), px_send.at[step], me_s, px_ref)

    def px_pass(step):
        source = chip_at(step)
        return px_copy(partner, px_fwd.at[step], source, rows_of(source))

    to_partner = px_copy(partner, px_send.at[0], me_s, px_ref)
    for step in range(1, chips):
        px_out(step).start()
    to_partner.start()
    for p in range(pieces):
        for kind in order:
            owner, j = weight_from(kind)
            pl.when(owner == me_f)(own_weight(kind, p, j).start)

    def gate_from(which):
        column = which * heads + group * 2
        return column // gate_cols, lax.rem(column, gate_cols)

    def gate_copy(which, dest):
        return pltpu.make_async_remote_copy(
            src_ref=g_out.at[which],
            dst_ref=g_in.at[which],
            send_sem=g_send.at[which, dest],
            recv_sem=g_recv.at[which],
            device_id=(dest, me_s),
            device_id_type=MESH,
        )

    own_gate.wait()
    weights_here = wg_own[...].astype(f32)
    rows_here = lax.broadcasted_iota(jnp.int32, weights_here.shape, 0)
    lines = features // width
    for which in range(2):
        owner, row = gate_from(which)

        @pl.when(owner == me_f)
        def _(which=which, owner=owner, row=row):
            picked = [
                jnp.sum(jnp.where(rows_here == row + a, weights_here, 0.0), axis=0, keepdims=True)
                for a in range(2)
            ]
            parts = [
                picked[a][:, i * width : (i + 1) * width] for a in range(2) for i in range(lines)
            ]
            g_out[which] = jnp.concatenate(parts, axis=0).astype(bf16)
            for dest in range(faces):
                pl.when(dest != me_f)(gate_copy(which, dest).start)
            pltpu.make_async_copy(g_out.at[which], g_in.at[which], g_recv.at[which]).start()

    ti = lax.broadcasted_iota(jnp.int32, (width, width), 0)
    tj = lax.broadcasted_iota(jnp.int32, (width, width), 1)
    for level in range(LEVELS):
        half = 1 << level
        here = (ti // (2 * half)) == (tj // (2 * half))
        here = here & (lax.rem(ti, 2 * half) >= half) & (lax.rem(tj, 2 * half) < half)
        masks[level] = here.astype(f32).astype(bf16)
    eye = (ti == tj).astype(f32)
    masks[LEVELS] = eye.astype(bf16)
    same_head = (ti // dk) == (tj // dk)
    masks[LEVELS + 1] = same_head.astype(f32).astype(bf16)
    tri = same_head & (ti >= tj)
    masks[LEVELS + 2] = tri.astype(f32).astype(bf16)

    def px_wait(strip):
        pltpu.make_async_copy(px_ref, rows_of(strip), px_recv.at[strip]).wait()

    def pass_pixels(step):
        px_wait(chip_at(step))
        px_pass(step).start()

    def pass_weights(distance, p):
        for kind in order:
            owner, _ = weight_from(kind)

            @pl.when(jnp.abs(owner - me_f) == distance)
            def _(kind=kind, owner=owner):
                weight_wait(kind, p)
                for dest in range(faces):
                    pl.when(away(owner, dest))(
                        weight_copy(kind, p, weight_at(kind, p), dest).start
                    )

    for p in range(pieces):
        pass_weights(1, p)
        if p < chips - 1:
            pass_pixels(p + 1)
    for step in range(pieces + 1, chips):
        pass_pixels(step)
    for distance in range(2, faces - 1):
        for p in range(pieces):
            pass_weights(distance, p)

    for which in range(2):
        pltpu.make_async_copy(g_in.at[which], g_in.at[which], g_recv.at[which]).wait()
        got = g_in[which].astype(f32)
        for a in range(2):
            for i in range(lines):
                line = got[a * lines + i : a * lines + i + 1, :]
                at = which * width + a * dk
                g_rows[at : at + dk, i * width : (i + 1) * width] = jnp.broadcast_to(
                    line, (dk, width)
                ).astype(bf16)
    px_wait(me_s)
    px_wait(partner)
    for step in range(1, chips):
        px_wait(lax.rem(chip + step, chips) * 2 + (1 - core))

    lane = lax.broadcasted_iota(jnp.int32, (1, width), 1) // dk
    first = group * 2

    def by_head(ref):
        return jnp.where(lane == 0, ref[first], ref[first + 1])

    logits = lax.dot_general(
        px_all[...], g_rows[...], (((1,), (1,)), ((), ())), preferred_element_type=f32
    )
    logits = logits.astype(bf16).astype(f32)
    flat[0] = -by_head(rate_ref) * jnp.exp(logits[:, :width])
    flat[1] = jax.nn.sigmoid(logits[:, width:] + by_head(bias_ref))

    head_ones = masks[LEVELS + 1]

    def features_of(kind):
        for p in range(pieces):
            own, _ = weight_from(kind)
            gap = jnp.abs(own - me_f)
            relayed = (gap > 0) & (gap < faces - 1)
            pl.when(jnp.logical_not(relayed))(functools.partial(weight_wait, kind, p))
        x = jnp.dot(px_all[...], wbuf[kind], preferred_element_type=f32)
        x = x.astype(bf16).astype(f32)
        if kind < 2:
            x = x * lax.rsqrt(mm(x * x, head_ones) + 1e-06)
        flat[2 + kind] = x

    def load(which, i, by_column):
        if not by_column:
            return flat[which, pl.ds(pl.multiple_of(i * SPAN, SPAN), SPAN), :]
        return jnp.concatenate(
            [flat[which, pl.ds(i * columns + c, tall, stride=wide), :] for c in range(columns)],
            axis=0,
        )

    half_masks = [(lane == a).astype(f32).astype(bf16) for a in range(2)]

    def stacked(x):
        x = x.astype(bf16)
        return jnp.concatenate([x * half_masks[0], x * half_masks[1]], axis=0)

    def twice(x):
        return jnp.concatenate([x, x], axis=0)

    def slot(i, o):
        return i * 2 + o

    ri = lax.broadcasted_iota(jnp.int32, (SPAN, width), 0)
    rj = lax.rem(lax.broadcasted_iota(jnp.int32, (SPAN, width), 1), dk)
    inclusive = ri >= rj

    def each_span(body, per_turn):
        def turn(t, carry):
            body([(t * per_turn + u, o) for u in range(per_turn) for o in range(2)])
            return carry

        lax.fori_loop(0, spans // per_turn, turn, 0)

    def key_stage(units):
        lows, tails, kbs = [], [], []
        for i, o in units:
            decay, beta, k = load(0, i, o), load(1, i, o), load(3, i, o)
            cum = split_mm(masks[LEVELS + 2], twice(decay), 3)[:SPAN]
            turned = twice(cum).T
            across = jnp.where(lane == 0, turned[0:1, :], turned[dk : dk + 1, :])
            gap = cum - across
            within = jnp.exp(jnp.where(inclusive, gap, -1e30))
            ks = stacked(k)
            gram = mm(k, ks, ((1,), (1,)))
            lows.append(twice((within * gram * beta).astype(bf16)))
            scale = jnp.exp(cum)
            last = cum[SPAN - 1 : SPAN, :]
            tails.append(stacked(k * jnp.exp(last - cum)))
            kb = stacked(k * (beta * scale))
            kbs.append(kb)
            at = slot(i, o)
            cums[at] = jnp.exp(last)
            ordered[0, at] = scale
            ordered[1, at] = within
            sides[0, at] = ks
            sides[1, at] = kb
        xs = [masks[LEVELS] - low * masks[0] for low in lows]
        for level in range(1, LEVELS):
            mids = [mm(low * masks[level], x) for low, x in zip(lows, xs)]
            ends = [mm(x, mid) for x, mid in zip(xs, mids)]
            xs = [x - end.astype(bf16) for x, end in zip(xs, ends)]
        hs = [mm(tail, x, ((0,), (0,))).astype(bf16) for tail, x in zip(tails, xs)]
        ms = [mm(h, kb).astype(bf16) for h, kb in zip(hs, kbs)]
        for (i, o), x, h, m in zip(units, xs, hs, ms):
            at = slot(i, o)
            inv[at] = x
            into[at] = h
            trans[at] = m

    def query_stage(units):
        for i, o in units:
            at = slot(i, o)
            q = load(2, i, o)
            scores = ordered[1, at] * mm(q, sides[0, at], ((1,), (1,)))
            g = mm(scores, inv[at]).astype(bf16)
            reads[at] = g
            asks[at] = (q * ordered[0, at] - mm(g, sides[1, at])).astype(bf16)

    def value_stage(units):
        for i, o in units:
            at = slot(i, o)
            vb = stacked(load(4, i, o) * load(1, i, o))
            keyed[at] = mm(into[at], vb)
            sides[0, at] = vb

    features_of(1)
    each_span(key_stage, 4)
    features_of(0)
    each_span(query_stage, 4)
    features_of(2)
    each_span(value_stage, 4)

    state = [jnp.zeros((width, width), f32) for _ in range(2)]
    for i in range(spans):
        for o in range(2):
            at = slot(i, o)
            held = state[o].astype(bf16)
            states[at] = held
            if i < spans - 1:
                state[o] = state[o] * cums[at] + (keyed[at] - mm(trans[at], held))

    def output_stage(units):
        for i, o in units:
            at = slot(i, o)
            out = mm(reads[at], sides[0, at]) + mm(asks[at], states[at])
            if o == 0:
                outs[0, pl.ds(pl.multiple_of(i * SPAN, SPAN), SPAN), :] = out
            else:
                for c in range(columns):
                    outs[1, pl.ds(i * columns + c, tall, stride=wide), :] = out[
                        c * tall : (c + 1) * tall
                    ]

    each_span(output_stage, 4)

    normed = []
    for o in range(2):
        x = outs[o]
        normed.append(x * lax.rsqrt(mm(x * x, head_ones) * (1.0 / dk) + 1e-06))
    total = (normed[0] + normed[1].astype(bf16).astype(f32)).astype(bf16)
    for s in range(strips):
        mixed[s] = total[s * block : (s + 1) * block]

    def lanes_of(owner):
        return out_ref.at[:, pl.ds(pl.multiple_of(owner * width, width), width)]

    def give(step):
        dest = lax.rem(me_s + step, strips)
        return pltpu.make_async_remote_copy(
            src_ref=mixed.at[dest],
            dst_ref=lanes_of(group),
            send_sem=r_send.at[step],
            recv_sem=r_recv.at[group],
            device_id=(me_f, dest),
            device_id_type=MESH,
        )

    for step in range(1, strips):
        give(step).start()
    pltpu.make_async_copy(mixed.at[me_s], lanes_of(group), r_recv.at[group]).start()

    to_partner.wait_send()
    for step in range(1, chips):
        px_out(step).wait_send()
        px_pass(step).wait_send()
    for which in range(2):
        owner, _ = gate_from(which)
        for dest in range(faces):
            pl.when((owner == me_f) & (dest != me_f))(gate_copy(which, dest).wait_send)
    for p in range(pieces):
        for kind in range(3):
            owner, _ = weight_from(kind)
            for dest in range(faces):
                pl.when(away(owner, dest))(
                    weight_copy(kind, p, weight_at(kind, p), dest).wait_send
                )
    for owner in range(strips):
        pltpu.make_async_copy(mixed.at[0], lanes_of(owner), r_recv.at[owner]).wait()
    for step in range(1, strips):
        give(step).wait_send()


def fused_call(faces, strips, px, w_qkv, w_gate_t, decay_rate, beta_bias, tall, wide):
    block, features = px.shape
    count = block * strips
    width = w_qkv.shape[1] * faces // 3 // strips
    units = 2 * count // SPAN
    pieces = 2
    vmem = pl.BlockSpec(memory_space=pltpu.VMEM)
    smem = pl.BlockSpec(memory_space=pltpu.SMEM)
    hbm = pl.BlockSpec(memory_space=pl.ANY)
    dma = pltpu.SemaphoreType.DMA
    square = (units, width, width)
    return pl.pallas_call(
        functools.partial(
            fused_kernel, (faces, strips, w_qkv.shape[1] // width, pieces, tall, wide)
        ),
        out_shape=jax.ShapeDtypeStruct((block, strips * width), bf16),
        in_specs=[hbm, hbm, hbm, smem, smem],
        out_specs=hbm,
        scratch_shapes=[
            pltpu.VMEM((count, features), bf16),
            pltpu.VMEM((3, features, width), bf16),
            pltpu.VMEM(w_gate_t.shape, bf16),
            pltpu.VMEM((2, 2 * features // width, width), bf16),
            pltpu.VMEM((2, 2 * features // width, width), bf16),
            pltpu.VMEM((2 * width, features), bf16),
            pltpu.VMEM((LEVELS + 3, width, width), bf16),
            pltpu.VMEM((5, count, width), f32),
            pltpu.VMEM((2, units, SPAN, width), f32),
            pltpu.VMEM((units, 1, width), f32),
            pltpu.VMEM((2,) + square, bf16),
            pltpu.VMEM(square, bf16),
            pltpu.VMEM(square, bf16),
            pltpu.VMEM(square, bf16),
            pltpu.VMEM(square, f32),
            pltpu.VMEM((units, SPAN, width), bf16),
            pltpu.VMEM((units, SPAN, width), bf16),
            pltpu.VMEM(square, bf16),
            pltpu.VMEM((2, count, width), f32),
            pltpu.VMEM((strips, block, width), bf16),
            dma((strips // 2,)),
            dma((strips // 2,)),
            dma((strips,)),
            dma((3, pieces, faces)),
            dma((3, pieces)),
            dma((2, faces)),
            dma((2,)),
            dma((1,)),
            dma((strips,)),
            dma((strips,)),
        ],
        compiler_params=pltpu.CompilerParams(
            collective_id=2, has_side_effects=True, vmem_limit_bytes=56 * 2**20
        ),
        name="layer",
    )(px, w_qkv, w_gate_t, decay_rate, beta_bias)


def fits_fused(strips, heads, dk, count, tall, wide, gate_cols, features, block):
    return (
        heads == 2 * strips
        and dk == SPAN
        and 2 * dk == 128
        and strips % 2 == 0
        and count % (4 * SPAN) == 0
        and count <= 1024
        and block % 16 == 0
        and tall % 8 == 0
        and SPAN % tall == 0
        and wide % (SPAN // tall) == 0
        and gate_cols % 8 == 0
        and features % 1024 == 0
    )


def on_device(faces, strips, pixels_in, w_qkv, w_gate, decay_rate, beta_bias):
    _, rows_here, wide, features = pixels_in.shape
    heads = decay_rate.shape[0]
    block = rows_here * wide
    count = block * strips
    tall = rows_here * strips
    model = w_qkv.shape[1] * faces // 3
    dk = model // heads
    groups = min(strips, heads)
    per_group = heads // groups
    width = per_group * dk
    n_slab = w_qkv.shape[1] // width
    gate_cols = w_gate.shape[1]
    if fits_fused(strips, heads, dk, count, tall, wide, gate_cols, features, block):
        out = fused_call(
            faces, strips, pixels_in.reshape(block, features), w_qkv, w_gate.T,
            decay_rate, beta_bias, tall, wide,
        )
        return out.reshape(1, rows_here, wide, model)
    pieces = 4
    chunk = min(128, count)
    chips = strips // 2
    vmem = pl.BlockSpec(memory_space=pltpu.VMEM)
    dma = pltpu.SemaphoreType.DMA
    if width % 128:
        w_qkv = w_qkv.reshape(features, n_slab, width).transpose(1, 0, 2)
    slabs, gates = pl.pallas_call(
        functools.partial(project_kernel, (faces, strips, groups, n_slab, pieces)),
        out_shape=(
            jax.ShapeDtypeStruct((3, count, width), bf16),
            jax.ShapeDtypeStruct((count // chunk, 2 * heads, chunk), f32),
        ),
        in_specs=[vmem, pl.BlockSpec(memory_space=pl.ANY), vmem],
        out_specs=(vmem, vmem),
        scratch_shapes=[
            pltpu.VMEM((count, features), bf16),
            pltpu.VMEM((3, features, width), bf16),
            pltpu.VMEM((gate_cols, features), f32),
            pltpu.VMEM((faces, gate_cols, features), f32),
            pltpu.VMEM((count, 3 * width), f32),
            dma((chips,)),
            dma((chips,)),
            dma((strips,)),
            dma((3, pieces, 2)),
            dma((3, pieces)),
            dma((faces,)),
            dma((faces,)),
        ],
        compiler_params=pltpu.CompilerParams(collective_id=0, has_side_effects=True),
        name="project",
    )(pixels_in.reshape(block, features), w_qkv, w_gate.T)
    group = group_of(lax.axis_index("strip"), strips, groups)
    first = (group * per_group).astype(jnp.int32).reshape(1)
    mixed = scan_call(
        first, slabs, gates, decay_rate, beta_bias, strips, per_group, tall, wide, dk
    )
    returned = pl.pallas_call(
        functools.partial(return_kernel, strips, groups),
        out_shape=jax.ShapeDtypeStruct((groups, block, width), bf16),
        in_specs=[vmem],
        out_specs=vmem,
        scratch_shapes=[dma((strips,)), dma((groups,))],
        compiler_params=pltpu.CompilerParams(collective_id=1, has_side_effects=True),
        name="give_back",
    )(mixed)
    return returned.transpose(1, 0, 2).reshape(1, rows_here, wide, model)


def solution(mesh):
    in_specs = (P("face", "strip", None, None), P(None, "face"), P(None, "face"), P(), P())
    out_specs = P("face", "strip", None, None)
    return jax.shard_map(
        functools.partial(on_device, mesh.shape["face"], mesh.shape["strip"]),
        mesh=mesh,
        in_specs=in_specs,
        out_specs=out_specs,
        check_vma=False,
    )
```

```python
import functools

import jax
import jax.numpy as jnp
from jax import lax
from jax.experimental import pallas as pl
from jax.experimental.pallas import tpu as pltpu
from jax.sharding import PartitionSpec as P

MESH = pl.DeviceIdType.MESH
f32 = jnp.float32
bf16 = jnp.bfloat16


def group_of(place, strips, groups):
    rep = strips // groups
    if rep > 1 or groups % 2:
        return place // rep
    return jnp.where(lax.rem(place, 2) == 0, place // 2, groups - 1 - place // 2)


def project_kernel(
    cfg, px_ref, wq_ref, wg_ref, slabs_ref, gates_ref,
    px_all, wbuf, wg_own, wg_all, acc, px_send, px_fwd, px_recv, w_send, w_recv, g_send, g_recv,
):
    faces, strips, groups, n_slab, pieces = cfg
    me_f, me_s = lax.axis_index("face"), lax.axis_index("strip")
    block, features = px_ref.shape
    count = strips * block
    width = wbuf.shape[2]
    chips = strips // 2
    core, chip = lax.rem(me_s, 2), me_s // 2
    partner = chip * 2 + (1 - core)
    group = group_of(me_s, strips, groups)
    depth = features // pieces

    def chip_at(step):
        return lax.rem(chip + step, chips) * 2 + core

    barrier = pltpu.get_barrier_semaphore()

    def greet(face, strip):
        pl.semaphore_signal(barrier, inc=1, device_id=(face, strip), device_id_type=MESH)

    greet(me_f, partner)
    for step in range(1, chips):
        greet(me_f, chip_at(step))
    for step in range(1, faces):
        greet(lax.rem(me_f + step, faces), me_s)

    wg_own[...] = wg_ref[...].astype(f32)

    def rows_of(strip):
        return px_all.at[pl.ds(pl.multiple_of(strip * block, block), block)]

    own_px = pltpu.make_async_copy(px_ref, rows_of(me_s), px_recv.at[me_s])
    own_px.start()
    pl.semaphore_wait(barrier, 1 + chips - 1 + faces - 1)

    def weight_from(kind):
        slab = kind * groups + group
        return slab // n_slab, lax.rem(slab, n_slab)

    def weight_src(j, p):
        rows = pl.ds(p * depth, depth)
        if len(wq_ref.shape) == 3:
            return wq_ref.at[j, rows]
        return wq_ref.at[rows, pl.ds(pl.multiple_of(j * width, width), width)]

    def weight_copy(kind, p, src, side):
        return pltpu.make_async_remote_copy(
            src_ref=src,
            dst_ref=wbuf.at[kind, pl.ds(p * depth, depth)],
            send_sem=w_send.at[kind, p, side],
            recv_sem=w_recv.at[kind, p],
            device_id=(me_f + (1 if side else -1), me_s),
            device_id_type=MESH,
        )

    def own_weight(kind, p, j):
        return pltpu.make_async_copy(
            weight_src(j, p), wbuf.at[kind, pl.ds(p * depth, depth)], w_recv.at[kind, p]
        )

    for p in range(pieces):
        for kind in range(3):
            owner, j = weight_from(kind)

            @pl.when(owner == me_f)
            def _(kind=kind, p=p, j=j):
                pl.when(me_f + 1 < faces)(weight_copy(kind, p, weight_src(j, p), 1).start)
                pl.when(me_f > 0)(weight_copy(kind, p, weight_src(j, p), 0).start)
                own_weight(kind, p, j).start()

    def px_copy(dest, sem, source, src):
        return pltpu.make_async_remote_copy(
            src_ref=src,
            dst_ref=rows_of(source),
            send_sem=sem,
            recv_sem=px_recv.at[source],
            device_id=(me_f, dest),
            device_id_type=MESH,
        )

    def px_out(step):
        return px_copy(chip_at(step), px_send.at[step], me_s, px_ref)

    def px_pass(step):
        source = chip_at(step)
        return px_copy(partner, px_fwd.at[step], source, rows_of(source))

    to_partner = px_copy(partner, px_send.at[0], me_s, px_ref)
    for step in range(1, chips):
        px_out(step).start()
    to_partner.start()

    def gate_copy(step):
        return pltpu.make_async_remote_copy(
            src_ref=wg_own,
            dst_ref=wg_all.at[me_f],
            send_sem=g_send.at[step],
            recv_sem=g_recv.at[me_f],
            device_id=(lax.rem(me_f + step, faces), me_s),
            device_id_type=MESH,
        )

    for step in range(1, faces):
        gate_copy(step).start()
    own_gate = pltpu.make_async_copy(wg_own, wg_all.at[me_f], g_recv.at[me_f])
    own_gate.start()

    def px_wait(strip):
        pltpu.make_async_copy(px_ref, rows_of(strip), px_recv.at[strip]).wait()

    def pass_pixels(step):
        px_wait(chip_at(step))
        px_pass(step).start()

    def pass_weights(p):
        for kind in range(3):
            owner, _ = weight_from(kind)
            here = wbuf.at[kind, pl.ds(p * depth, depth)]
            pltpu.make_async_copy(here, here, w_recv.at[kind, p]).wait()
            pl.when((owner < me_f) & (me_f + 1 < faces))(weight_copy(kind, p, here, 1).start)
            pl.when((owner > me_f) & (me_f > 0))(weight_copy(kind, p, here, 0).start)

    tile = min(512, count)

    def each_tile(body):
        if count == tile:
            body(pl.ds(0, tile), 0)
        else:

            def one(i, carry):
                body(pl.ds(pl.multiple_of(i * tile, tile), tile), i)
                return carry

            lax.fori_loop(0, count // tile, one, 0)

    def multiply(p):
        rows = pl.ds(p * depth, depth)
        weights = jnp.concatenate([wbuf[kind, rows, :] for kind in range(3)], axis=1)

        def body(at, _):
            term = jnp.dot(px_all[at, rows], weights, preferred_element_type=f32)
            if p > 0:
                term = term + acc[at, :]
            if p < pieces - 1:
                acc[at, :] = term
            else:
                for kind in range(3):
                    slabs_ref[kind, at, :] = term[
                        :, kind * width : (kind + 1) * width
                    ].astype(bf16)

        each_tile(body)

    for turn in range(max(pieces - 1, chips - 1)):
        if turn < pieces - 1:
            pass_weights(turn)
        if turn < chips - 1:
            pass_pixels(turn + 1)
    px_wait(me_s)
    px_wait(partner)
    for step in range(1, chips):
        px_wait(lax.rem(chip + step, chips) * 2 + (1 - core))
    for face in range(faces):
        pltpu.make_async_copy(wg_own, wg_all.at[face], g_recv.at[face]).wait()
    gate_w = jnp.concatenate([wg_all[face] for face in range(faces)], axis=0).astype(bf16)

    chunk = gates_ref.shape[2]

    def gate_body(at, i):
        logits = lax.dot_general(
            gate_w, px_all[at, :], (((1,), (1,)), ((), ())), preferred_element_type=f32
        )
        logits = logits.astype(bf16).astype(f32)
        for c in range(tile // chunk):
            gates_ref[i * (tile // chunk) + c] = logits[:, c * chunk : (c + 1) * chunk]

    each_tile(gate_body)
    for p in range(pieces - 1):
        multiply(p)
    pass_weights(pieces - 1)
    multiply(pieces - 1)

    to_partner.wait_send()
    for step in range(1, chips):
        px_out(step).wait_send()
        px_pass(step).wait_send()
    for step in range(1, faces):
        gate_copy(step).wait_send()
    for p in range(pieces):
        for kind in range(3):
            owner, _ = weight_from(kind)
            here = wbuf.at[kind, pl.ds(p * depth, depth)]
            pl.when((owner <= me_f) & (me_f + 1 < faces))(
                weight_copy(kind, p, here, 1).wait_send
            )
            pl.when((owner >= me_f) & (me_f > 0))(weight_copy(kind, p, here, 0).wait_send)


def mm(a, b, dims=((1,), (0,))):
    return lax.dot_general(
        a.astype(bf16), b.astype(bf16), (dims, ((), ())), preferred_element_type=f32
    )


def split_mm(exact, wide, pieces):
    exact = exact.astype(bf16)
    total, rest = None, wide
    for _ in range(pieces):
        piece = rest.astype(bf16)
        rest = rest - piece.astype(f32)
        term = jnp.dot(exact, piece, preferred_element_type=f32)
        total = term if total is None else total + term
    return total


def mm_split(wide, exact, pieces):
    exact = exact.astype(bf16)
    total, rest = None, wide
    for _ in range(pieces):
        piece = rest.astype(bf16)
        rest = rest - piece.astype(f32)
        term = jnp.dot(piece, exact, preferred_element_type=f32)
        total = term if total is None else total + term
    return total


def scan_kernel(
    cfg, first_ref, slabs_ref, gates_ref, rate_ref, bias_ref, out_ref,
    feats, gates, row_buf, col_buf, states,
):
    chunk, per_group, tall, wide, dk = cfg
    count, width = slabs_ref.shape[1:]
    strips, block, _ = out_ref.shape
    heads = gates_ref.shape[1] // 2
    first = first_ref[0]

    lane = lax.broadcasted_iota(jnp.int32, (width, width), 1)
    sub = lax.broadcasted_iota(jnp.int32, (width, width), 0)
    same_head = (lane // dk) == (sub // dk)
    head_ones = same_head.astype(f32)
    ti = lax.broadcasted_iota(jnp.int32, (chunk, chunk), 0)
    tj = lax.broadcasted_iota(jnp.int32, (chunk, chunk), 1)
    inclusive = ti >= tj
    tri = inclusive.astype(f32)
    eye = (ti == tj).astype(f32)

    def prepare(i, carry):
        at = pl.ds(pl.multiple_of(i * chunk, chunk), chunk)
        for kind in range(3):
            x = slabs_ref[kind, at, :].astype(f32)
            if kind < 2:
                x = x * lax.rsqrt(mm_split(x * x, head_ones, 2) + 1e-06)
            feats[kind, at, :] = x
        for a in range(per_group):
            head = first + a
            decay = -rate_ref[head] * jnp.exp(gates_ref[i, pl.ds(head, 1), :])
            strength = jax.nn.sigmoid(gates_ref[i, pl.ds(heads + head, 1), :] + bias_ref[head])
            gates[a, at, :] = jnp.broadcast_to(decay, (chunk, chunk)).T
            gates[per_group + a, at, :] = jnp.broadcast_to(strength, (chunk, chunk)).T
        return carry

    lax.fori_loop(0, count // chunk, prepare, 0, unroll=count // chunk <= 4)

    columns = chunk // tall
    flane = lax.broadcasted_iota(jnp.int32, (chunk, width), 1) // dk

    def lanes_of(parts):
        out = parts[0][:, :width]
        for a in range(1, per_group):
            out = jnp.where(flane == a, parts[a][:, :width], out)
        return out

    def stacked(x):
        if per_group == 1:
            return x
        return jnp.concatenate(
            [jnp.where(flane == a, x, jnp.zeros_like(x)) for a in range(per_group)], axis=0
        )

    def side_by_side(parts):
        return parts[0] if per_group == 1 else jnp.concatenate(parts, axis=1)

    def load(ref, which, i, by_column):
        if not by_column:
            return ref[which, pl.ds(pl.multiple_of(i * chunk, chunk), chunk), :]
        return jnp.concatenate(
            [ref[which, pl.ds(i * columns + c, tall, stride=wide), :] for c in range(columns)],
            axis=0,
        )

    states[...] = jnp.zeros_like(states)

    def advance(i, carry):
        work = []
        for order in range(2):
            q, k, v = (load(feats, kind, i, order) for kind in range(3))
            cums, betas, systems, scores = [], [], [], []
            for a in range(per_group):
                cum = split_mm(tri, load(gates, a, i, order), 3)
                beta = load(gates, per_group + a, i, order)
                gap = cum - cum.T
                within = jnp.where(inclusive, jnp.exp(jnp.where(inclusive, gap, 0.0)), 0.0)
                k_a = k if per_group == 1 else jnp.where(flane == a, k, 0.0)
                q_a = q if per_group == 1 else jnp.where(flane == a, q, 0.0)
                dots = mm(jnp.concatenate([k_a, q_a], axis=0), k, ((1,), (1,)))
                systems.append(within * dots[:chunk] * beta)
                scores.append(within * dots[chunk:])
                cums.append(cum)
                betas.append(beta)
            work.append((q, k, v, cums, betas, systems, scores))

        inverses = [[None] * per_group for _ in range(2)]
        half = 1
        while half < chunk:
            here = ((ti // (2 * half)) == (tj // (2 * half))) & (
                (lax.rem(ti, 2 * half) >= half) & (lax.rem(tj, 2 * half) < half)
            )
            lows = [
                [jnp.where(here, work[o][5][a], 0.0) for a in range(per_group)] for o in range(2)
            ]
            if half == 1:
                inverses = [[eye - low for low in row] for row in lows]
            else:
                firsts = [
                    [mm(lows[o][a], inverses[o][a]) for a in range(per_group)] for o in range(2)
                ]
                inverses = [
                    [inverses[o][a] - mm(inverses[o][a], firsts[o][a]) for a in range(per_group)]
                    for o in range(2)
                ]
            half *= 2

        for order in range(2):
            q, k, v, cums, betas, _, scores = work[order]
            beta = lanes_of(betas)
            cum = lanes_of(cums)
            scale = jnp.exp(cum)
            last = cum[chunk - 1 : chunk, :]
            tail = jnp.exp(last - cum)
            both = side_by_side(inverses[order])
            u = mm(both, stacked(v * beta))
            w = mm(both, stacked(k * (beta * scale)))
            state = states[order]
            fresh = u - mm(w, state)
            out = mm(q * scale, state) + mm(side_by_side(scores), stacked(fresh))
            grown = mm(k * tail, fresh, ((0,), (0,)))
            decayed = state * jnp.exp(last)
            states[order] = decayed + jnp.where(same_head, grown, 0.0)
            normed = out * lax.rsqrt(mm_split(out * out, head_ones, 2) * (1.0 / dk) + 1e-06)
            if order == 0:
                row_buf[pl.ds(pl.multiple_of(i * chunk, chunk), chunk), :] = normed
            else:
                normed = normed.astype(bf16).astype(f32)
                for c in range(columns):
                    col_buf[pl.ds(i * columns + c, tall, stride=wide), :] = normed[
                        c * tall : (c + 1) * tall
                    ]
        return carry

    lax.fori_loop(0, count // chunk, advance, 0)

    def finish(s, carry):
        at = pl.ds(s * block, block)
        out_ref[s] = (row_buf[at, :] + col_buf[at, :]).astype(bf16)
        return carry

    lax.fori_loop(0, strips, finish, 0)


def return_kernel(strips, groups, mixed_ref, out_ref, send_sem, recv_sem):
    me_f, me_s = lax.axis_index("face"), lax.axis_index("strip")
    rep = strips // groups
    barrier = pltpu.get_barrier_semaphore()
    for step in range(1, strips):
        pl.semaphore_signal(
            barrier, inc=1, device_id=(me_f, lax.rem(me_s + step, strips)), device_id_type=MESH
        )
    pl.semaphore_wait(barrier, strips - 1)
    mine = group_of(me_s, strips, groups)
    sends = lax.rem(me_s, rep) == 0

    def copy(step):
        dest = lax.rem(me_s + step, strips)
        return pltpu.make_async_remote_copy(
            src_ref=mixed_ref.at[dest],
            dst_ref=out_ref.at[mine],
            send_sem=send_sem.at[step],
            recv_sem=recv_sem.at[mine],
            device_id=(me_f, dest),
            device_id_type=MESH,
        )

    @pl.when(sends)
    def _():
        for step in range(1, strips):
            copy(step).start()
        pltpu.make_async_copy(mixed_ref.at[me_s], out_ref.at[mine], recv_sem.at[mine]).start()
        for step in range(1, strips):
            copy(step).wait_send()

    for group in range(groups):
        pltpu.make_async_copy(mixed_ref.at[0], out_ref.at[group], recv_sem.at[group]).wait()


def scan_call(
    first, slabs, gates, decay_rate, beta_bias, strips, per_group, tall, wide, dk
):
    count, width = slabs.shape[1:]
    block = count // strips
    chunk = min(128, count)
    vmem = pl.BlockSpec(memory_space=pltpu.VMEM)
    smem = pl.BlockSpec(memory_space=pltpu.SMEM)
    return pl.pallas_call(
        functools.partial(scan_kernel, (chunk, per_group, tall, wide, dk)),
        out_shape=jax.ShapeDtypeStruct((strips, block, width), bf16),
        in_specs=[smem, vmem, vmem, smem, smem],
        out_specs=vmem,
        scratch_shapes=[
            pltpu.VMEM((3, count, width), f32),
            pltpu.VMEM((2 * per_group, count, chunk), f32),
            pltpu.VMEM((count, width), f32),
            pltpu.VMEM((count, width), f32),
            pltpu.VMEM((2, width, width), f32),
        ],
        name="scans",
    )(first, slabs, gates, decay_rate, beta_bias)


LEVELS = 6
SPAN = 1 << LEVELS


def fused_kernel(
    cfg, px_ref, wq_ref, wg_ref, rate_ref, bias_ref, out_ref,
    px_all, wbuf, wg_own, g_out, g_in, g_rows, masks, flat, ordered, cums, sides,
    inv, into, trans, keyed, reads, asks, states, outs, mixed,
    px_send, px_fwd, px_recv, w_send, w_recv, g_send, g_recv, wg_sem, r_send, r_recv,
):
    faces, strips, n_slab, pieces, tall, wide = cfg
    me_f, me_s = lax.axis_index("face"), lax.axis_index("strip")
    block, features = px_ref.shape
    count = strips * block
    width = wbuf.shape[2]
    dk = width // 2
    heads = rate_ref.shape[0]
    gate_cols = wg_ref.shape[0]
    chips = strips // 2
    core, chip = lax.rem(me_s, 2), me_s // 2
    partner = chip * 2 + (1 - core)
    group = group_of(me_s, strips, strips)
    depth = features // pieces
    spans = count // SPAN
    columns = SPAN // tall

    barrier = pltpu.get_barrier_semaphore()
    for step in range(1, strips):
        pl.semaphore_signal(
            barrier, inc=1, device_id=(me_f, lax.rem(me_s + step, strips)), device_id_type=MESH
        )
    for step in range(1, faces):
        pl.semaphore_signal(
            barrier, inc=1, device_id=(lax.rem(me_f + step, faces), me_s), device_id_type=MESH
        )

    def chip_at(step, on=None):
        other, bit = chip, 1
        while bit < chips:
            if step & bit:
                other = other + bit - 2 * bit * lax.rem(other // bit, 2)
            bit *= 2
        return other * 2 + (core if on is None else on)

    def rows_of(strip):
        return px_all.at[pl.ds(pl.multiple_of(strip * block, block), block)]

    def weight_from(kind):
        slab = kind * strips + group
        return slab // n_slab, lax.rem(slab, n_slab)

    def weight_src(j, p):
        return wq_ref.at[pl.ds(p * depth, depth), pl.ds(pl.multiple_of(j * width, width), width)]

    def weight_at(kind, p):
        return wbuf.at[kind, pl.ds(p * depth, depth)]

    def weight_copy(kind, p, src, dest):
        return pltpu.make_async_remote_copy(
            src_ref=src,
            dst_ref=weight_at(kind, p),
            send_sem=w_send.at[kind, p, dest],
            recv_sem=w_recv.at[kind, p],
            device_id=(dest, me_s),
            device_id_type=MESH,
        )

    def own_weight(kind, p, j):
        return pltpu.make_async_copy(weight_src(j, p), weight_at(kind, p), w_recv.at[kind, p])

    def weight_wait(kind, p):
        here = weight_at(kind, p)
        pltpu.make_async_copy(here, here, w_recv.at[kind, p]).wait()

    def relays(owner, dest):
        up = (dest == me_f + 1) & (owner == me_f - 1)
        return up | ((dest == me_f - 1) & (owner == me_f + 1))

    def direct(owner, dest, far):
        gap = jnp.abs(dest - me_f)
        return (owner == me_f) & ((gap > 2) if far else (gap == 1))

    def sends(owner, dest):
        return direct(owner, dest, False) | direct(owner, dest, True) | relays(owner, dest)

    def gate_from(which):
        column = which * heads + group * 2
        return column // gate_cols, lax.rem(column, gate_cols)

    def gate_copy(which, dest):
        return pltpu.make_async_remote_copy(
            src_ref=g_out.at[which],
            dst_ref=g_in.at[which],
            send_sem=g_send.at[which, dest],
            recv_sem=g_recv.at[which],
            device_id=(dest, me_s),
            device_id_type=MESH,
        )

    lines = features // width

    def pick_gates():
        here = wg_own[...].astype(f32)
        row_of = lax.broadcasted_iota(jnp.int32, here.shape, 0)
        for which in range(2):
            owner, row = gate_from(which)

            @pl.when(owner == me_f)
            def _(which=which, row=row):
                picked = [
                    jnp.sum(jnp.where(row_of == row + a, here, 0.0), axis=0, keepdims=True)
                    for a in range(2)
                ]
                parts = [
                    picked[a][:, i * width : (i + 1) * width]
                    for a in range(2)
                    for i in range(lines)
                ]
                g_out[which] = jnp.concatenate(parts, axis=0).astype(bf16)

    def send_gates():
        for which in range(2):
            owner, _ = gate_from(which)

            @pl.when(owner == me_f)
            def _(which=which):
                for dest in range(faces):
                    pl.when(dest != me_f)(gate_copy(which, dest).start)
                pltpu.make_async_copy(g_out.at[which], g_in.at[which], g_recv.at[which]).start()

    own_px = pltpu.make_async_copy(px_ref, rows_of(me_s), px_recv.at[me_s])
    own_px.start()
    own_gate = pltpu.make_async_copy(wg_ref, wg_own, wg_sem.at[0])
    own_gate.start()
    own_gate.wait()
    pick_gates()
    pl.semaphore_wait(barrier, strips - 1 + faces - 1)
    send_gates()

    def send_weights(kind, far):
        owner, j = weight_from(kind)

        @pl.when(owner == me_f)
        def _():
            for p in range(pieces):
                for dest in range(faces):
                    pl.when(direct(owner, dest, far))(
                        weight_copy(kind, p, weight_src(j, p), dest).start
                    )

    def own_weights(kind):
        owner, j = weight_from(kind)

        @pl.when(owner == me_f)
        def _():
            for p in range(pieces):
                own_weight(kind, p, j).start()

    send_weights(1, False)
    send_weights(1, True)
    def px_copy(dest, sem, source, src):
        return pltpu.make_async_remote_copy(
            src_ref=src,
            dst_ref=rows_of(source),
            send_sem=sem,
            recv_sem=px_recv.at[source],
            device_id=(me_f, dest),
            device_id_type=MESH,
        )

    def px_out(step):
        return px_copy(chip_at(step), px_send.at[step], me_s, px_ref)

    def px_pass(step):
        source = chip_at(step)
        return px_copy(partner, px_fwd.at[step], source, rows_of(source))

    to_partner = px_copy(partner, px_send.at[0], me_s, px_ref)
    for step in range(1, chips):
        px_out(step).start()
    to_partner.start()
    own_weights(1)

    ti = lax.broadcasted_iota(jnp.int32, (width, width), 0)
    tj = lax.broadcasted_iota(jnp.int32, (width, width), 1)
    for level in range(LEVELS):
        half = 1 << level
        here = (ti // (2 * half)) == (tj // (2 * half))
        here = here & (lax.rem(ti, 2 * half) >= half) & (lax.rem(tj, 2 * half) < half)
        masks[level] = here.astype(f32).astype(bf16)
    eye = (ti == tj).astype(f32)
    masks[LEVELS] = eye.astype(bf16)
    same_head = (ti // dk) == (tj // dk)
    masks[LEVELS + 1] = same_head.astype(f32).astype(bf16)
    tri = same_head & (ti >= tj)
    masks[LEVELS + 2] = tri.astype(f32).astype(bf16)

    def px_wait(strip):
        pltpu.make_async_copy(px_ref, rows_of(strip), px_recv.at[strip]).wait()

    def pass_pixels(step):
        px_wait(chip_at(step))
        px_pass(step).start()

    def relayed(owner):
        return (jnp.abs(owner - me_f) == 1) & (
            ((2 * me_f - owner) >= 0) & ((2 * me_f - owner) < faces)
        )

    def pass_weights(kind, p):
        owner, _ = weight_from(kind)

        @pl.when(relayed(owner))
        def _():
            weight_wait(kind, p)
            for dest in range(faces):
                pl.when(relays(owner, dest))(weight_copy(kind, p, weight_at(kind, p), dest).start)

    for p in range(pieces):
        pass_weights(1, p)
    for kind in (0, 2):
        send_weights(kind, False)
    for kind in (0, 2):
        own_weights(kind)
    for step in range(1, chips):
        pass_pixels(step)
    for p in range(pieces):
        for kind in (0, 2):
            pass_weights(kind, p)

    for which in range(2):
        pltpu.make_async_copy(g_in.at[which], g_in.at[which], g_recv.at[which]).wait()
        got = g_in[which].astype(f32)
        for a in range(2):
            for i in range(lines):
                line = got[a * lines + i : a * lines + i + 1, :]
                at = which * width + a * dk
                g_rows[at : at + dk, i * width : (i + 1) * width] = jnp.broadcast_to(
                    line, (dk, width)
                ).astype(bf16)
    px_wait(me_s)
    px_wait(partner)
    for step in range(1, chips):
        px_wait(chip_at(step, 1 - core))

    lane = lax.broadcasted_iota(jnp.int32, (1, width), 1) // dk
    first = group * 2

    def by_head(ref):
        return jnp.where(lane == 0, ref[first], ref[first + 1])

    logits = lax.dot_general(
        px_all[...], g_rows[...], (((1,), (1,)), ((), ())), preferred_element_type=f32
    )
    logits = logits.astype(bf16).astype(f32)
    flat[0] = -by_head(rate_ref) * jnp.exp(logits[:, :width])
    flat[1] = jax.nn.sigmoid(logits[:, width:] + by_head(bias_ref))

    head_ones = masks[LEVELS + 1]

    def features_of(kind):
        owner, _ = weight_from(kind)
        for p in range(pieces):
            pl.when(jnp.logical_not(relayed(owner)))(functools.partial(weight_wait, kind, p))
        if kind == 1:
            for late in (0, 2):
                send_weights(late, True)
        x = jnp.dot(px_all[...], wbuf[kind], preferred_element_type=f32)
        x = x.astype(bf16).astype(f32)
        if kind < 2:
            x = x * lax.rsqrt(mm(x * x, head_ones) + 1e-06)
        flat[2 + kind] = x

    def rows_at(i):
        return pl.ds(i * SPAN if isinstance(i, int) else pl.multiple_of(i * SPAN, SPAN), SPAN)

    def load(which, i, by_column):
        if not by_column:
            return flat[which, rows_at(i), :]
        return jnp.concatenate(
            [flat[which, pl.ds(i * columns + c, tall, stride=wide), :] for c in range(columns)],
            axis=0,
        )

    half_masks = [(lane == a).astype(f32).astype(bf16) for a in range(2)]

    def stacked(x):
        x = x.astype(bf16)
        return jnp.concatenate([x * half_masks[0], x * half_masks[1]], axis=0)

    def twice(x):
        return jnp.concatenate([x, x], axis=0)

    def slot(i, o):
        return i * 2 + o

    ri = lax.broadcasted_iota(jnp.int32, (SPAN, width), 0)
    rj = lax.rem(lax.broadcasted_iota(jnp.int32, (SPAN, width), 1), dk)
    inclusive = ri >= rj

    units_all = [(i, o) for i in range(spans) for o in range(2)]

    def each_span(body, per_turn):
        def turn(t, carry):
            body([(t * per_turn + u, o) for u in range(per_turn) for o in range(2)])
            return carry

        lax.fori_loop(0, spans // per_turn, turn, 0)

    def key_stage(units):
        lows, tails, kbs = [], [], []
        for i, o in units:
            decay, beta, k = load(0, i, o), load(1, i, o), load(3, i, o)
            cum = split_mm(masks[LEVELS + 2], twice(decay), 3)[:SPAN]
            turned = twice(cum).T
            across = jnp.where(lane == 0, turned[0:1, :], turned[dk : dk + 1, :])
            gap = cum - across
            within = jnp.exp(jnp.where(inclusive, gap, -1e30))
            ks = stacked(k)
            gram = mm(k, ks, ((1,), (1,)))
            lows.append(twice((within * gram * beta).astype(bf16)))
            scale = jnp.exp(cum)
            last = cum[SPAN - 1 : SPAN, :]
            tails.append(stacked(k * jnp.exp(last - cum)))
            kb = stacked(k * (beta * scale))
            kbs.append(kb)
            at = slot(i, o)
            cums[at] = jnp.exp(last)
            ordered[0, at] = scale
            ordered[1, at] = within
            sides[0, at] = ks
            sides[1, at] = kb
        xs = [masks[LEVELS] - low * masks[0] for low in lows]
        for level in range(1, LEVELS):
            mids = [mm(low * masks[level], x) for low, x in zip(lows, xs)]
            ends = [mm(x, mid) for x, mid in zip(xs, mids)]
            xs = [x - end.astype(bf16) for x, end in zip(xs, ends)]
        hs = [mm(tail, x, ((0,), (0,))).astype(bf16) for tail, x in zip(tails, xs)]
        ms = [mm(h, kb).astype(bf16) for h, kb in zip(hs, kbs)]
        for (i, o), x, h, m in zip(units, xs, hs, ms):
            at = slot(i, o)
            inv[at] = x
            into[at] = h
            trans[at] = m

    def query_stage(units):
        for i, o in units:
            at = slot(i, o)
            q = load(2, i, o)
            scores = ordered[1, at] * mm(q, sides[0, at], ((1,), (1,)))
            g = mm(scores, inv[at]).astype(bf16)
            reads[at] = g
            asks[at] = (q * ordered[0, at] - mm(g, sides[1, at])).astype(bf16)

    def value_stage(units):
        for i, o in units:
            at = slot(i, o)
            vb = stacked(load(4, i, o) * load(1, i, o))
            keyed[at] = mm(into[at], vb)
            sides[2, at] = vb

    def value_scan():
        features_of(2)
        each_span(value_stage, 4)
        state = [jnp.zeros((width, width), f32) for _ in range(2)]
        for i in range(spans):
            for o in range(2):
                at = slot(i, o)
                held = state[o].astype(bf16)
                states[at] = held
                if i < spans - 1:
                    state[o] = state[o] * cums[at] + (keyed[at] - mm(trans[at], held))

    queries_last = me_f * 2 >= faces
    features_of(1)
    key_stage(units_all)
    pl.when(queries_last)(value_scan)
    features_of(0)
    each_span(query_stage, 4)
    pl.when(jnp.logical_not(queries_last))(value_scan)

    def output_stage(units):
        for i, o in units:
            at = slot(i, o)
            out = mm(reads[at], sides[2, at]) + mm(asks[at], states[at])
            if o == 0:
                outs[0, rows_at(i), :] = out
            else:
                for c in range(columns):
                    outs[1, pl.ds(i * columns + c, tall, stride=wide), :] = out[
                        c * tall : (c + 1) * tall
                    ]

    each_span(output_stage, 4)
    normed = []
    for o in range(2):
        x = outs[o]
        normed.append(x * lax.rsqrt(mm(x * x, head_ones) * (1.0 / dk) + 1e-06))
    total = (normed[0] + normed[1].astype(bf16).astype(f32)).astype(bf16)
    for s in range(strips):
        mixed[s] = total[s * block : (s + 1) * block]

    def lanes_of(owner):
        return out_ref.at[:, pl.ds(pl.multiple_of(owner * width, width), width)]

    def give(step):
        dest = lax.rem(me_s + step, strips)
        return pltpu.make_async_remote_copy(
            src_ref=mixed.at[dest],
            dst_ref=lanes_of(group),
            send_sem=r_send.at[step],
            recv_sem=r_recv.at[group],
            device_id=(me_f, dest),
            device_id_type=MESH,
        )

    for step in range(1, strips):
        give(step).start()
    pltpu.make_async_copy(mixed.at[me_s], lanes_of(group), r_recv.at[group]).start()

    to_partner.wait_send()
    for step in range(1, chips):
        px_out(step).wait_send()
        px_pass(step).wait_send()
    for which in range(2):
        owner, _ = gate_from(which)
        for dest in range(faces):
            pl.when((owner == me_f) & (dest != me_f))(gate_copy(which, dest).wait_send)
    for p in range(pieces):
        for kind in range(3):
            owner, _ = weight_from(kind)
            for dest in range(faces):
                pl.when(sends(owner, dest))(
                    weight_copy(kind, p, weight_at(kind, p), dest).wait_send
                )
    for owner in range(strips):
        pltpu.make_async_copy(mixed.at[0], lanes_of(owner), r_recv.at[owner]).wait()
    for step in range(1, strips):
        give(step).wait_send()


def fused_call(faces, strips, px, w_qkv, w_gate_t, decay_rate, beta_bias, tall, wide):
    block, features = px.shape
    count = block * strips
    width = w_qkv.shape[1] * faces // 3 // strips
    units = 2 * count // SPAN
    pieces = 2
    vmem = pl.BlockSpec(memory_space=pltpu.VMEM)
    smem = pl.BlockSpec(memory_space=pltpu.SMEM)
    hbm = pl.BlockSpec(memory_space=pl.ANY)
    dma = pltpu.SemaphoreType.DMA
    square = (units, width, width)
    return pl.pallas_call(
        functools.partial(
            fused_kernel, (faces, strips, w_qkv.shape[1] // width, pieces, tall, wide)
        ),
        out_shape=jax.ShapeDtypeStruct((block, strips * width), bf16),
        in_specs=[hbm, hbm, hbm, smem, smem],
        out_specs=hbm,
        scratch_shapes=[
            pltpu.VMEM((count, features), bf16),
            pltpu.VMEM((3, features, width), bf16),
            pltpu.VMEM(w_gate_t.shape, bf16),
            pltpu.VMEM((2, 2 * features // width, width), bf16),
            pltpu.VMEM((2, 2 * features // width, width), bf16),
            pltpu.VMEM((2 * width, features), bf16),
            pltpu.VMEM((LEVELS + 3, width, width), bf16),
            pltpu.VMEM((5, count, width), f32),
            pltpu.VMEM((2, units, SPAN, width), f32),
            pltpu.VMEM((units, 1, width), f32),
            pltpu.VMEM((3,) + square, bf16),
            pltpu.VMEM(square, bf16),
            pltpu.VMEM(square, bf16),
            pltpu.VMEM(square, bf16),
            pltpu.VMEM(square, f32),
            pltpu.VMEM((units, SPAN, width), bf16),
            pltpu.VMEM((units, SPAN, width), bf16),
            pltpu.VMEM(square, bf16),
            pltpu.VMEM((2, count, width), f32),
            pltpu.VMEM((strips, block, width), bf16),
            dma((strips // 2,)),
            dma((strips // 2,)),
            dma((strips,)),
            dma((3, pieces, faces)),
            dma((3, pieces)),
            dma((2, faces)),
            dma((2,)),
            dma((1,)),
            dma((strips,)),
            dma((strips,)),
        ],
        compiler_params=pltpu.CompilerParams(
            collective_id=2, has_side_effects=True, vmem_limit_bytes=56 * 2**20
        ),
        name="layer",
    )(px, w_qkv, w_gate_t, decay_rate, beta_bias)


def fits_fused(strips, heads, dk, count, tall, wide, gate_cols, features, block):
    return (
        heads == 2 * strips
        and dk == SPAN
        and 2 * dk == 128
        and strips & (strips - 1) == 0
        and strips > 1
        and count % (4 * SPAN) == 0
        and count <= 1024
        and block % 16 == 0
        and tall % 8 == 0
        and SPAN % tall == 0
        and wide % (SPAN // tall) == 0
        and gate_cols % 8 == 0
        and features % 1024 == 0
    )


def on_device(faces, strips, pixels_in, w_qkv, w_gate, decay_rate, beta_bias):
    _, rows_here, wide, features = pixels_in.shape
    heads = decay_rate.shape[0]
    block = rows_here * wide
    count = block * strips
    tall = rows_here * strips
    model = w_qkv.shape[1] * faces // 3
    dk = model // heads
    groups = min(strips, heads)
    per_group = heads // groups
    width = per_group * dk
    n_slab = w_qkv.shape[1] // width
    gate_cols = w_gate.shape[1]
    if fits_fused(strips, heads, dk, count, tall, wide, gate_cols, features, block):
        out = fused_call(
            faces, strips, pixels_in.reshape(block, features), w_qkv, w_gate.T,
            decay_rate, beta_bias, tall, wide,
        )
        return out.reshape(1, rows_here, wide, model)
    pieces = 4
    chunk = min(128, count)
    chips = strips // 2
    vmem = pl.BlockSpec(memory_space=pltpu.VMEM)
    dma = pltpu.SemaphoreType.DMA
    if width % 128:
        w_qkv = w_qkv.reshape(features, n_slab, width).transpose(1, 0, 2)
    slabs, gates = pl.pallas_call(
        functools.partial(project_kernel, (faces, strips, groups, n_slab, pieces)),
        out_shape=(
            jax.ShapeDtypeStruct((3, count, width), bf16),
            jax.ShapeDtypeStruct((count // chunk, 2 * heads, chunk), f32),
        ),
        in_specs=[vmem, pl.BlockSpec(memory_space=pl.ANY), vmem],
        out_specs=(vmem, vmem),
        scratch_shapes=[
            pltpu.VMEM((count, features), bf16),
            pltpu.VMEM((3, features, width), bf16),
            pltpu.VMEM((gate_cols, features), f32),
            pltpu.VMEM((faces, gate_cols, features), f32),
            pltpu.VMEM((count, 3 * width), f32),
            dma((chips,)),
            dma((chips,)),
            dma((strips,)),
            dma((3, pieces, 2)),
            dma((3, pieces)),
            dma((faces,)),
            dma((faces,)),
        ],
        compiler_params=pltpu.CompilerParams(collective_id=0, has_side_effects=True),
        name="project",
    )(pixels_in.reshape(block, features), w_qkv, w_gate.T)
    group = group_of(lax.axis_index("strip"), strips, groups)
    first = (group * per_group).astype(jnp.int32).reshape(1)
    mixed = scan_call(
        first, slabs, gates, decay_rate, beta_bias, strips, per_group, tall, wide, dk
    )
    returned = pl.pallas_call(
        functools.partial(return_kernel, strips, groups),
        out_shape=jax.ShapeDtypeStruct((groups, block, width), bf16),
        in_specs=[vmem],
        out_specs=vmem,
        scratch_shapes=[dma((strips,)), dma((groups,))],
        compiler_params=pltpu.CompilerParams(collective_id=1, has_side_effects=True),
        name="give_back",
    )(mixed)
    return returned.transpose(1, 0, 2).reshape(1, rows_here, wide, model)


def solution(mesh):
    in_specs = (P("face", "strip", None, None), P(None, "face"), P(None, "face"), P(), P())
    out_specs = P("face", "strip", None, None)
    return jax.shard_map(
        functools.partial(on_device, mesh.shape["face"], mesh.shape["strip"]),
        mesh=mesh,
        in_specs=in_specs,
        out_specs=out_specs,
        check_vma=False,
    )
```

```python
import functools

import jax
import jax.numpy as jnp
from jax import lax
from jax.experimental import pallas as pl
from jax.experimental.pallas import tpu as pltpu
from jax.sharding import PartitionSpec as P

MESH = pl.DeviceIdType.MESH
f32 = jnp.float32
bf16 = jnp.bfloat16


def group_of(place, strips, groups):
    rep = strips // groups
    if rep > 1 or groups % 2:
        return place // rep
    return jnp.where(lax.rem(place, 2) == 0, place // 2, groups - 1 - place // 2)


def project_kernel(
    cfg, px_ref, wq_ref, wg_ref, slabs_ref, gates_ref,
    px_all, wbuf, wg_own, wg_all, acc, px_send, px_fwd, px_recv, w_send, w_recv, g_send, g_recv,
):
    faces, strips, groups, n_slab, pieces = cfg
    me_f, me_s = lax.axis_index("face"), lax.axis_index("strip")
    block, features = px_ref.shape
    count = strips * block
    width = wbuf.shape[2]
    chips = strips // 2
    core, chip = lax.rem(me_s, 2), me_s // 2
    partner = chip * 2 + (1 - core)
    group = group_of(me_s, strips, groups)
    depth = features // pieces

    def chip_at(step):
        return lax.rem(chip + step, chips) * 2 + core

    barrier = pltpu.get_barrier_semaphore()

    def greet(face, strip):
        pl.semaphore_signal(barrier, inc=1, device_id=(face, strip), device_id_type=MESH)

    greet(me_f, partner)
    for step in range(1, chips):
        greet(me_f, chip_at(step))
    for step in range(1, faces):
        greet(lax.rem(me_f + step, faces), me_s)

    wg_own[...] = wg_ref[...].astype(f32)

    def rows_of(strip):
        return px_all.at[pl.ds(pl.multiple_of(strip * block, block), block)]

    own_px = pltpu.make_async_copy(px_ref, rows_of(me_s), px_recv.at[me_s])
    own_px.start()
    pl.semaphore_wait(barrier, 1 + chips - 1 + faces - 1)

    def weight_from(kind):
        slab = kind * groups + group
        return slab // n_slab, lax.rem(slab, n_slab)

    def weight_src(j, p):
        rows = pl.ds(p * depth, depth)
        if len(wq_ref.shape) == 3:
            return wq_ref.at[j, rows]
        return wq_ref.at[rows, pl.ds(pl.multiple_of(j * width, width), width)]

    def weight_copy(kind, p, src, side):
        return pltpu.make_async_remote_copy(
            src_ref=src,
            dst_ref=wbuf.at[kind, pl.ds(p * depth, depth)],
            send_sem=w_send.at[kind, p, side],
            recv_sem=w_recv.at[kind, p],
            device_id=(me_f + (1 if side else -1), me_s),
            device_id_type=MESH,
        )

    def own_weight(kind, p, j):
        return pltpu.make_async_copy(
            weight_src(j, p), wbuf.at[kind, pl.ds(p * depth, depth)], w_recv.at[kind, p]
        )

    for p in range(pieces):
        for kind in range(3):
            owner, j = weight_from(kind)

            @pl.when(owner == me_f)
            def _(kind=kind, p=p, j=j):
                pl.when(me_f + 1 < faces)(weight_copy(kind, p, weight_src(j, p), 1).start)
                pl.when(me_f > 0)(weight_copy(kind, p, weight_src(j, p), 0).start)
                own_weight(kind, p, j).start()

    def px_copy(dest, sem, source, src):
        return pltpu.make_async_remote_copy(
            src_ref=src,
            dst_ref=rows_of(source),
            send_sem=sem,
            recv_sem=px_recv.at[source],
            device_id=(me_f, dest),
            device_id_type=MESH,
        )

    def px_out(step):
        return px_copy(chip_at(step), px_send.at[step], me_s, px_ref)

    def px_pass(step):
        source = chip_at(step)
        return px_copy(partner, px_fwd.at[step], source, rows_of(source))

    to_partner = px_copy(partner, px_send.at[0], me_s, px_ref)
    for step in range(1, chips):
        px_out(step).start()
    to_partner.start()

    def gate_copy(step):
        return pltpu.make_async_remote_copy(
            src_ref=wg_own,
            dst_ref=wg_all.at[me_f],
            send_sem=g_send.at[step],
            recv_sem=g_recv.at[me_f],
            device_id=(lax.rem(me_f + step, faces), me_s),
            device_id_type=MESH,
        )

    for step in range(1, faces):
        gate_copy(step).start()
    own_gate = pltpu.make_async_copy(wg_own, wg_all.at[me_f], g_recv.at[me_f])
    own_gate.start()

    def px_wait(strip):
        pltpu.make_async_copy(px_ref, rows_of(strip), px_recv.at[strip]).wait()

    def pass_pixels(step):
        px_wait(chip_at(step))
        px_pass(step).start()

    def pass_weights(p):
        for kind in range(3):
            owner, _ = weight_from(kind)
            here = wbuf.at[kind, pl.ds(p * depth, depth)]
            pltpu.make_async_copy(here, here, w_recv.at[kind, p]).wait()
            pl.when((owner < me_f) & (me_f + 1 < faces))(weight_copy(kind, p, here, 1).start)
            pl.when((owner > me_f) & (me_f > 0))(weight_copy(kind, p, here, 0).start)

    tile = min(512, count)

    def each_tile(body):
        if count == tile:
            body(pl.ds(0, tile), 0)
        else:

            def one(i, carry):
                body(pl.ds(pl.multiple_of(i * tile, tile), tile), i)
                return carry

            lax.fori_loop(0, count // tile, one, 0)

    def multiply(p):
        rows = pl.ds(p * depth, depth)
        weights = jnp.concatenate([wbuf[kind, rows, :] for kind in range(3)], axis=1)

        def body(at, _):
            term = jnp.dot(px_all[at, rows], weights, preferred_element_type=f32)
            if p > 0:
                term = term + acc[at, :]
            if p < pieces - 1:
                acc[at, :] = term
            else:
                for kind in range(3):
                    slabs_ref[kind, at, :] = term[
                        :, kind * width : (kind + 1) * width
                    ].astype(bf16)

        each_tile(body)

    for turn in range(max(pieces - 1, chips - 1)):
        if turn < pieces - 1:
            pass_weights(turn)
        if turn < chips - 1:
            pass_pixels(turn + 1)
    px_wait(me_s)
    px_wait(partner)
    for step in range(1, chips):
        px_wait(lax.rem(chip + step, chips) * 2 + (1 - core))
    for face in range(faces):
        pltpu.make_async_copy(wg_own, wg_all.at[face], g_recv.at[face]).wait()
    gate_w = jnp.concatenate([wg_all[face] for face in range(faces)], axis=0).astype(bf16)

    chunk = gates_ref.shape[2]

    def gate_body(at, i):
        logits = lax.dot_general(
            gate_w, px_all[at, :], (((1,), (1,)), ((), ())), preferred_element_type=f32
        )
        logits = logits.astype(bf16).astype(f32)
        for c in range(tile // chunk):
            gates_ref[i * (tile // chunk) + c] = logits[:, c * chunk : (c + 1) * chunk]

    each_tile(gate_body)
    for p in range(pieces - 1):
        multiply(p)
    pass_weights(pieces - 1)
    multiply(pieces - 1)

    to_partner.wait_send()
    for step in range(1, chips):
        px_out(step).wait_send()
        px_pass(step).wait_send()
    for step in range(1, faces):
        gate_copy(step).wait_send()
    for p in range(pieces):
        for kind in range(3):
            owner, _ = weight_from(kind)
            here = wbuf.at[kind, pl.ds(p * depth, depth)]
            pl.when((owner <= me_f) & (me_f + 1 < faces))(
                weight_copy(kind, p, here, 1).wait_send
            )
            pl.when((owner >= me_f) & (me_f > 0))(weight_copy(kind, p, here, 0).wait_send)


def mm(a, b, dims=((1,), (0,))):
    return lax.dot_general(
        a.astype(bf16), b.astype(bf16), (dims, ((), ())), preferred_element_type=f32
    )


def split_mm(exact, wide, pieces):
    exact = exact.astype(bf16)
    total, rest = None, wide
    for _ in range(pieces):
        piece = rest.astype(bf16)
        rest = rest - piece.astype(f32)
        term = jnp.dot(exact, piece, preferred_element_type=f32)
        total = term if total is None else total + term
    return total


def mm_split(wide, exact, pieces):
    exact = exact.astype(bf16)
    total, rest = None, wide
    for _ in range(pieces):
        piece = rest.astype(bf16)
        rest = rest - piece.astype(f32)
        term = jnp.dot(piece, exact, preferred_element_type=f32)
        total = term if total is None else total + term
    return total


def scan_kernel(
    cfg, first_ref, slabs_ref, gates_ref, rate_ref, bias_ref, out_ref,
    feats, gates, row_buf, col_buf, states,
):
    chunk, per_group, tall, wide, dk = cfg
    count, width = slabs_ref.shape[1:]
    strips, block, _ = out_ref.shape
    heads = gates_ref.shape[1] // 2
    first = first_ref[0]

    lane = lax.broadcasted_iota(jnp.int32, (width, width), 1)
    sub = lax.broadcasted_iota(jnp.int32, (width, width), 0)
    same_head = (lane // dk) == (sub // dk)
    head_ones = same_head.astype(f32)
    ti = lax.broadcasted_iota(jnp.int32, (chunk, chunk), 0)
    tj = lax.broadcasted_iota(jnp.int32, (chunk, chunk), 1)
    inclusive = ti >= tj
    tri = inclusive.astype(f32)
    eye = (ti == tj).astype(f32)

    def prepare(i, carry):
        at = pl.ds(pl.multiple_of(i * chunk, chunk), chunk)
        for kind in range(3):
            x = slabs_ref[kind, at, :].astype(f32)
            if kind < 2:
                x = x * lax.rsqrt(mm_split(x * x, head_ones, 2) + 1e-06)
            feats[kind, at, :] = x
        for a in range(per_group):
            head = first + a
            decay = -rate_ref[head] * jnp.exp(gates_ref[i, pl.ds(head, 1), :])
            strength = jax.nn.sigmoid(gates_ref[i, pl.ds(heads + head, 1), :] + bias_ref[head])
            gates[a, at, :] = jnp.broadcast_to(decay, (chunk, chunk)).T
            gates[per_group + a, at, :] = jnp.broadcast_to(strength, (chunk, chunk)).T
        return carry

    lax.fori_loop(0, count // chunk, prepare, 0, unroll=count // chunk <= 4)

    columns = chunk // tall
    flane = lax.broadcasted_iota(jnp.int32, (chunk, width), 1) // dk

    def lanes_of(parts):
        out = parts[0][:, :width]
        for a in range(1, per_group):
            out = jnp.where(flane == a, parts[a][:, :width], out)
        return out

    def stacked(x):
        if per_group == 1:
            return x
        return jnp.concatenate(
            [jnp.where(flane == a, x, jnp.zeros_like(x)) for a in range(per_group)], axis=0
        )

    def side_by_side(parts):
        return parts[0] if per_group == 1 else jnp.concatenate(parts, axis=1)

    def load(ref, which, i, by_column):
        if not by_column:
            return ref[which, pl.ds(pl.multiple_of(i * chunk, chunk), chunk), :]
        return jnp.concatenate(
            [ref[which, pl.ds(i * columns + c, tall, stride=wide), :] for c in range(columns)],
            axis=0,
        )

    states[...] = jnp.zeros_like(states)

    def advance(i, carry):
        work = []
        for order in range(2):
            q, k, v = (load(feats, kind, i, order) for kind in range(3))
            cums, betas, systems, scores = [], [], [], []
            for a in range(per_group):
                cum = split_mm(tri, load(gates, a, i, order), 3)
                beta = load(gates, per_group + a, i, order)
                gap = cum - cum.T
                within = jnp.where(inclusive, jnp.exp(jnp.where(inclusive, gap, 0.0)), 0.0)
                k_a = k if per_group == 1 else jnp.where(flane == a, k, 0.0)
                q_a = q if per_group == 1 else jnp.where(flane == a, q, 0.0)
                dots = mm(jnp.concatenate([k_a, q_a], axis=0), k, ((1,), (1,)))
                systems.append(within * dots[:chunk] * beta)
                scores.append(within * dots[chunk:])
                cums.append(cum)
                betas.append(beta)
            work.append((q, k, v, cums, betas, systems, scores))

        inverses = [[None] * per_group for _ in range(2)]
        half = 1
        while half < chunk:
            here = ((ti // (2 * half)) == (tj // (2 * half))) & (
                (lax.rem(ti, 2 * half) >= half) & (lax.rem(tj, 2 * half) < half)
            )
            lows = [
                [jnp.where(here, work[o][5][a], 0.0) for a in range(per_group)] for o in range(2)
            ]
            if half == 1:
                inverses = [[eye - low for low in row] for row in lows]
            else:
                firsts = [
                    [mm(lows[o][a], inverses[o][a]) for a in range(per_group)] for o in range(2)
                ]
                inverses = [
                    [inverses[o][a] - mm(inverses[o][a], firsts[o][a]) for a in range(per_group)]
                    for o in range(2)
                ]
            half *= 2

        for order in range(2):
            q, k, v, cums, betas, _, scores = work[order]
            beta = lanes_of(betas)
            cum = lanes_of(cums)
            scale = jnp.exp(cum)
            last = cum[chunk - 1 : chunk, :]
            tail = jnp.exp(last - cum)
            both = side_by_side(inverses[order])
            u = mm(both, stacked(v * beta))
            w = mm(both, stacked(k * (beta * scale)))
            state = states[order]
            fresh = u - mm(w, state)
            out = mm(q * scale, state) + mm(side_by_side(scores), stacked(fresh))
            grown = mm(k * tail, fresh, ((0,), (0,)))
            decayed = state * jnp.exp(last)
            states[order] = decayed + jnp.where(same_head, grown, 0.0)
            normed = out * lax.rsqrt(mm_split(out * out, head_ones, 2) * (1.0 / dk) + 1e-06)
            if order == 0:
                row_buf[pl.ds(pl.multiple_of(i * chunk, chunk), chunk), :] = normed
            else:
                normed = normed.astype(bf16).astype(f32)
                for c in range(columns):
                    col_buf[pl.ds(i * columns + c, tall, stride=wide), :] = normed[
                        c * tall : (c + 1) * tall
                    ]
        return carry

    lax.fori_loop(0, count // chunk, advance, 0)

    def finish(s, carry):
        at = pl.ds(s * block, block)
        out_ref[s] = (row_buf[at, :] + col_buf[at, :]).astype(bf16)
        return carry

    lax.fori_loop(0, strips, finish, 0)


def return_kernel(strips, groups, mixed_ref, out_ref, send_sem, recv_sem):
    me_f, me_s = lax.axis_index("face"), lax.axis_index("strip")
    rep = strips // groups
    barrier = pltpu.get_barrier_semaphore()
    for step in range(1, strips):
        pl.semaphore_signal(
            barrier, inc=1, device_id=(me_f, lax.rem(me_s + step, strips)), device_id_type=MESH
        )
    pl.semaphore_wait(barrier, strips - 1)
    mine = group_of(me_s, strips, groups)
    sends = lax.rem(me_s, rep) == 0

    def copy(step):
        dest = lax.rem(me_s + step, strips)
        return pltpu.make_async_remote_copy(
            src_ref=mixed_ref.at[dest],
            dst_ref=out_ref.at[mine],
            send_sem=send_sem.at[step],
            recv_sem=recv_sem.at[mine],
            device_id=(me_f, dest),
            device_id_type=MESH,
        )

    @pl.when(sends)
    def _():
        for step in range(1, strips):
            copy(step).start()
        pltpu.make_async_copy(mixed_ref.at[me_s], out_ref.at[mine], recv_sem.at[mine]).start()
        for step in range(1, strips):
            copy(step).wait_send()

    for group in range(groups):
        pltpu.make_async_copy(mixed_ref.at[0], out_ref.at[group], recv_sem.at[group]).wait()


def scan_call(
    first, slabs, gates, decay_rate, beta_bias, strips, per_group, tall, wide, dk
):
    count, width = slabs.shape[1:]
    block = count // strips
    chunk = min(128, count)
    vmem = pl.BlockSpec(memory_space=pltpu.VMEM)
    smem = pl.BlockSpec(memory_space=pltpu.SMEM)
    return pl.pallas_call(
        functools.partial(scan_kernel, (chunk, per_group, tall, wide, dk)),
        out_shape=jax.ShapeDtypeStruct((strips, block, width), bf16),
        in_specs=[smem, vmem, vmem, smem, smem],
        out_specs=vmem,
        scratch_shapes=[
            pltpu.VMEM((3, count, width), f32),
            pltpu.VMEM((2 * per_group, count, chunk), f32),
            pltpu.VMEM((count, width), f32),
            pltpu.VMEM((count, width), f32),
            pltpu.VMEM((2, width, width), f32),
        ],
        name="scans",
    )(first, slabs, gates, decay_rate, beta_bias)


LEVELS = 6
SPAN = 1 << LEVELS


def fused_kernel(
    cfg, px_ref, wq_ref, wg_ref, rate_ref, bias_ref, out_ref,
    px_all, wbuf, wg_own, g_out, g_in, g_rows, masks, flat, ordered, cums, sides,
    inv, into, trans, keyed, reads, asks, states, outs, mixed,
    px_send, px_fwd, px_recv, w_send, w_recv, g_send, g_recv, wg_sem, r_send, r_recv,
):
    faces, strips, n_slab, pieces, tall, wide = cfg
    me_f, me_s = lax.axis_index("face"), lax.axis_index("strip")
    block, features = px_ref.shape
    count = strips * block
    width = wbuf.shape[2]
    dk = width // 2
    heads = rate_ref.shape[0]
    gate_cols = wg_ref.shape[0]
    chips = strips // 2
    core, chip = lax.rem(me_s, 2), me_s // 2
    partner = chip * 2 + (1 - core)
    group = group_of(lax.rem(me_s + strips // 2, strips), strips, strips)
    depth = features // pieces
    spans = count // SPAN
    columns = SPAN // tall

    barrier = pltpu.get_barrier_semaphore()
    for step in range(1, strips):
        pl.semaphore_signal(
            barrier, inc=1, device_id=(me_f, lax.rem(me_s + step, strips)), device_id_type=MESH
        )
    for step in range(1, faces):
        pl.semaphore_signal(
            barrier, inc=1, device_id=(lax.rem(me_f + step, faces), me_s), device_id_type=MESH
        )

    def chip_at(step, on=None):
        other, bit = chip, 1
        while bit < chips:
            if step & bit:
                other = other + bit - 2 * bit * lax.rem(other // bit, 2)
            bit *= 2
        return other * 2 + (core if on is None else on)

    def rows_of(strip):
        return px_all.at[pl.ds(pl.multiple_of(strip * block, block), block)]

    def weight_from(kind):
        slab = kind * strips + group
        return slab // n_slab, lax.rem(slab, n_slab)

    def weight_src(j, p):
        return wq_ref.at[pl.ds(p * depth, depth), pl.ds(pl.multiple_of(j * width, width), width)]

    def weight_at(kind, p):
        return wbuf.at[kind, pl.ds(p * depth, depth)]

    def weight_copy(kind, p, src, dest):
        return pltpu.make_async_remote_copy(
            src_ref=src,
            dst_ref=weight_at(kind, p),
            send_sem=w_send.at[kind, p, dest],
            recv_sem=w_recv.at[kind, p],
            device_id=(dest, me_s),
            device_id_type=MESH,
        )

    def own_weight(kind, p, j):
        return pltpu.make_async_copy(weight_src(j, p), weight_at(kind, p), w_recv.at[kind, p])

    def weight_wait(kind, p):
        here = weight_at(kind, p)
        pltpu.make_async_copy(here, here, w_recv.at[kind, p]).wait()

    def relays(owner, dest):
        up = (dest == me_f + 1) & (owner == me_f - 1)
        return up | ((dest == me_f - 1) & (owner == me_f + 1))

    def direct(owner, dest, far):
        gap = jnp.abs(dest - me_f)
        return (owner == me_f) & ((gap > 2) if far else (gap == 1))

    def sends(owner, dest):
        return direct(owner, dest, False) | direct(owner, dest, True) | relays(owner, dest)

    def gate_from(which):
        column = which * heads + group * 2
        return column // gate_cols, lax.rem(column, gate_cols)

    def gate_copy(which, dest):
        return pltpu.make_async_remote_copy(
            src_ref=g_out.at[which],
            dst_ref=g_in.at[which],
            send_sem=g_send.at[which, dest],
            recv_sem=g_recv.at[which],
            device_id=(dest, me_s),
            device_id_type=MESH,
        )

    lines = features // width

    def pick_gates():
        here = wg_own[...].astype(f32)
        row_of = lax.broadcasted_iota(jnp.int32, here.shape, 0)
        for which in range(2):
            owner, row = gate_from(which)

            @pl.when(owner == me_f)
            def _(which=which, row=row):
                picked = [
                    jnp.sum(jnp.where(row_of == row + a, here, 0.0), axis=0, keepdims=True)
                    for a in range(2)
                ]
                parts = [
                    picked[a][:, i * width : (i + 1) * width]
                    for a in range(2)
                    for i in range(lines)
                ]
                g_out[which] = jnp.concatenate(parts, axis=0).astype(bf16)

    def send_gates():
        for which in range(2):
            owner, _ = gate_from(which)

            @pl.when(owner == me_f)
            def _(which=which):
                for dest in range(faces):
                    pl.when(dest != me_f)(gate_copy(which, dest).start)
                pltpu.make_async_copy(g_out.at[which], g_in.at[which], g_recv.at[which]).start()

    own_px = pltpu.make_async_copy(px_ref, rows_of(me_s), px_recv.at[me_s])
    own_px.start()
    own_gate = pltpu.make_async_copy(wg_ref, wg_own, wg_sem.at[0])
    own_gate.start()
    own_gate.wait()
    pick_gates()
    pl.semaphore_wait(barrier, strips - 1 + faces - 1)
    send_gates()

    def send_weights(kind, far):
        owner, j = weight_from(kind)

        @pl.when(owner == me_f)
        def _():
            for p in range(pieces):
                for dest in range(faces):
                    pl.when(direct(owner, dest, far))(
                        weight_copy(kind, p, weight_src(j, p), dest).start
                    )

    def own_weights(kind):
        owner, j = weight_from(kind)

        @pl.when(owner == me_f)
        def _():
            for p in range(pieces):
                own_weight(kind, p, j).start()

    send_weights(1, False)
    send_weights(1, True)
    def px_copy(dest, sem, source, src):
        return pltpu.make_async_remote_copy(
            src_ref=src,
            dst_ref=rows_of(source),
            send_sem=sem,
            recv_sem=px_recv.at[source],
            device_id=(me_f, dest),
            device_id_type=MESH,
        )

    def px_out(step):
        return px_copy(chip_at(step), px_send.at[step], me_s, px_ref)

    def px_pass(step):
        source = chip_at(step)
        return px_copy(partner, px_fwd.at[step], source, rows_of(source))

    to_partner = px_copy(partner, px_send.at[0], me_s, px_ref)
    for step in range(1, chips):
        px_out(step).start()
    to_partner.start()
    own_weights(1)

    ti = lax.broadcasted_iota(jnp.int32, (width, width), 0)
    tj = lax.broadcasted_iota(jnp.int32, (width, width), 1)
    for level in range(LEVELS):
        half = 1 << level
        here = (ti // (2 * half)) == (tj // (2 * half))
        here = here & (lax.rem(ti, 2 * half) >= half) & (lax.rem(tj, 2 * half) < half)
        masks[level] = here.astype(f32).astype(bf16)
    eye = (ti == tj).astype(f32)
    masks[LEVELS] = eye.astype(bf16)
    same_head = (ti // dk) == (tj // dk)
    masks[LEVELS + 1] = same_head.astype(f32).astype(bf16)
    tri = same_head & (ti >= tj)
    masks[LEVELS + 2] = tri.astype(f32).astype(bf16)

    def px_wait(strip):
        pltpu.make_async_copy(px_ref, rows_of(strip), px_recv.at[strip]).wait()

    def pass_pixels(step):
        px_wait(chip_at(step))
        px_pass(step).start()

    def relayed(owner):
        return (jnp.abs(owner - me_f) == 1) & (
            ((2 * me_f - owner) >= 0) & ((2 * me_f - owner) < faces)
        )

    def pass_weights(kind, p):
        owner, _ = weight_from(kind)

        @pl.when(relayed(owner))
        def _():
            weight_wait(kind, p)
            for dest in range(faces):
                pl.when(relays(owner, dest))(weight_copy(kind, p, weight_at(kind, p), dest).start)

    for p in range(pieces):
        pass_weights(1, p)
    for kind in (0, 2):
        send_weights(kind, False)
    for kind in (0, 2):
        own_weights(kind)
    for step in range(1, chips):
        pass_pixels(step)
    for p in range(pieces):
        for kind in (0, 2):
            pass_weights(kind, p)

    for which in range(2):
        pltpu.make_async_copy(g_in.at[which], g_in.at[which], g_recv.at[which]).wait()
        got = g_in[which].astype(f32)
        for a in range(2):
            for i in range(lines):
                line = got[a * lines + i : a * lines + i + 1, :]
                at = which * width + a * dk
                g_rows[at : at + dk, i * width : (i + 1) * width] = jnp.broadcast_to(
                    line, (dk, width)
                ).astype(bf16)
    px_wait(me_s)
    px_wait(partner)
    for step in range(1, chips):
        px_wait(chip_at(step, 1 - core))

    lane = lax.broadcasted_iota(jnp.int32, (1, width), 1) // dk
    first = group * 2

    def by_head(ref):
        return jnp.where(lane == 0, ref[first], ref[first + 1])

    logits = lax.dot_general(
        px_all[...], g_rows[...], (((1,), (1,)), ((), ())), preferred_element_type=f32
    )
    logits = logits.astype(bf16).astype(f32)
    flat[0] = -by_head(rate_ref) * jnp.exp(logits[:, :width])
    flat[1] = jax.nn.sigmoid(logits[:, width:] + by_head(bias_ref))

    head_ones = masks[LEVELS + 1]

    def features_of(kind):
        owner, _ = weight_from(kind)
        for p in range(pieces):
            pl.when(jnp.logical_not(relayed(owner)))(functools.partial(weight_wait, kind, p))
        if kind == 1:
            for late in (0, 2):
                send_weights(late, True)
        x = jnp.dot(px_all[...], wbuf[kind], preferred_element_type=f32)
        x = x.astype(bf16).astype(f32)
        if kind < 2:
            x = x * lax.rsqrt(mm(x * x, head_ones) + 1e-06)
        flat[2 + kind] = x

    def rows_at(i):
        return pl.ds(i * SPAN if isinstance(i, int) else pl.multiple_of(i * SPAN, SPAN), SPAN)

    def load(which, i, by_column):
        if not by_column:
            return flat[which, rows_at(i), :]
        return jnp.concatenate(
            [flat[which, pl.ds(i * columns + c, tall, stride=wide), :] for c in range(columns)],
            axis=0,
        )

    half_masks = [(lane == a).astype(f32).astype(bf16) for a in range(2)]

    def stacked(x):
        x = x.astype(bf16)
        return jnp.concatenate([x * half_masks[0], x * half_masks[1]], axis=0)

    def twice(x):
        return jnp.concatenate([x, x], axis=0)

    def slot(i, o):
        return i * 2 + o

    ri = lax.broadcasted_iota(jnp.int32, (SPAN, width), 0)
    rj = lax.rem(lax.broadcasted_iota(jnp.int32, (SPAN, width), 1), dk)
    inclusive = ri >= rj

    units_all = [(i, o) for i in range(spans) for o in range(2)]

    def each_span(body, per_turn):
        def turn(t, carry):
            body([(t * per_turn + u, o) for u in range(per_turn) for o in range(2)])
            return carry

        lax.fori_loop(0, spans // per_turn, turn, 0)

    def key_stage(units):
        lows, tails, kbs = [], [], []
        for i, o in units:
            decay, beta, k = load(0, i, o), load(1, i, o), load(3, i, o)
            cum = split_mm(masks[LEVELS + 2], twice(decay), 3)[:SPAN]
            turned = twice(cum).T
            across = jnp.where(lane == 0, turned[0:1, :], turned[dk : dk + 1, :])
            gap = cum - across
            within = jnp.exp(jnp.where(inclusive, gap, -1e30))
            ks = stacked(k)
            gram = mm(k, ks, ((1,), (1,)))
            lows.append(twice((within * gram * beta).astype(bf16)))
            scale = jnp.exp(cum)
            last = cum[SPAN - 1 : SPAN, :]
            tails.append(stacked(k * jnp.exp(last - cum)))
            kb = stacked(k * (beta * scale))
            kbs.append(kb)
            at = slot(i, o)
            cums[at] = jnp.exp(last)
            ordered[0, at] = scale
            ordered[1, at] = within
            sides[0, at] = ks
            sides[1, at] = kb
        xs = [masks[LEVELS] - low * masks[0] for low in lows]
        for level in range(1, LEVELS):
            mids = [mm(low * masks[level], x) for low, x in zip(lows, xs)]
            ends = [mm(x, mid) for x, mid in zip(xs, mids)]
            xs = [x - end.astype(bf16) for x, end in zip(xs, ends)]
        hs = [mm(tail, x, ((0,), (0,))).astype(bf16) for tail, x in zip(tails, xs)]
        ms = [mm(h, kb).astype(bf16) for h, kb in zip(hs, kbs)]
        for (i, o), x, h, m in zip(units, xs, hs, ms):
            at = slot(i, o)
            inv[at] = x
            into[at] = h
            trans[at] = m

    def query_stage(units):
        for i, o in units:
            at = slot(i, o)
            q = load(2, i, o)
            scores = ordered[1, at] * mm(q, sides[0, at], ((1,), (1,)))
            g = mm(scores, inv[at]).astype(bf16)
            reads[at] = g
            asks[at] = (q * ordered[0, at] - mm(g, sides[1, at])).astype(bf16)

    def value_stage(units):
        for i, o in units:
            at = slot(i, o)
            vb = stacked(load(4, i, o) * load(1, i, o))
            keyed[at] = mm(into[at], vb)
            sides[2, at] = vb

    def value_scan():
        features_of(2)
        each_span(value_stage, 4)
        state = [jnp.zeros((width, width), f32) for _ in range(2)]
        for i in range(spans):
            for o in range(2):
                at = slot(i, o)
                held = state[o].astype(bf16)
                states[at] = held
                if i < spans - 1:
                    state[o] = state[o] * cums[at] + (keyed[at] - mm(trans[at], held))

    queries_last = me_f * 2 >= faces
    features_of(1)
    key_stage(units_all)
    pl.when(queries_last)(value_scan)
    features_of(0)
    each_span(query_stage, 4)
    pl.when(jnp.logical_not(queries_last))(value_scan)

    def output_stage(units):
        for i, o in units:
            at = slot(i, o)
            out = mm(reads[at], sides[2, at]) + mm(asks[at], states[at])
            if o == 0:
                outs[0, rows_at(i), :] = out
            else:
                for c in range(columns):
                    outs[1, pl.ds(i * columns + c, tall, stride=wide), :] = out[
                        c * tall : (c + 1) * tall
                    ]

    each_span(output_stage, 4)
    normed = []
    for o in range(2):
        x = outs[o]
        normed.append(x * lax.rsqrt(mm(x * x, head_ones) * (1.0 / dk) + 1e-06))
    total = (normed[0] + normed[1].astype(bf16).astype(f32)).astype(bf16)
    for s in range(strips):
        mixed[s] = total[s * block : (s + 1) * block]

    def lanes_of(owner):
        return out_ref.at[:, pl.ds(pl.multiple_of(owner * width, width), width)]

    def give(step):
        dest = lax.rem(me_s + step, strips)
        return pltpu.make_async_remote_copy(
            src_ref=mixed.at[dest],
            dst_ref=lanes_of(group),
            send_sem=r_send.at[step],
            recv_sem=r_recv.at[group],
            device_id=(me_f, dest),
            device_id_type=MESH,
        )

    for step in range(1, strips):
        give(step).start()
    pltpu.make_async_copy(mixed.at[me_s], lanes_of(group), r_recv.at[group]).start()

    to_partner.wait_send()
    for step in range(1, chips):
        px_out(step).wait_send()
        px_pass(step).wait_send()
    for which in range(2):
        owner, _ = gate_from(which)
        for dest in range(faces):
            pl.when((owner == me_f) & (dest != me_f))(gate_copy(which, dest).wait_send)
    for p in range(pieces):
        for kind in range(3):
            owner, _ = weight_from(kind)
            for dest in range(faces):
                pl.when(sends(owner, dest))(
                    weight_copy(kind, p, weight_at(kind, p), dest).wait_send
                )
    for owner in range(strips):
        pltpu.make_async_copy(mixed.at[0], lanes_of(owner), r_recv.at[owner]).wait()
    for step in range(1, strips):
        give(step).wait_send()


def fused_call(faces, strips, px, w_qkv, w_gate_t, decay_rate, beta_bias, tall, wide):
    block, features = px.shape
    count = block * strips
    width = w_qkv.shape[1] * faces // 3 // strips
    units = 2 * count // SPAN
    pieces = 2
    vmem = pl.BlockSpec(memory_space=pltpu.VMEM)
    smem = pl.BlockSpec(memory_space=pltpu.SMEM)
    hbm = pl.BlockSpec(memory_space=pltpu.HBM)
    dma = pltpu.SemaphoreType.DMA
    square = (units, width, width)
    return pl.pallas_call(
        functools.partial(
            fused_kernel, (faces, strips, w_qkv.shape[1] // width, pieces, tall, wide)
        ),
        out_shape=jax.ShapeDtypeStruct((block, strips * width), bf16),
        in_specs=[hbm, hbm, hbm, smem, smem],
        out_specs=pl.BlockSpec(memory_space=pl.ANY),
        scratch_shapes=[
            pltpu.VMEM((count, features), bf16),
            pltpu.VMEM((3, features, width), bf16),
            pltpu.VMEM(w_gate_t.shape, bf16),
            pltpu.VMEM((2, 2 * features // width, width), bf16),
            pltpu.VMEM((2, 2 * features // width, width), bf16),
            pltpu.VMEM((2 * width, features), bf16),
            pltpu.VMEM((LEVELS + 3, width, width), bf16),
            pltpu.VMEM((5, count, width), f32),
            pltpu.VMEM((2, units, SPAN, width), f32),
            pltpu.VMEM((units, 1, width), f32),
            pltpu.VMEM((3,) + square, bf16),
            pltpu.VMEM(square, bf16),
            pltpu.VMEM(square, bf16),
            pltpu.VMEM(square, bf16),
            pltpu.VMEM(square, f32),
            pltpu.VMEM((units, SPAN, width), bf16),
            pltpu.VMEM((units, SPAN, width), bf16),
            pltpu.VMEM(square, bf16),
            pltpu.VMEM((2, count, width), f32),
            pltpu.VMEM((strips, block, width), bf16),
            dma((strips // 2,)),
            dma((strips // 2,)),
            dma((strips,)),
            dma((3, pieces, faces)),
            dma((3, pieces)),
            dma((2, faces)),
            dma((2,)),
            dma((1,)),
            dma((strips,)),
            dma((strips,)),
        ],
        compiler_params=pltpu.CompilerParams(
            collective_id=2, has_side_effects=True, vmem_limit_bytes=20 * 2**20
        ),
        name="layer",
    )(*[
        pltpu.with_memory_space_constraint(x, pltpu.HBM)
        for x in (px, w_qkv, w_gate_t, decay_rate, beta_bias)
    ])


def fits_fused(strips, heads, dk, count, tall, wide, gate_cols, features, block):
    return (
        heads == 2 * strips
        and dk == SPAN
        and 2 * dk == 128
        and strips & (strips - 1) == 0
        and strips > 1
        and count % (4 * SPAN) == 0
        and count <= 1024
        and block % 16 == 0
        and tall % 8 == 0
        and SPAN % tall == 0
        and wide % (SPAN // tall) == 0
        and gate_cols % 8 == 0
        and features % 1024 == 0
    )


def on_device(faces, strips, pixels_in, w_qkv, w_gate, decay_rate, beta_bias):
    _, rows_here, wide, features = pixels_in.shape
    heads = decay_rate.shape[0]
    block = rows_here * wide
    count = block * strips
    tall = rows_here * strips
    model = w_qkv.shape[1] * faces // 3
    dk = model // heads
    groups = min(strips, heads)
    per_group = heads // groups
    width = per_group * dk
    n_slab = w_qkv.shape[1] // width
    gate_cols = w_gate.shape[1]
    if fits_fused(strips, heads, dk, count, tall, wide, gate_cols, features, block):
        out = fused_call(
            faces, strips, pixels_in.reshape(block, features), w_qkv, w_gate.T,
            decay_rate, beta_bias, tall, wide,
        )
        return out.reshape(1, rows_here, wide, model)
    pieces = 4
    chunk = min(128, count)
    chips = strips // 2
    vmem = pl.BlockSpec(memory_space=pltpu.VMEM)
    dma = pltpu.SemaphoreType.DMA
    if width % 128:
        w_qkv = w_qkv.reshape(features, n_slab, width).transpose(1, 0, 2)
    slabs, gates = pl.pallas_call(
        functools.partial(project_kernel, (faces, strips, groups, n_slab, pieces)),
        out_shape=(
            jax.ShapeDtypeStruct((3, count, width), bf16),
            jax.ShapeDtypeStruct((count // chunk, 2 * heads, chunk), f32),
        ),
        in_specs=[vmem, pl.BlockSpec(memory_space=pl.ANY), vmem],
        out_specs=(vmem, vmem),
        scratch_shapes=[
            pltpu.VMEM((count, features), bf16),
            pltpu.VMEM((3, features, width), bf16),
            pltpu.VMEM((gate_cols, features), f32),
            pltpu.VMEM((faces, gate_cols, features), f32),
            pltpu.VMEM((count, 3 * width), f32),
            dma((chips,)),
            dma((chips,)),
            dma((strips,)),
            dma((3, pieces, 2)),
            dma((3, pieces)),
            dma((faces,)),
            dma((faces,)),
        ],
        compiler_params=pltpu.CompilerParams(collective_id=0, has_side_effects=True),
        name="project",
    )(pixels_in.reshape(block, features), w_qkv, w_gate.T)
    group = group_of(lax.axis_index("strip"), strips, groups)
    first = (group * per_group).astype(jnp.int32).reshape(1)
    mixed = scan_call(
        first, slabs, gates, decay_rate, beta_bias, strips, per_group, tall, wide, dk
    )
    returned = pl.pallas_call(
        functools.partial(return_kernel, strips, groups),
        out_shape=jax.ShapeDtypeStruct((groups, block, width), bf16),
        in_specs=[vmem],
        out_specs=vmem,
        scratch_shapes=[dma((strips,)), dma((groups,))],
        compiler_params=pltpu.CompilerParams(collective_id=1, has_side_effects=True),
        name="give_back",
    )(mixed)
    return returned.transpose(1, 0, 2).reshape(1, rows_here, wide, model)


def solution(mesh):
    in_specs = (P("face", "strip", None, None), P(None, "face"), P(None, "face"), P(), P())
    out_specs = P("face", "strip", None, None)
    return jax.shard_map(
        functools.partial(on_device, mesh.shape["face"], mesh.shape["strip"]),
        mesh=mesh,
        in_specs=in_specs,
        out_specs=out_specs,
        check_vma=False,
    )
```

```python
import functools

import jax
import jax.numpy as jnp
from jax import lax
from jax.experimental import pallas as pl
from jax.experimental.pallas import tpu as pltpu
from jax.sharding import PartitionSpec as P

MESH = pl.DeviceIdType.MESH
f32 = jnp.float32
bf16 = jnp.bfloat16


def group_of(place, strips, groups):
    rep = strips // groups
    if rep > 1 or groups % 2:
        return place // rep
    return jnp.where(lax.rem(place, 2) == 0, place // 2, groups - 1 - place // 2)


def project_kernel(
    cfg, px_ref, wq_ref, wg_ref, slabs_ref, gates_ref,
    px_all, wbuf, wg_own, wg_all, acc, px_send, px_fwd, px_recv, w_send, w_recv, g_send, g_recv,
):
    faces, strips, groups, n_slab, pieces = cfg
    me_f, me_s = lax.axis_index("face"), lax.axis_index("strip")
    block, features = px_ref.shape
    count = strips * block
    width = wbuf.shape[2]
    chips = strips // 2
    core, chip = lax.rem(me_s, 2), me_s // 2
    partner = chip * 2 + (1 - core)
    group = group_of(me_s, strips, groups)
    depth = features // pieces

    def chip_at(step):
        return lax.rem(chip + step, chips) * 2 + core

    barrier = pltpu.get_barrier_semaphore()

    def greet(face, strip):
        pl.semaphore_signal(barrier, inc=1, device_id=(face, strip), device_id_type=MESH)

    greet(me_f, partner)
    for step in range(1, chips):
        greet(me_f, chip_at(step))
    for step in range(1, faces):
        greet(lax.rem(me_f + step, faces), me_s)

    wg_own[...] = wg_ref[...].astype(f32)

    def rows_of(strip):
        return px_all.at[pl.ds(pl.multiple_of(strip * block, block), block)]

    own_px = pltpu.make_async_copy(px_ref, rows_of(me_s), px_recv.at[me_s])
    own_px.start()
    pl.semaphore_wait(barrier, 1 + chips - 1 + faces - 1)

    def weight_from(kind):
        slab = kind * groups + group
        return slab // n_slab, lax.rem(slab, n_slab)

    def weight_src(j, p):
        rows = pl.ds(p * depth, depth)
        if len(wq_ref.shape) == 3:
            return wq_ref.at[j, rows]
        return wq_ref.at[rows, pl.ds(pl.multiple_of(j * width, width), width)]

    def weight_copy(kind, p, src, side):
        return pltpu.make_async_remote_copy(
            src_ref=src,
            dst_ref=wbuf.at[kind, pl.ds(p * depth, depth)],
            send_sem=w_send.at[kind, p, side],
            recv_sem=w_recv.at[kind, p],
            device_id=(me_f + (1 if side else -1), me_s),
            device_id_type=MESH,
        )

    def own_weight(kind, p, j):
        return pltpu.make_async_copy(
            weight_src(j, p), wbuf.at[kind, pl.ds(p * depth, depth)], w_recv.at[kind, p]
        )

    for p in range(pieces):
        for kind in range(3):
            owner, j = weight_from(kind)

            @pl.when(owner == me_f)
            def _(kind=kind, p=p, j=j):
                pl.when(me_f + 1 < faces)(weight_copy(kind, p, weight_src(j, p), 1).start)
                pl.when(me_f > 0)(weight_copy(kind, p, weight_src(j, p), 0).start)
                own_weight(kind, p, j).start()

    def px_copy(dest, sem, source, src):
        return pltpu.make_async_remote_copy(
            src_ref=src,
            dst_ref=rows_of(source),
            send_sem=sem,
            recv_sem=px_recv.at[source],
            device_id=(me_f, dest),
            device_id_type=MESH,
        )

    def px_out(step):
        return px_copy(chip_at(step), px_send.at[step], me_s, px_ref)

    def px_pass(step):
        source = chip_at(step)
        return px_copy(partner, px_fwd.at[step], source, rows_of(source))

    to_partner = px_copy(partner, px_send.at[0], me_s, px_ref)
    for step in range(1, chips):
        px_out(step).start()
    to_partner.start()

    def gate_copy(step):
        return pltpu.make_async_remote_copy(
            src_ref=wg_own,
            dst_ref=wg_all.at[me_f],
            send_sem=g_send.at[step],
            recv_sem=g_recv.at[me_f],
            device_id=(lax.rem(me_f + step, faces), me_s),
            device_id_type=MESH,
        )

    for step in range(1, faces):
        gate_copy(step).start()
    own_gate = pltpu.make_async_copy(wg_own, wg_all.at[me_f], g_recv.at[me_f])
    own_gate.start()

    def px_wait(strip):
        pltpu.make_async_copy(px_ref, rows_of(strip), px_recv.at[strip]).wait()

    def pass_pixels(step):
        px_wait(chip_at(step))
        px_pass(step).start()

    def pass_weights(p):
        for kind in range(3):
            owner, _ = weight_from(kind)
            here = wbuf.at[kind, pl.ds(p * depth, depth)]
            pltpu.make_async_copy(here, here, w_recv.at[kind, p]).wait()
            pl.when((owner < me_f) & (me_f + 1 < faces))(weight_copy(kind, p, here, 1).start)
            pl.when((owner > me_f) & (me_f > 0))(weight_copy(kind, p, here, 0).start)

    tile = min(512, count)

    def each_tile(body):
        if count == tile:
            body(pl.ds(0, tile), 0)
        else:

            def one(i, carry):
                body(pl.ds(pl.multiple_of(i * tile, tile), tile), i)
                return carry

            lax.fori_loop(0, count // tile, one, 0)

    def multiply(p):
        rows = pl.ds(p * depth, depth)
        weights = jnp.concatenate([wbuf[kind, rows, :] for kind in range(3)], axis=1)

        def body(at, _):
            term = jnp.dot(px_all[at, rows], weights, preferred_element_type=f32)
            if p > 0:
                term = term + acc[at, :]
            if p < pieces - 1:
                acc[at, :] = term
            else:
                for kind in range(3):
                    slabs_ref[kind, at, :] = term[
                        :, kind * width : (kind + 1) * width
                    ].astype(bf16)

        each_tile(body)

    for turn in range(max(pieces - 1, chips - 1)):
        if turn < pieces - 1:
            pass_weights(turn)
        if turn < chips - 1:
            pass_pixels(turn + 1)
    px_wait(me_s)
    px_wait(partner)
    for step in range(1, chips):
        px_wait(lax.rem(chip + step, chips) * 2 + (1 - core))
    for face in range(faces):
        pltpu.make_async_copy(wg_own, wg_all.at[face], g_recv.at[face]).wait()
    gate_w = jnp.concatenate([wg_all[face] for face in range(faces)], axis=0).astype(bf16)

    chunk = gates_ref.shape[2]

    def gate_body(at, i):
        logits = lax.dot_general(
            gate_w, px_all[at, :], (((1,), (1,)), ((), ())), preferred_element_type=f32
        )
        logits = logits.astype(bf16).astype(f32)
        for c in range(tile // chunk):
            gates_ref[i * (tile // chunk) + c] = logits[:, c * chunk : (c + 1) * chunk]

    each_tile(gate_body)
    for p in range(pieces - 1):
        multiply(p)
    pass_weights(pieces - 1)
    multiply(pieces - 1)

    to_partner.wait_send()
    for step in range(1, chips):
        px_out(step).wait_send()
        px_pass(step).wait_send()
    for step in range(1, faces):
        gate_copy(step).wait_send()
    for p in range(pieces):
        for kind in range(3):
            owner, _ = weight_from(kind)
            here = wbuf.at[kind, pl.ds(p * depth, depth)]
            pl.when((owner <= me_f) & (me_f + 1 < faces))(
                weight_copy(kind, p, here, 1).wait_send
            )
            pl.when((owner >= me_f) & (me_f > 0))(weight_copy(kind, p, here, 0).wait_send)


def mm(a, b, dims=((1,), (0,))):
    return lax.dot_general(
        a.astype(bf16), b.astype(bf16), (dims, ((), ())), preferred_element_type=f32
    )


def split_mm(exact, wide, pieces):
    exact = exact.astype(bf16)
    total, rest = None, wide
    for _ in range(pieces):
        piece = rest.astype(bf16)
        rest = rest - piece.astype(f32)
        term = jnp.dot(exact, piece, preferred_element_type=f32)
        total = term if total is None else total + term
    return total


def mm_split(wide, exact, pieces):
    exact = exact.astype(bf16)
    total, rest = None, wide
    for _ in range(pieces):
        piece = rest.astype(bf16)
        rest = rest - piece.astype(f32)
        term = jnp.dot(piece, exact, preferred_element_type=f32)
        total = term if total is None else total + term
    return total


def scan_kernel(
    cfg, first_ref, slabs_ref, gates_ref, rate_ref, bias_ref, out_ref,
    feats, gates, row_buf, col_buf, states,
):
    chunk, per_group, tall, wide, dk = cfg
    count, width = slabs_ref.shape[1:]
    strips, block, _ = out_ref.shape
    heads = gates_ref.shape[1] // 2
    first = first_ref[0]

    lane = lax.broadcasted_iota(jnp.int32, (width, width), 1)
    sub = lax.broadcasted_iota(jnp.int32, (width, width), 0)
    same_head = (lane // dk) == (sub // dk)
    head_ones = same_head.astype(f32)
    ti = lax.broadcasted_iota(jnp.int32, (chunk, chunk), 0)
    tj = lax.broadcasted_iota(jnp.int32, (chunk, chunk), 1)
    inclusive = ti >= tj
    tri = inclusive.astype(f32)
    eye = (ti == tj).astype(f32)

    def prepare(i, carry):
        at = pl.ds(pl.multiple_of(i * chunk, chunk), chunk)
        for kind in range(3):
            x = slabs_ref[kind, at, :].astype(f32)
            if kind < 2:
                x = x * lax.rsqrt(mm_split(x * x, head_ones, 2) + 1e-06)
            feats[kind, at, :] = x
        for a in range(per_group):
            head = first + a
            decay = -rate_ref[head] * jnp.exp(gates_ref[i, pl.ds(head, 1), :])
            strength = jax.nn.sigmoid(gates_ref[i, pl.ds(heads + head, 1), :] + bias_ref[head])
            gates[a, at, :] = jnp.broadcast_to(decay, (chunk, chunk)).T
            gates[per_group + a, at, :] = jnp.broadcast_to(strength, (chunk, chunk)).T
        return carry

    lax.fori_loop(0, count // chunk, prepare, 0, unroll=count // chunk <= 4)

    columns = chunk // tall
    flane = lax.broadcasted_iota(jnp.int32, (chunk, width), 1) // dk

    def lanes_of(parts):
        out = parts[0][:, :width]
        for a in range(1, per_group):
            out = jnp.where(flane == a, parts[a][:, :width], out)
        return out

    def stacked(x):
        if per_group == 1:
            return x
        return jnp.concatenate(
            [jnp.where(flane == a, x, jnp.zeros_like(x)) for a in range(per_group)], axis=0
        )

    def side_by_side(parts):
        return parts[0] if per_group == 1 else jnp.concatenate(parts, axis=1)

    def load(ref, which, i, by_column):
        if not by_column:
            return ref[which, pl.ds(pl.multiple_of(i * chunk, chunk), chunk), :]
        return jnp.concatenate(
            [ref[which, pl.ds(i * columns + c, tall, stride=wide), :] for c in range(columns)],
            axis=0,
        )

    states[...] = jnp.zeros_like(states)

    def advance(i, carry):
        work = []
        for order in range(2):
            q, k, v = (load(feats, kind, i, order) for kind in range(3))
            cums, betas, systems, scores = [], [], [], []
            for a in range(per_group):
                cum = split_mm(tri, load(gates, a, i, order), 3)
                beta = load(gates, per_group + a, i, order)
                gap = cum - cum.T
                within = jnp.where(inclusive, jnp.exp(jnp.where(inclusive, gap, 0.0)), 0.0)
                k_a = k if per_group == 1 else jnp.where(flane == a, k, 0.0)
                q_a = q if per_group == 1 else jnp.where(flane == a, q, 0.0)
                dots = mm(jnp.concatenate([k_a, q_a], axis=0), k, ((1,), (1,)))
                systems.append(within * dots[:chunk] * beta)
                scores.append(within * dots[chunk:])
                cums.append(cum)
                betas.append(beta)
            work.append((q, k, v, cums, betas, systems, scores))

        inverses = [[None] * per_group for _ in range(2)]
        half = 1
        while half < chunk:
            here = ((ti // (2 * half)) == (tj // (2 * half))) & (
                (lax.rem(ti, 2 * half) >= half) & (lax.rem(tj, 2 * half) < half)
            )
            lows = [
                [jnp.where(here, work[o][5][a], 0.0) for a in range(per_group)] for o in range(2)
            ]
            if half == 1:
                inverses = [[eye - low for low in row] for row in lows]
            else:
                firsts = [
                    [mm(lows[o][a], inverses[o][a]) for a in range(per_group)] for o in range(2)
                ]
                inverses = [
                    [inverses[o][a] - mm(inverses[o][a], firsts[o][a]) for a in range(per_group)]
                    for o in range(2)
                ]
            half *= 2

        for order in range(2):
            q, k, v, cums, betas, _, scores = work[order]
            beta = lanes_of(betas)
            cum = lanes_of(cums)
            scale = jnp.exp(cum)
            last = cum[chunk - 1 : chunk, :]
            tail = jnp.exp(last - cum)
            both = side_by_side(inverses[order])
            u = mm(both, stacked(v * beta))
            w = mm(both, stacked(k * (beta * scale)))
            state = states[order]
            fresh = u - mm(w, state)
            out = mm(q * scale, state) + mm(side_by_side(scores), stacked(fresh))
            grown = mm(k * tail, fresh, ((0,), (0,)))
            decayed = state * jnp.exp(last)
            states[order] = decayed + jnp.where(same_head, grown, 0.0)
            normed = out * lax.rsqrt(mm_split(out * out, head_ones, 2) * (1.0 / dk) + 1e-06)
            if order == 0:
                row_buf[pl.ds(pl.multiple_of(i * chunk, chunk), chunk), :] = normed
            else:
                normed = normed.astype(bf16).astype(f32)
                for c in range(columns):
                    col_buf[pl.ds(i * columns + c, tall, stride=wide), :] = normed[
                        c * tall : (c + 1) * tall
                    ]
        return carry

    lax.fori_loop(0, count // chunk, advance, 0)

    def finish(s, carry):
        at = pl.ds(s * block, block)
        out_ref[s] = (row_buf[at, :] + col_buf[at, :]).astype(bf16)
        return carry

    lax.fori_loop(0, strips, finish, 0)


def return_kernel(strips, groups, mixed_ref, out_ref, send_sem, recv_sem):
    me_f, me_s = lax.axis_index("face"), lax.axis_index("strip")
    rep = strips // groups
    barrier = pltpu.get_barrier_semaphore()
    for step in range(1, strips):
        pl.semaphore_signal(
            barrier, inc=1, device_id=(me_f, lax.rem(me_s + step, strips)), device_id_type=MESH
        )
    pl.semaphore_wait(barrier, strips - 1)
    mine = group_of(me_s, strips, groups)
    sends = lax.rem(me_s, rep) == 0

    def copy(step):
        dest = lax.rem(me_s + step, strips)
        return pltpu.make_async_remote_copy(
            src_ref=mixed_ref.at[dest],
            dst_ref=out_ref.at[mine],
            send_sem=send_sem.at[step],
            recv_sem=recv_sem.at[mine],
            device_id=(me_f, dest),
            device_id_type=MESH,
        )

    @pl.when(sends)
    def _():
        for step in range(1, strips):
            copy(step).start()
        pltpu.make_async_copy(mixed_ref.at[me_s], out_ref.at[mine], recv_sem.at[mine]).start()
        for step in range(1, strips):
            copy(step).wait_send()

    for group in range(groups):
        pltpu.make_async_copy(mixed_ref.at[0], out_ref.at[group], recv_sem.at[group]).wait()


def scan_call(
    first, slabs, gates, decay_rate, beta_bias, strips, per_group, tall, wide, dk
):
    count, width = slabs.shape[1:]
    block = count // strips
    chunk = min(128, count)
    vmem = pl.BlockSpec(memory_space=pltpu.VMEM)
    smem = pl.BlockSpec(memory_space=pltpu.SMEM)
    return pl.pallas_call(
        functools.partial(scan_kernel, (chunk, per_group, tall, wide, dk)),
        out_shape=jax.ShapeDtypeStruct((strips, block, width), bf16),
        in_specs=[smem, vmem, vmem, smem, smem],
        out_specs=vmem,
        scratch_shapes=[
            pltpu.VMEM((3, count, width), f32),
            pltpu.VMEM((2 * per_group, count, chunk), f32),
            pltpu.VMEM((count, width), f32),
            pltpu.VMEM((count, width), f32),
            pltpu.VMEM((2, width, width), f32),
        ],
        name="scans",
    )(first, slabs, gates, decay_rate, beta_bias)


LEVELS = 6
SPAN = 1 << LEVELS


def fused_kernel(
    cfg, px_ref, wq_ref, wg_ref, rate_ref, bias_ref, out_ref,
    px_all, wbuf, wg_own, g_out, g_in, g_rows, masks, flat, ordered, cums, sides,
    inv, into, trans, keyed, reads, asks, states, outs, mixed,
    px_send, px_fwd, px_recv, w_send, w_recv, g_send, g_recv, wg_sem, r_send, r_recv,
):
    faces, strips, n_slab, pieces, tall, wide = cfg
    me_f, me_s = lax.axis_index("face"), lax.axis_index("strip")
    block, features = px_ref.shape
    count = strips * block
    width = wbuf.shape[2]
    dk = width // 2
    heads = rate_ref.shape[0]
    gate_cols = wg_ref.shape[0]
    chips = strips // 2
    core, chip = lax.rem(me_s, 2), me_s // 2
    partner = chip * 2 + (1 - core)
    group = group_of(lax.rem(me_s + strips // 2, strips), strips, strips)
    depth = features // pieces
    spans = count // SPAN
    columns = SPAN // tall

    barrier = pltpu.get_barrier_semaphore()
    for step in range(1, strips):
        pl.semaphore_signal(
            barrier, inc=1, device_id=(me_f, lax.rem(me_s + step, strips)), device_id_type=MESH
        )
    for step in range(1, faces):
        pl.semaphore_signal(
            barrier, inc=1, device_id=(lax.rem(me_f + step, faces), me_s), device_id_type=MESH
        )

    def chip_at(step, on=None):
        other, bit = chip, 1
        while bit < chips:
            if step & bit:
                other = other + bit - 2 * bit * lax.rem(other // bit, 2)
            bit *= 2
        return other * 2 + (core if on is None else on)

    def rows_of(strip):
        return px_all.at[pl.ds(pl.multiple_of(strip * block, block), block)]

    def weight_from(kind):
        slab = kind * strips + group
        return slab // n_slab, lax.rem(slab, n_slab)

    def weight_src(j, p):
        return wq_ref.at[pl.ds(p * depth, depth), pl.ds(pl.multiple_of(j * width, width), width)]

    def weight_at(kind, p):
        return wbuf.at[kind, pl.ds(p * depth, depth)]

    def weight_copy(kind, p, src, dest):
        return pltpu.make_async_remote_copy(
            src_ref=src,
            dst_ref=weight_at(kind, p),
            send_sem=w_send.at[kind, p, dest],
            recv_sem=w_recv.at[kind, p],
            device_id=(dest, me_s),
            device_id_type=MESH,
        )

    def own_weight(kind, p, j):
        return pltpu.make_async_copy(weight_src(j, p), weight_at(kind, p), w_recv.at[kind, p])

    def weight_wait(kind, p):
        here = weight_at(kind, p)
        pltpu.make_async_copy(here, here, w_recv.at[kind, p]).wait()

    def relays(owner, dest):
        up = (dest == me_f + 1) & (owner == me_f - 1)
        return up | ((dest == me_f - 1) & (owner == me_f + 1))

    def direct(owner, dest, far):
        gap = jnp.abs(dest - me_f)
        return (owner == me_f) & ((gap > 2) if far else (gap == 1))

    def sends(owner, dest):
        return direct(owner, dest, False) | direct(owner, dest, True) | relays(owner, dest)

    def gate_from(which):
        column = which * heads + group * 2
        return column // gate_cols, lax.rem(column, gate_cols)

    def gate_copy(which, dest):
        return pltpu.make_async_remote_copy(
            src_ref=g_out.at[which],
            dst_ref=g_in.at[which],
            send_sem=g_send.at[which, dest],
            recv_sem=g_recv.at[which],
            device_id=(dest, me_s),
            device_id_type=MESH,
        )

    lines = features // width

    def pick_gates():
        here = wg_own[...].astype(f32)
        row_of = lax.broadcasted_iota(jnp.int32, here.shape, 0)
        for which in range(2):
            owner, row = gate_from(which)

            @pl.when(owner == me_f)
            def _(which=which, row=row):
                picked = [
                    jnp.sum(jnp.where(row_of == row + a, here, 0.0), axis=0, keepdims=True)
                    for a in range(2)
                ]
                parts = [
                    picked[a][:, i * width : (i + 1) * width]
                    for a in range(2)
                    for i in range(lines)
                ]
                g_out[which] = jnp.concatenate(parts, axis=0).astype(bf16)

    def send_gates():
        for which in range(2):
            owner, _ = gate_from(which)

            @pl.when(owner == me_f)
            def _(which=which):
                for dest in range(faces):
                    pl.when(dest != me_f)(gate_copy(which, dest).start)
                pltpu.make_async_copy(g_out.at[which], g_in.at[which], g_recv.at[which]).start()

    own_px = pltpu.make_async_copy(px_ref, rows_of(me_s), px_recv.at[me_s])
    own_px.start()
    own_gate = pltpu.make_async_copy(wg_ref, wg_own, wg_sem.at[0])
    own_gate.start()
    own_gate.wait()
    pick_gates()
    pl.semaphore_wait(barrier, strips - 1 + faces - 1)
    send_gates()

    def send_weights(kind, far):
        owner, j = weight_from(kind)

        @pl.when(owner == me_f)
        def _():
            for p in range(pieces):
                for dest in range(faces):
                    pl.when(direct(owner, dest, far))(
                        weight_copy(kind, p, weight_src(j, p), dest).start
                    )

    def own_weights(kind):
        owner, j = weight_from(kind)

        @pl.when(owner == me_f)
        def _():
            for p in range(pieces):
                own_weight(kind, p, j).start()

    send_weights(1, False)
    send_weights(1, True)
    def px_copy(dest, sem, source, src):
        return pltpu.make_async_remote_copy(
            src_ref=src,
            dst_ref=rows_of(source),
            send_sem=sem,
            recv_sem=px_recv.at[source],
            device_id=(me_f, dest),
            device_id_type=MESH,
        )

    def px_out(step):
        return px_copy(chip_at(step), px_send.at[step], me_s, px_ref)

    def px_pass(step):
        source = chip_at(step)
        return px_copy(partner, px_fwd.at[step], source, rows_of(source))

    to_partner = px_copy(partner, px_send.at[0], me_s, px_ref)
    for step in range(1, chips):
        px_out(step).start()
    to_partner.start()
    own_weights(1)

    ti = lax.broadcasted_iota(jnp.int32, (width, width), 0)
    tj = lax.broadcasted_iota(jnp.int32, (width, width), 1)
    for level in range(LEVELS):
        half = 1 << level
        here = (ti // (2 * half)) == (tj // (2 * half))
        here = here & (lax.rem(ti, 2 * half) >= half) & (lax.rem(tj, 2 * half) < half)
        masks[level] = here.astype(f32).astype(bf16)
    eye = (ti == tj).astype(f32)
    masks[LEVELS] = eye.astype(bf16)
    same_head = (ti // dk) == (tj // dk)
    masks[LEVELS + 1] = same_head.astype(f32).astype(bf16)
    tri = same_head & (ti >= tj)
    masks[LEVELS + 2] = tri.astype(f32).astype(bf16)

    def px_wait(strip):
        pltpu.make_async_copy(px_ref, rows_of(strip), px_recv.at[strip]).wait()

    def pass_pixels(step):
        px_wait(chip_at(step))
        px_pass(step).start()

    def relayed(owner):
        return (jnp.abs(owner - me_f) == 1) & (
            ((2 * me_f - owner) >= 0) & ((2 * me_f - owner) < faces)
        )

    def pass_weights(kind, p):
        owner, _ = weight_from(kind)

        @pl.when(relayed(owner))
        def _():
            weight_wait(kind, p)
            for dest in range(faces):
                pl.when(relays(owner, dest))(weight_copy(kind, p, weight_at(kind, p), dest).start)

    for p in range(pieces):
        pass_weights(1, p)
    for kind in (0, 2):
        send_weights(kind, False)
    for kind in (0, 2):
        own_weights(kind)
    upper = me_f * 2 >= faces

    def early(p):
        pl.when(upper)(functools.partial(pass_weights, 2, p))
        pl.when(jnp.logical_not(upper))(functools.partial(pass_weights, 0, p))

    def late(p):
        pl.when(upper)(functools.partial(pass_weights, 0, p))
        pl.when(jnp.logical_not(upper))(functools.partial(pass_weights, 2, p))

    for p in range(pieces):
        early(p)
    for step in range(1, chips):
        pass_pixels(step)
    for which in range(2):
        pltpu.make_async_copy(g_in.at[which], g_in.at[which], g_recv.at[which]).wait()
        got = g_in[which].astype(f32)
        for a in range(2):
            for i in range(lines):
                line = got[a * lines + i : a * lines + i + 1, :]
                at = which * width + a * dk
                g_rows[at : at + dk, i * width : (i + 1) * width] = jnp.broadcast_to(
                    line, (dk, width)
                ).astype(bf16)
    px_wait(me_s)
    px_wait(partner)
    for step in range(1, chips):
        px_wait(chip_at(step, 1 - core))

    lane = lax.broadcasted_iota(jnp.int32, (1, width), 1) // dk
    first = group * 2

    def by_head(ref):
        return jnp.where(lane == 0, ref[first], ref[first + 1])

    logits = lax.dot_general(
        px_all[...], g_rows[...], (((1,), (1,)), ((), ())), preferred_element_type=f32
    )
    logits = logits.astype(bf16).astype(f32)
    flat[0] = -by_head(rate_ref) * jnp.exp(logits[:, :width])
    flat[1] = jax.nn.sigmoid(logits[:, width:] + by_head(bias_ref))

    head_ones = masks[LEVELS + 1]

    def features_of(kind):
        owner, _ = weight_from(kind)
        for p in range(pieces):
            pl.when(jnp.logical_not(relayed(owner)))(functools.partial(weight_wait, kind, p))
        if kind == 1:
            for late in (0, 2):
                send_weights(late, True)
        x = jnp.dot(px_all[...], wbuf[kind], preferred_element_type=f32)
        x = x.astype(bf16).astype(f32)
        if kind < 2:
            x = x * lax.rsqrt(mm(x * x, head_ones) + 1e-06)
        flat[2 + kind] = x

    def rows_at(i):
        return pl.ds(i * SPAN if isinstance(i, int) else pl.multiple_of(i * SPAN, SPAN), SPAN)

    def load(which, i, by_column):
        if not by_column:
            return flat[which, rows_at(i), :]
        return jnp.concatenate(
            [flat[which, pl.ds(i * columns + c, tall, stride=wide), :] for c in range(columns)],
            axis=0,
        )

    half_masks = [(lane == a).astype(f32).astype(bf16) for a in range(2)]

    def stacked(x):
        x = x.astype(bf16)
        return jnp.concatenate([x * half_masks[0], x * half_masks[1]], axis=0)

    def twice(x):
        return jnp.concatenate([x, x], axis=0)

    def slot(i, o):
        return i * 2 + o

    ri = lax.broadcasted_iota(jnp.int32, (SPAN, width), 0)
    rj = lax.rem(lax.broadcasted_iota(jnp.int32, (SPAN, width), 1), dk)
    inclusive = ri >= rj

    units_all = [(i, o) for i in range(spans) for o in range(2)]

    def each_span(body, per_turn):
        def turn(t, carry):
            body([(t * per_turn + u, o) for u in range(per_turn) for o in range(2)])
            return carry

        lax.fori_loop(0, spans // per_turn, turn, 0)

    def key_stage(units):
        lows, tails, kbs = [], [], []
        for i, o in units:
            decay, beta, k = load(0, i, o), load(1, i, o), load(3, i, o)
            cum = split_mm(masks[LEVELS + 2], twice(decay), 3)[:SPAN]
            turned = twice(cum).T
            across = jnp.where(lane == 0, turned[0:1, :], turned[dk : dk + 1, :])
            gap = cum - across
            within = jnp.exp(jnp.where(inclusive, gap, -1e30))
            ks = stacked(k)
            gram = mm(k, ks, ((1,), (1,)))
            lows.append(twice((within * gram * beta).astype(bf16)))
            scale = jnp.exp(cum)
            last = cum[SPAN - 1 : SPAN, :]
            tails.append(stacked(k * jnp.exp(last - cum)))
            kb = stacked(k * (beta * scale))
            kbs.append(kb)
            at = slot(i, o)
            cums[at] = jnp.exp(last)
            ordered[0, at] = scale
            ordered[1, at] = within
            sides[0, at] = ks
            sides[1, at] = kb
        xs = [masks[LEVELS] - low * masks[0] for low in lows]
        for level in range(1, LEVELS):
            mids = [mm(low * masks[level], x) for low, x in zip(lows, xs)]
            ends = [mm(x, mid) for x, mid in zip(xs, mids)]
            xs = [x - end.astype(bf16) for x, end in zip(xs, ends)]
        hs = [mm(tail, x, ((0,), (0,))).astype(bf16) for tail, x in zip(tails, xs)]
        ms = [mm(h, kb).astype(bf16) for h, kb in zip(hs, kbs)]
        for (i, o), x, h, m in zip(units, xs, hs, ms):
            at = slot(i, o)
            inv[at] = x
            into[at] = h
            trans[at] = m

    def query_stage(units):
        for i, o in units:
            at = slot(i, o)
            q = load(2, i, o)
            scores = ordered[1, at] * mm(q, sides[0, at], ((1,), (1,)))
            g = mm(scores, inv[at]).astype(bf16)
            reads[at] = g
            asks[at] = (q * ordered[0, at] - mm(g, sides[1, at])).astype(bf16)

    def value_stage(units):
        for i, o in units:
            at = slot(i, o)
            vb = stacked(load(4, i, o) * load(1, i, o))
            keyed[at] = mm(into[at], vb)
            sides[2, at] = vb

    def value_scan():
        features_of(2)
        each_span(value_stage, 4)
        state = [jnp.zeros((width, width), f32) for _ in range(2)]
        for i in range(spans):
            for o in range(2):
                at = slot(i, o)
                held = state[o].astype(bf16)
                states[at] = held
                if i < spans - 1:
                    state[o] = state[o] * cums[at] + (keyed[at] - mm(trans[at], held))

    queries_last = me_f * 2 >= faces
    features_of(1)
    for p in range(pieces):
        late(p)
    key_stage(units_all)
    pl.when(queries_last)(value_scan)
    features_of(0)
    each_span(query_stage, 4)
    pl.when(jnp.logical_not(queries_last))(value_scan)

    def output_stage(units):
        for i, o in units:
            at = slot(i, o)
            out = mm(reads[at], sides[2, at]) + mm(asks[at], states[at])
            if o == 0:
                outs[0, rows_at(i), :] = out
            else:
                for c in range(columns):
                    outs[1, pl.ds(i * columns + c, tall, stride=wide), :] = out[
                        c * tall : (c + 1) * tall
                    ]

    each_span(output_stage, 8)
    def lanes_of(owner):
        return out_ref.at[:, pl.ds(pl.multiple_of(owner * width, width), width)]

    def give(step):
        return give_to(lax.rem(me_s + step, strips))

    def give_to(dest):
        return pltpu.make_async_remote_copy(
            src_ref=mixed.at[dest],
            dst_ref=lanes_of(group),
            send_sem=r_send.at[dest],
            recv_sem=r_recv.at[group],
            device_id=(me_f, dest),
            device_id_type=MESH,
        )

    squares = [outs[o] * outs[o] for o in range(2)]
    scales = [lax.rsqrt(mm(x, head_ones) * (1.0 / dk) + 1e-06) for x in squares]
    for s in range(strips):
        at = slice(s * block, (s + 1) * block)
        across = (outs[0, at, :] * scales[0][at], outs[1, at, :] * scales[1][at])
        mixed[s] = (across[0] + across[1].astype(bf16).astype(f32)).astype(bf16)
        pl.when(s != me_s)(give_to(s).start)
    pltpu.make_async_copy(mixed.at[me_s], lanes_of(group), r_recv.at[group]).start()

    to_partner.wait_send()
    for step in range(1, chips):
        px_out(step).wait_send()
        px_pass(step).wait_send()
    for which in range(2):
        owner, _ = gate_from(which)
        for dest in range(faces):
            pl.when((owner == me_f) & (dest != me_f))(gate_copy(which, dest).wait_send)
    for p in range(pieces):
        for kind in range(3):
            owner, _ = weight_from(kind)
            for dest in range(faces):
                pl.when(sends(owner, dest))(
                    weight_copy(kind, p, weight_at(kind, p), dest).wait_send
                )
    for owner in range(strips):
        pltpu.make_async_copy(mixed.at[0], lanes_of(owner), r_recv.at[owner]).wait()
    for step in range(1, strips):
        give(step).wait_send()


def fused_call(faces, strips, px, w_qkv, w_gate_t, decay_rate, beta_bias, tall, wide):
    block, features = px.shape
    count = block * strips
    width = w_qkv.shape[1] * faces // 3 // strips
    units = 2 * count // SPAN
    pieces = 2
    vmem = pl.BlockSpec(memory_space=pltpu.VMEM)
    smem = pl.BlockSpec(memory_space=pltpu.SMEM)
    hbm = pl.BlockSpec(memory_space=pltpu.HBM)
    dma = pltpu.SemaphoreType.DMA
    square = (units, width, width)
    return pl.pallas_call(
        functools.partial(
            fused_kernel, (faces, strips, w_qkv.shape[1] // width, pieces, tall, wide)
        ),
        out_shape=jax.ShapeDtypeStruct((block, strips * width), bf16),
        in_specs=[hbm, hbm, hbm, smem, smem],
        out_specs=pl.BlockSpec(memory_space=pl.ANY),
        scratch_shapes=[
            pltpu.VMEM((count, features), bf16),
            pltpu.VMEM((3, features, width), bf16),
            pltpu.VMEM(w_gate_t.shape, bf16),
            pltpu.VMEM((2, 2 * features // width, width), bf16),
            pltpu.VMEM((2, 2 * features // width, width), bf16),
            pltpu.VMEM((2 * width, features), bf16),
            pltpu.VMEM((LEVELS + 3, width, width), bf16),
            pltpu.VMEM((5, count, width), f32),
            pltpu.VMEM((2, units, SPAN, width), f32),
            pltpu.VMEM((units, 1, width), f32),
            pltpu.VMEM((3,) + square, bf16),
            pltpu.VMEM(square, bf16),
            pltpu.VMEM(square, bf16),
            pltpu.VMEM(square, bf16),
            pltpu.VMEM(square, f32),
            pltpu.VMEM((units, SPAN, width), bf16),
            pltpu.VMEM((units, SPAN, width), bf16),
            pltpu.VMEM(square, bf16),
            pltpu.VMEM((2, count, width), f32),
            pltpu.VMEM((strips, block, width), bf16),
            dma((strips // 2,)),
            dma((strips // 2,)),
            dma((strips,)),
            dma((3, pieces, faces)),
            dma((3, pieces)),
            dma((2, faces)),
            dma((2,)),
            dma((1,)),
            dma((strips,)),
            dma((strips,)),
        ],
        compiler_params=pltpu.CompilerParams(
            collective_id=2, has_side_effects=True, vmem_limit_bytes=20 * 2**20
        ),
        name="layer",
    )(*[
        pltpu.with_memory_space_constraint(x, pltpu.HBM)
        for x in (px, w_qkv, w_gate_t, decay_rate, beta_bias)
    ])


def fits_fused(strips, heads, dk, count, tall, wide, gate_cols, features, block):
    return (
        heads == 2 * strips
        and dk == SPAN
        and 2 * dk == 128
        and strips & (strips - 1) == 0
        and strips > 1
        and count % (4 * SPAN) == 0
        and count <= 1024
        and block % 16 == 0
        and tall % 8 == 0
        and SPAN % tall == 0
        and wide % (SPAN // tall) == 0
        and gate_cols % 8 == 0
        and features % 1024 == 0
    )


def on_device(faces, strips, pixels_in, w_qkv, w_gate, decay_rate, beta_bias):
    _, rows_here, wide, features = pixels_in.shape
    heads = decay_rate.shape[0]
    block = rows_here * wide
    count = block * strips
    tall = rows_here * strips
    model = w_qkv.shape[1] * faces // 3
    dk = model // heads
    groups = min(strips, heads)
    per_group = heads // groups
    width = per_group * dk
    n_slab = w_qkv.shape[1] // width
    gate_cols = w_gate.shape[1]
    if fits_fused(strips, heads, dk, count, tall, wide, gate_cols, features, block):
        out = fused_call(
            faces, strips, pixels_in.reshape(block, features), w_qkv, w_gate.T,
            decay_rate, beta_bias, tall, wide,
        )
        return out.reshape(1, rows_here, wide, model)
    pieces = 4
    chunk = min(128, count)
    chips = strips // 2
    vmem = pl.BlockSpec(memory_space=pltpu.VMEM)
    dma = pltpu.SemaphoreType.DMA
    if width % 128:
        w_qkv = w_qkv.reshape(features, n_slab, width).transpose(1, 0, 2)
    slabs, gates = pl.pallas_call(
        functools.partial(project_kernel, (faces, strips, groups, n_slab, pieces)),
        out_shape=(
            jax.ShapeDtypeStruct((3, count, width), bf16),
            jax.ShapeDtypeStruct((count // chunk, 2 * heads, chunk), f32),
        ),
        in_specs=[vmem, pl.BlockSpec(memory_space=pl.ANY), vmem],
        out_specs=(vmem, vmem),
        scratch_shapes=[
            pltpu.VMEM((count, features), bf16),
            pltpu.VMEM((3, features, width), bf16),
            pltpu.VMEM((gate_cols, features), f32),
            pltpu.VMEM((faces, gate_cols, features), f32),
            pltpu.VMEM((count, 3 * width), f32),
            dma((chips,)),
            dma((chips,)),
            dma((strips,)),
            dma((3, pieces, 2)),
            dma((3, pieces)),
            dma((faces,)),
            dma((faces,)),
        ],
        compiler_params=pltpu.CompilerParams(collective_id=0, has_side_effects=True),
        name="project",
    )(pixels_in.reshape(block, features), w_qkv, w_gate.T)
    group = group_of(lax.axis_index("strip"), strips, groups)
    first = (group * per_group).astype(jnp.int32).reshape(1)
    mixed = scan_call(
        first, slabs, gates, decay_rate, beta_bias, strips, per_group, tall, wide, dk
    )
    returned = pl.pallas_call(
        functools.partial(return_kernel, strips, groups),
        out_shape=jax.ShapeDtypeStruct((groups, block, width), bf16),
        in_specs=[vmem],
        out_specs=vmem,
        scratch_shapes=[dma((strips,)), dma((groups,))],
        compiler_params=pltpu.CompilerParams(collective_id=1, has_side_effects=True),
        name="give_back",
    )(mixed)
    return returned.transpose(1, 0, 2).reshape(1, rows_here, wide, model)


def solution(mesh):
    in_specs = (P("face", "strip", None, None), P(None, "face"), P(None, "face"), P(), P())
    out_specs = P("face", "strip", None, None)
    return jax.shard_map(
        functools.partial(on_device, mesh.shape["face"], mesh.shape["strip"]),
        mesh=mesh,
        in_specs=in_specs,
        out_specs=out_specs,
        check_vma=False,
    )
```

```python
import functools

import jax
import jax.numpy as jnp
from jax import lax
from jax.experimental import pallas as pl
from jax.experimental.pallas import tpu as pltpu
from jax.sharding import PartitionSpec as P

MESH = pl.DeviceIdType.MESH
f32 = jnp.float32
bf16 = jnp.bfloat16


def group_of(place, strips, groups):
    rep = strips // groups
    if rep > 1 or groups % 2:
        return place // rep
    return jnp.where(lax.rem(place, 2) == 0, place // 2, groups - 1 - place // 2)


def project_kernel(
    cfg, px_ref, wq_ref, wg_ref, slabs_ref, gates_ref,
    px_all, wbuf, wg_own, wg_all, acc, px_send, px_fwd, px_recv, w_send, w_recv, g_send, g_recv,
):
    faces, strips, groups, n_slab, pieces = cfg
    me_f, me_s = lax.axis_index("face"), lax.axis_index("strip")
    block, features = px_ref.shape
    count = strips * block
    width = wbuf.shape[2]
    chips = strips // 2
    core, chip = lax.rem(me_s, 2), me_s // 2
    partner = chip * 2 + (1 - core)
    group = group_of(me_s, strips, groups)
    depth = features // pieces

    def chip_at(step):
        return lax.rem(chip + step, chips) * 2 + core

    barrier = pltpu.get_barrier_semaphore()

    def greet(face, strip):
        pl.semaphore_signal(barrier, inc=1, device_id=(face, strip), device_id_type=MESH)

    greet(me_f, partner)
    for step in range(1, chips):
        greet(me_f, chip_at(step))
    for step in range(1, faces):
        greet(lax.rem(me_f + step, faces), me_s)

    wg_own[...] = wg_ref[...].astype(f32)

    def rows_of(strip):
        return px_all.at[pl.ds(pl.multiple_of(strip * block, block), block)]

    own_px = pltpu.make_async_copy(px_ref, rows_of(me_s), px_recv.at[me_s])
    own_px.start()
    pl.semaphore_wait(barrier, 1 + chips - 1 + faces - 1)

    def weight_from(kind):
        slab = kind * groups + group
        return slab // n_slab, lax.rem(slab, n_slab)

    def weight_src(j, p):
        rows = pl.ds(p * depth, depth)
        if len(wq_ref.shape) == 3:
            return wq_ref.at[j, rows]
        return wq_ref.at[rows, pl.ds(pl.multiple_of(j * width, width), width)]

    def weight_copy(kind, p, src, side):
        return pltpu.make_async_remote_copy(
            src_ref=src,
            dst_ref=wbuf.at[kind, pl.ds(p * depth, depth)],
            send_sem=w_send.at[kind, p, side],
            recv_sem=w_recv.at[kind, p],
            device_id=(me_f + (1 if side else -1), me_s),
            device_id_type=MESH,
        )

    def own_weight(kind, p, j):
        return pltpu.make_async_copy(
            weight_src(j, p), wbuf.at[kind, pl.ds(p * depth, depth)], w_recv.at[kind, p]
        )

    for p in range(pieces):
        for kind in range(3):
            owner, j = weight_from(kind)

            @pl.when(owner == me_f)
            def _(kind=kind, p=p, j=j):
                pl.when(me_f + 1 < faces)(weight_copy(kind, p, weight_src(j, p), 1).start)
                pl.when(me_f > 0)(weight_copy(kind, p, weight_src(j, p), 0).start)
                own_weight(kind, p, j).start()

    def px_copy(dest, sem, source, src):
        return pltpu.make_async_remote_copy(
            src_ref=src,
            dst_ref=rows_of(source),
            send_sem=sem,
            recv_sem=px_recv.at[source],
            device_id=(me_f, dest),
            device_id_type=MESH,
        )

    def px_out(step):
        return px_copy(chip_at(step), px_send.at[step], me_s, px_ref)

    def px_pass(step):
        source = chip_at(step)
        return px_copy(partner, px_fwd.at[step], source, rows_of(source))

    to_partner = px_copy(partner, px_send.at[0], me_s, px_ref)
    for step in range(1, chips):
        px_out(step).start()
    to_partner.start()

    def gate_copy(step):
        return pltpu.make_async_remote_copy(
            src_ref=wg_own,
            dst_ref=wg_all.at[me_f],
            send_sem=g_send.at[step],
            recv_sem=g_recv.at[me_f],
            device_id=(lax.rem(me_f + step, faces), me_s),
            device_id_type=MESH,
        )

    for step in range(1, faces):
        gate_copy(step).start()
    own_gate = pltpu.make_async_copy(wg_own, wg_all.at[me_f], g_recv.at[me_f])
    own_gate.start()

    def px_wait(strip):
        pltpu.make_async_copy(px_ref, rows_of(strip), px_recv.at[strip]).wait()

    def pass_pixels(step):
        px_wait(chip_at(step))
        px_pass(step).start()

    def pass_weights(p):
        for kind in range(3):
            owner, _ = weight_from(kind)
            here = wbuf.at[kind, pl.ds(p * depth, depth)]
            pltpu.make_async_copy(here, here, w_recv.at[kind, p]).wait()
            pl.when((owner < me_f) & (me_f + 1 < faces))(weight_copy(kind, p, here, 1).start)
            pl.when((owner > me_f) & (me_f > 0))(weight_copy(kind, p, here, 0).start)

    tile = min(512, count)

    def each_tile(body):
        if count == tile:
            body(pl.ds(0, tile), 0)
        else:

            def one(i, carry):
                body(pl.ds(pl.multiple_of(i * tile, tile), tile), i)
                return carry

            lax.fori_loop(0, count // tile, one, 0)

    def multiply(p):
        rows = pl.ds(p * depth, depth)
        weights = jnp.concatenate([wbuf[kind, rows, :] for kind in range(3)], axis=1)

        def body(at, _):
            term = jnp.dot(px_all[at, rows], weights, preferred_element_type=f32)
            if p > 0:
                term = term + acc[at, :]
            if p < pieces - 1:
                acc[at, :] = term
            else:
                for kind in range(3):
                    slabs_ref[kind, at, :] = term[
                        :, kind * width : (kind + 1) * width
                    ].astype(bf16)

        each_tile(body)

    for turn in range(max(pieces - 1, chips - 1)):
        if turn < pieces - 1:
            pass_weights(turn)
        if turn < chips - 1:
            pass_pixels(turn + 1)
    px_wait(me_s)
    px_wait(partner)
    for step in range(1, chips):
        px_wait(lax.rem(chip + step, chips) * 2 + (1 - core))
    for face in range(faces):
        pltpu.make_async_copy(wg_own, wg_all.at[face], g_recv.at[face]).wait()
    gate_w = jnp.concatenate([wg_all[face] for face in range(faces)], axis=0).astype(bf16)

    chunk = gates_ref.shape[2]

    def gate_body(at, i):
        logits = lax.dot_general(
            gate_w, px_all[at, :], (((1,), (1,)), ((), ())), preferred_element_type=f32
        )
        logits = logits.astype(bf16).astype(f32)
        for c in range(tile // chunk):
            gates_ref[i * (tile // chunk) + c] = logits[:, c * chunk : (c + 1) * chunk]

    each_tile(gate_body)
    for p in range(pieces - 1):
        multiply(p)
    pass_weights(pieces - 1)
    multiply(pieces - 1)

    to_partner.wait_send()
    for step in range(1, chips):
        px_out(step).wait_send()
        px_pass(step).wait_send()
    for step in range(1, faces):
        gate_copy(step).wait_send()
    for p in range(pieces):
        for kind in range(3):
            owner, _ = weight_from(kind)
            here = wbuf.at[kind, pl.ds(p * depth, depth)]
            pl.when((owner <= me_f) & (me_f + 1 < faces))(
                weight_copy(kind, p, here, 1).wait_send
            )
            pl.when((owner >= me_f) & (me_f > 0))(weight_copy(kind, p, here, 0).wait_send)


def mm(a, b, dims=((1,), (0,))):
    return lax.dot_general(
        a.astype(bf16), b.astype(bf16), (dims, ((), ())), preferred_element_type=f32
    )


def split_mm(exact, wide, pieces):
    exact = exact.astype(bf16)
    total, rest = None, wide
    for _ in range(pieces):
        piece = rest.astype(bf16)
        rest = rest - piece.astype(f32)
        term = jnp.dot(exact, piece, preferred_element_type=f32)
        total = term if total is None else total + term
    return total


def mm_split(wide, exact, pieces):
    exact = exact.astype(bf16)
    total, rest = None, wide
    for _ in range(pieces):
        piece = rest.astype(bf16)
        rest = rest - piece.astype(f32)
        term = jnp.dot(piece, exact, preferred_element_type=f32)
        total = term if total is None else total + term
    return total


def scan_kernel(
    cfg, first_ref, slabs_ref, gates_ref, rate_ref, bias_ref, out_ref,
    feats, gates, row_buf, col_buf, states,
):
    chunk, per_group, tall, wide, dk = cfg
    count, width = slabs_ref.shape[1:]
    strips, block, _ = out_ref.shape
    heads = gates_ref.shape[1] // 2
    first = first_ref[0]

    lane = lax.broadcasted_iota(jnp.int32, (width, width), 1)
    sub = lax.broadcasted_iota(jnp.int32, (width, width), 0)
    same_head = (lane // dk) == (sub // dk)
    head_ones = same_head.astype(f32)
    ti = lax.broadcasted_iota(jnp.int32, (chunk, chunk), 0)
    tj = lax.broadcasted_iota(jnp.int32, (chunk, chunk), 1)
    inclusive = ti >= tj
    tri = inclusive.astype(f32)
    eye = (ti == tj).astype(f32)

    def prepare(i, carry):
        at = pl.ds(pl.multiple_of(i * chunk, chunk), chunk)
        for kind in range(3):
            x = slabs_ref[kind, at, :].astype(f32)
            if kind < 2:
                x = x * lax.rsqrt(mm_split(x * x, head_ones, 2) + 1e-06)
            feats[kind, at, :] = x
        for a in range(per_group):
            head = first + a
            decay = -rate_ref[head] * jnp.exp(gates_ref[i, pl.ds(head, 1), :])
            strength = jax.nn.sigmoid(gates_ref[i, pl.ds(heads + head, 1), :] + bias_ref[head])
            gates[a, at, :] = jnp.broadcast_to(decay, (chunk, chunk)).T
            gates[per_group + a, at, :] = jnp.broadcast_to(strength, (chunk, chunk)).T
        return carry

    lax.fori_loop(0, count // chunk, prepare, 0, unroll=count // chunk <= 4)

    columns = chunk // tall
    flane = lax.broadcasted_iota(jnp.int32, (chunk, width), 1) // dk

    def lanes_of(parts):
        out = parts[0][:, :width]
        for a in range(1, per_group):
            out = jnp.where(flane == a, parts[a][:, :width], out)
        return out

    def stacked(x):
        if per_group == 1:
            return x
        return jnp.concatenate(
            [jnp.where(flane == a, x, jnp.zeros_like(x)) for a in range(per_group)], axis=0
        )

    def side_by_side(parts):
        return parts[0] if per_group == 1 else jnp.concatenate(parts, axis=1)

    def load(ref, which, i, by_column):
        if not by_column:
            return ref[which, pl.ds(pl.multiple_of(i * chunk, chunk), chunk), :]
        return jnp.concatenate(
            [ref[which, pl.ds(i * columns + c, tall, stride=wide), :] for c in range(columns)],
            axis=0,
        )

    states[...] = jnp.zeros_like(states)

    def advance(i, carry):
        work = []
        for order in range(2):
            q, k, v = (load(feats, kind, i, order) for kind in range(3))
            cums, betas, systems, scores = [], [], [], []
            for a in range(per_group):
                cum = split_mm(tri, load(gates, a, i, order), 3)
                beta = load(gates, per_group + a, i, order)
                gap = cum - cum.T
                within = jnp.where(inclusive, jnp.exp(jnp.where(inclusive, gap, 0.0)), 0.0)
                k_a = k if per_group == 1 else jnp.where(flane == a, k, 0.0)
                q_a = q if per_group == 1 else jnp.where(flane == a, q, 0.0)
                dots = mm(jnp.concatenate([k_a, q_a], axis=0), k, ((1,), (1,)))
                systems.append(within * dots[:chunk] * beta)
                scores.append(within * dots[chunk:])
                cums.append(cum)
                betas.append(beta)
            work.append((q, k, v, cums, betas, systems, scores))

        inverses = [[None] * per_group for _ in range(2)]
        half = 1
        while half < chunk:
            here = ((ti // (2 * half)) == (tj // (2 * half))) & (
                (lax.rem(ti, 2 * half) >= half) & (lax.rem(tj, 2 * half) < half)
            )
            lows = [
                [jnp.where(here, work[o][5][a], 0.0) for a in range(per_group)] for o in range(2)
            ]
            if half == 1:
                inverses = [[eye - low for low in row] for row in lows]
            else:
                firsts = [
                    [mm(lows[o][a], inverses[o][a]) for a in range(per_group)] for o in range(2)
                ]
                inverses = [
                    [inverses[o][a] - mm(inverses[o][a], firsts[o][a]) for a in range(per_group)]
                    for o in range(2)
                ]
            half *= 2

        for order in range(2):
            q, k, v, cums, betas, _, scores = work[order]
            beta = lanes_of(betas)
            cum = lanes_of(cums)
            scale = jnp.exp(cum)
            last = cum[chunk - 1 : chunk, :]
            tail = jnp.exp(last - cum)
            both = side_by_side(inverses[order])
            u = mm(both, stacked(v * beta))
            w = mm(both, stacked(k * (beta * scale)))
            state = states[order]
            fresh = u - mm(w, state)
            out = mm(q * scale, state) + mm(side_by_side(scores), stacked(fresh))
            grown = mm(k * tail, fresh, ((0,), (0,)))
            decayed = state * jnp.exp(last)
            states[order] = decayed + jnp.where(same_head, grown, 0.0)
            normed = out * lax.rsqrt(mm_split(out * out, head_ones, 2) * (1.0 / dk) + 1e-06)
            if order == 0:
                row_buf[pl.ds(pl.multiple_of(i * chunk, chunk), chunk), :] = normed
            else:
                normed = normed.astype(bf16).astype(f32)
                for c in range(columns):
                    col_buf[pl.ds(i * columns + c, tall, stride=wide), :] = normed[
                        c * tall : (c + 1) * tall
                    ]
        return carry

    lax.fori_loop(0, count // chunk, advance, 0)

    def finish(s, carry):
        at = pl.ds(s * block, block)
        out_ref[s] = (row_buf[at, :] + col_buf[at, :]).astype(bf16)
        return carry

    lax.fori_loop(0, strips, finish, 0)


def return_kernel(strips, groups, mixed_ref, out_ref, send_sem, recv_sem):
    me_f, me_s = lax.axis_index("face"), lax.axis_index("strip")
    rep = strips // groups
    barrier = pltpu.get_barrier_semaphore()
    for step in range(1, strips):
        pl.semaphore_signal(
            barrier, inc=1, device_id=(me_f, lax.rem(me_s + step, strips)), device_id_type=MESH
        )
    pl.semaphore_wait(barrier, strips - 1)
    mine = group_of(me_s, strips, groups)
    sends = lax.rem(me_s, rep) == 0

    def copy(step):
        dest = lax.rem(me_s + step, strips)
        return pltpu.make_async_remote_copy(
            src_ref=mixed_ref.at[dest],
            dst_ref=out_ref.at[mine],
            send_sem=send_sem.at[step],
            recv_sem=recv_sem.at[mine],
            device_id=(me_f, dest),
            device_id_type=MESH,
        )

    @pl.when(sends)
    def _():
        for step in range(1, strips):
            copy(step).start()
        pltpu.make_async_copy(mixed_ref.at[me_s], out_ref.at[mine], recv_sem.at[mine]).start()
        for step in range(1, strips):
            copy(step).wait_send()

    for group in range(groups):
        pltpu.make_async_copy(mixed_ref.at[0], out_ref.at[group], recv_sem.at[group]).wait()


def scan_call(
    first, slabs, gates, decay_rate, beta_bias, strips, per_group, tall, wide, dk
):
    count, width = slabs.shape[1:]
    block = count // strips
    chunk = min(128, count)
    vmem = pl.BlockSpec(memory_space=pltpu.VMEM)
    smem = pl.BlockSpec(memory_space=pltpu.SMEM)
    return pl.pallas_call(
        functools.partial(scan_kernel, (chunk, per_group, tall, wide, dk)),
        out_shape=jax.ShapeDtypeStruct((strips, block, width), bf16),
        in_specs=[smem, vmem, vmem, smem, smem],
        out_specs=vmem,
        scratch_shapes=[
            pltpu.VMEM((3, count, width), f32),
            pltpu.VMEM((2 * per_group, count, chunk), f32),
            pltpu.VMEM((count, width), f32),
            pltpu.VMEM((count, width), f32),
            pltpu.VMEM((2, width, width), f32),
        ],
        name="scans",
    )(first, slabs, gates, decay_rate, beta_bias)


LEVELS = 6
SPAN = 1 << LEVELS


def fused_kernel(
    cfg, px_ref, wq_ref, wg_ref, rate_ref, bias_ref, out_ref,
    px_all, wbuf, wg_own, g_out, g_in, g_rows, masks, flat, ordered, cums, sides,
    inv, into, trans, reads, asks, states, outs, mixed,
    px_send, px_fwd, px_recv, w_send, w_recv, g_send, g_recv, wg_sem, r_send, r_recv,
):
    faces, strips, n_slab, pieces, tall, wide = cfg
    me_f, me_s = lax.axis_index("face"), lax.axis_index("strip")
    block, features = px_ref.shape
    count = strips * block
    width = wbuf.shape[2]
    dk = width // 2
    heads = rate_ref.shape[0]
    gate_cols = wg_ref.shape[0]
    chips = strips // 2
    core, chip = lax.rem(me_s, 2), me_s // 2
    partner = chip * 2 + (1 - core)
    group = group_of(lax.rem(me_s + strips // 2, strips), strips, strips)
    depth = features // pieces
    spans = count // SPAN
    columns = SPAN // tall

    barrier = pltpu.get_barrier_semaphore()
    for step in range(1, strips):
        pl.semaphore_signal(
            barrier, inc=1, device_id=(me_f, lax.rem(me_s + step, strips)), device_id_type=MESH
        )
    for step in range(1, faces):
        pl.semaphore_signal(
            barrier, inc=1, device_id=(lax.rem(me_f + step, faces), me_s), device_id_type=MESH
        )

    def chip_at(step, on=None):
        other, bit = chip, 1
        while bit < chips:
            if step & bit:
                other = other + bit - 2 * bit * lax.rem(other // bit, 2)
            bit *= 2
        return other * 2 + (core if on is None else on)

    def rows_of(strip):
        return px_all.at[pl.ds(pl.multiple_of(strip * block, block), block)]

    def weight_from(kind):
        slab = kind * strips + group
        return slab // n_slab, lax.rem(slab, n_slab)

    def weight_src(j, p):
        return wq_ref.at[pl.ds(p * depth, depth), pl.ds(pl.multiple_of(j * width, width), width)]

    def weight_at(kind, p):
        return wbuf.at[kind, pl.ds(p * depth, depth)]

    def weight_copy(kind, p, src, dest):
        return pltpu.make_async_remote_copy(
            src_ref=src,
            dst_ref=weight_at(kind, p),
            send_sem=w_send.at[kind, p, dest],
            recv_sem=w_recv.at[kind, p],
            device_id=(dest, me_s),
            device_id_type=MESH,
        )

    def own_weight(kind, p, j):
        return pltpu.make_async_copy(weight_src(j, p), weight_at(kind, p), w_recv.at[kind, p])

    def weight_wait(kind, p):
        here = weight_at(kind, p)
        pltpu.make_async_copy(here, here, w_recv.at[kind, p]).wait()

    def relays(owner, dest):
        up = (dest == me_f + 1) & (owner == me_f - 1)
        return up | ((dest == me_f - 1) & (owner == me_f + 1))

    def direct(owner, dest, far):
        gap = jnp.abs(dest - me_f)
        return (owner == me_f) & ((gap > 2) if far else (gap == 1))

    def sends(owner, dest):
        return direct(owner, dest, False) | direct(owner, dest, True) | relays(owner, dest)

    def gate_from(which):
        column = which * heads + group * 2
        return column // gate_cols, lax.rem(column, gate_cols)

    def gate_copy(which, dest):
        return pltpu.make_async_remote_copy(
            src_ref=g_out.at[which],
            dst_ref=g_in.at[which],
            send_sem=g_send.at[which, dest],
            recv_sem=g_recv.at[which],
            device_id=(dest, me_s),
            device_id_type=MESH,
        )

    lines = features // width

    def pick_gates():
        here = wg_own[...].astype(f32)
        row_of = lax.broadcasted_iota(jnp.int32, here.shape, 0)
        for which in range(2):
            owner, row = gate_from(which)

            @pl.when(owner == me_f)
            def _(which=which, row=row):
                picked = [
                    jnp.sum(jnp.where(row_of == row + a, here, 0.0), axis=0, keepdims=True)
                    for a in range(2)
                ]
                parts = [
                    picked[a][:, i * width : (i + 1) * width]
                    for a in range(2)
                    for i in range(lines)
                ]
                g_out[which] = jnp.concatenate(parts, axis=0).astype(bf16)

    def send_gates():
        for which in range(2):
            owner, _ = gate_from(which)

            @pl.when(owner == me_f)
            def _(which=which):
                for dest in range(faces):
                    pl.when(dest != me_f)(gate_copy(which, dest).start)
                pltpu.make_async_copy(g_out.at[which], g_in.at[which], g_recv.at[which]).start()

    own_px = pltpu.make_async_copy(px_ref, rows_of(me_s), px_recv.at[me_s])
    own_px.start()
    own_gate = pltpu.make_async_copy(wg_ref, wg_own, wg_sem.at[0])
    own_gate.start()
    own_gate.wait()
    pick_gates()
    pl.semaphore_wait(barrier, strips - 1 + faces - 1)
    send_gates()

    def send_weights(kind, far):
        owner, j = weight_from(kind)

        @pl.when(owner == me_f)
        def _():
            for p in range(pieces):
                for dest in range(faces):
                    pl.when(direct(owner, dest, far))(
                        weight_copy(kind, p, weight_src(j, p), dest).start
                    )

    def own_weights(kind):
        owner, j = weight_from(kind)

        @pl.when(owner == me_f)
        def _():
            for p in range(pieces):
                own_weight(kind, p, j).start()

    send_weights(1, False)
    send_weights(1, True)
    def px_copy(dest, sem, source, src):
        return pltpu.make_async_remote_copy(
            src_ref=src,
            dst_ref=rows_of(source),
            send_sem=sem,
            recv_sem=px_recv.at[source],
            device_id=(me_f, dest),
            device_id_type=MESH,
        )

    def px_out(step):
        return px_copy(chip_at(step), px_send.at[step], me_s, px_ref)

    def px_pass(step):
        source = chip_at(step)
        return px_copy(partner, px_fwd.at[step], source, rows_of(source))

    to_partner = px_copy(partner, px_send.at[0], me_s, px_ref)
    for step in range(1, chips):
        px_out(step).start()
    to_partner.start()
    own_weights(1)

    ti = lax.broadcasted_iota(jnp.int32, (width, width), 0)
    tj = lax.broadcasted_iota(jnp.int32, (width, width), 1)
    for level in range(LEVELS):
        half = 1 << level
        here = (ti // (2 * half)) == (tj // (2 * half))
        here = here & (lax.rem(ti, 2 * half) >= half) & (lax.rem(tj, 2 * half) < half)
        masks[level] = here.astype(f32).astype(bf16)
    eye = (ti == tj).astype(f32)
    masks[LEVELS] = eye.astype(bf16)
    same_head = (ti // dk) == (tj // dk)
    masks[LEVELS + 1] = same_head.astype(f32).astype(bf16)
    tri = same_head & (ti >= tj)
    masks[LEVELS + 2] = tri.astype(f32).astype(bf16)

    def px_wait(strip):
        pltpu.make_async_copy(px_ref, rows_of(strip), px_recv.at[strip]).wait()

    def pass_pixels(step):
        px_wait(chip_at(step))
        px_pass(step).start()

    def relayed(owner):
        return (jnp.abs(owner - me_f) == 1) & (
            ((2 * me_f - owner) >= 0) & ((2 * me_f - owner) < faces)
        )

    def pass_weights(kind, p):
        owner, _ = weight_from(kind)

        @pl.when(relayed(owner))
        def _():
            weight_wait(kind, p)
            for dest in range(faces):
                pl.when(relays(owner, dest))(weight_copy(kind, p, weight_at(kind, p), dest).start)

    for p in range(pieces):
        pass_weights(1, p)
    for kind in (0, 2):
        send_weights(kind, False)
    for kind in (0, 2):
        own_weights(kind)
    upper = me_f * 2 >= faces

    def early(p):
        pl.when(upper)(functools.partial(pass_weights, 2, p))
        pl.when(jnp.logical_not(upper))(functools.partial(pass_weights, 0, p))

    def late(p):
        pl.when(upper)(functools.partial(pass_weights, 0, p))
        pl.when(jnp.logical_not(upper))(functools.partial(pass_weights, 2, p))

    for p in range(pieces):
        early(p)
    for step in range(1, chips):
        pass_pixels(step)
    for which in range(2):
        pltpu.make_async_copy(g_in.at[which], g_in.at[which], g_recv.at[which]).wait()
        got = g_in[which].astype(f32)
        for a in range(2):
            for i in range(lines):
                line = got[a * lines + i : a * lines + i + 1, :]
                at = which * width + a * dk
                g_rows[at : at + dk, i * width : (i + 1) * width] = jnp.broadcast_to(
                    line, (dk, width)
                ).astype(bf16)
    px_wait(me_s)
    px_wait(partner)
    for step in range(1, chips):
        px_wait(chip_at(step, 1 - core))

    lane = lax.broadcasted_iota(jnp.int32, (1, width), 1) // dk
    first = group * 2

    def by_head(ref):
        return jnp.where(lane == 0, ref[first], ref[first + 1])

    logits = lax.dot_general(
        px_all[...], g_rows[...], (((1,), (1,)), ((), ())), preferred_element_type=f32
    )
    logits = logits.astype(bf16).astype(f32)
    flat[0] = -by_head(rate_ref) * jnp.exp(logits[:, :width])
    flat[1] = jax.nn.sigmoid(logits[:, width:] + by_head(bias_ref))

    head_ones = masks[LEVELS + 1]

    def features_of(kind):
        owner, _ = weight_from(kind)
        for p in range(pieces):
            pl.when(jnp.logical_not(relayed(owner)))(functools.partial(weight_wait, kind, p))
        if kind == 1:
            for late in (0, 2):
                send_weights(late, True)
        x = jnp.dot(px_all[...], wbuf[kind], preferred_element_type=f32)
        x = x.astype(bf16).astype(f32)
        if kind < 2:
            x = x * lax.rsqrt(mm(x * x, head_ones) + 1e-06)
        flat[2 + kind] = x

    def rows_at(i):
        return pl.ds(i * SPAN if isinstance(i, int) else pl.multiple_of(i * SPAN, SPAN), SPAN)

    def load(which, i, by_column):
        if not by_column:
            return flat[which, rows_at(i), :]
        return jnp.concatenate(
            [flat[which, pl.ds(i * columns + c, tall, stride=wide), :] for c in range(columns)],
            axis=0,
        )

    half_masks = [(lane == a).astype(f32).astype(bf16) for a in range(2)]

    def stacked(x):
        x = x.astype(bf16)
        return jnp.concatenate([x * half_masks[0], x * half_masks[1]], axis=0)

    def twice(x):
        return jnp.concatenate([x, x], axis=0)

    def slot(i, o):
        return i * 2 + o

    ri = lax.broadcasted_iota(jnp.int32, (SPAN, width), 0)
    rj = lax.rem(lax.broadcasted_iota(jnp.int32, (SPAN, width), 1), dk)
    inclusive = ri >= rj

    units_all = [(i, o) for i in range(spans) for o in range(2)]

    def each_span(body, per_turn):
        def turn(t, carry):
            body([(t * per_turn + u, o) for u in range(per_turn) for o in range(2)])
            return carry

        lax.fori_loop(0, spans // per_turn, turn, 0)

    def key_stage(units):
        lows, tails, kbs = [], [], []
        for i, o in units:
            decay, beta, k = load(0, i, o), load(1, i, o), load(3, i, o)
            cum = split_mm(masks[LEVELS + 2], twice(decay), 3)[:SPAN]
            turned = twice(cum).T
            across = jnp.where(lane == 0, turned[0:1, :], turned[dk : dk + 1, :])
            gap = cum - across
            within = jnp.exp(jnp.where(inclusive, gap, -1e30))
            ks = stacked(k)
            gram = mm(k, ks, ((1,), (1,)))
            lows.append(twice((within * gram * beta).astype(bf16)))
            scale = jnp.exp(cum)
            last = cum[SPAN - 1 : SPAN, :]
            tails.append(stacked(k * jnp.exp(last - cum)))
            kb = stacked(k * (beta * scale))
            kbs.append(kb)
            at = slot(i, o)
            cums[at] = jnp.exp(last)
            ordered[0, at] = scale
            ordered[1, at] = within
            sides[0, at] = ks
            sides[1, at] = kb
        xs = [masks[LEVELS] - low * masks[0] for low in lows]
        for level in range(1, LEVELS):
            mids = [mm(low * masks[level], x) for low, x in zip(lows, xs)]
            ends = [mm(x, mid) for x, mid in zip(xs, mids)]
            xs = [x - end.astype(bf16) for x, end in zip(xs, ends)]
        hs = [mm(tail, x, ((0,), (0,))).astype(bf16) for tail, x in zip(tails, xs)]
        ms = [mm(h, kb).astype(bf16) for h, kb in zip(hs, kbs)]
        for (i, o), x, h, m in zip(units, xs, hs, ms):
            at = slot(i, o)
            inv[at] = x
            into[at] = h
            trans[at] = m

    def query_stage(units):
        for i, o in units:
            at = slot(i, o)
            q = load(2, i, o)
            scores = ordered[1, at] * mm(q, sides[0, at], ((1,), (1,)))
            g = mm(scores, inv[at]).astype(bf16)
            reads[at] = g
            asks[at] = (q * ordered[0, at] - mm(g, sides[1, at])).astype(bf16)

    def value_scan():
        features_of(2)
        state = [jnp.zeros((width, width), f32) for _ in range(2)]
        for i in range(spans):
            for o in range(2):
                at = slot(i, o)
                vb = stacked(load(4, i, o) * load(1, i, o))
                sides[2, at] = vb
                held = state[o].astype(bf16)
                states[at] = held
                if i < spans - 1:
                    wrote = mm(into[at], vb)
                    state[o] = state[o] * cums[at] + (wrote - mm(trans[at], held))

    queries_last = me_f * 2 >= faces
    features_of(1)
    for p in range(pieces):
        late(p)
    key_stage(units_all)
    pl.when(queries_last)(value_scan)
    features_of(0)
    each_span(query_stage, 4)
    pl.when(jnp.logical_not(queries_last))(value_scan)

    def output_stage(units):
        for i, o in units:
            at = slot(i, o)
            out = mm(reads[at], sides[2, at]) + mm(asks[at], states[at])
            if o == 0:
                outs[0, rows_at(i), :] = out
            else:
                for c in range(columns):
                    outs[1, pl.ds(i * columns + c, tall, stride=wide), :] = out[
                        c * tall : (c + 1) * tall
                    ]

    each_span(output_stage, 8)
    def lanes_of(owner):
        return out_ref.at[:, pl.ds(pl.multiple_of(owner * width, width), width)]

    def give(step):
        return give_to(lax.rem(me_s + step, strips))

    def give_to(dest):
        return pltpu.make_async_remote_copy(
            src_ref=mixed.at[dest],
            dst_ref=lanes_of(group),
            send_sem=r_send.at[dest],
            recv_sem=r_recv.at[group],
            device_id=(me_f, dest),
            device_id_type=MESH,
        )

    squares = [outs[o] * outs[o] for o in range(2)]
    scales = [lax.rsqrt(mm(x, head_ones) * (1.0 / dk) + 1e-06) for x in squares]
    for s in range(strips):
        at = slice(s * block, (s + 1) * block)
        across = (outs[0, at, :] * scales[0][at], outs[1, at, :] * scales[1][at])
        mixed[s] = (across[0] + across[1].astype(bf16).astype(f32)).astype(bf16)
        pl.when(s != me_s)(give_to(s).start)
    pltpu.make_async_copy(mixed.at[me_s], lanes_of(group), r_recv.at[group]).start()

    to_partner.wait_send()
    for step in range(1, chips):
        px_out(step).wait_send()
        px_pass(step).wait_send()
    for which in range(2):
        owner, _ = gate_from(which)
        for dest in range(faces):
            pl.when((owner == me_f) & (dest != me_f))(gate_copy(which, dest).wait_send)
    for p in range(pieces):
        for kind in range(3):
            owner, _ = weight_from(kind)
            for dest in range(faces):
                pl.when(sends(owner, dest))(
                    weight_copy(kind, p, weight_at(kind, p), dest).wait_send
                )
    for owner in range(strips):
        pltpu.make_async_copy(mixed.at[0], lanes_of(owner), r_recv.at[owner]).wait()
    for step in range(1, strips):
        give(step).wait_send()


def fused_call(faces, strips, px, w_qkv, w_gate_t, decay_rate, beta_bias, tall, wide):
    block, features = px.shape
    count = block * strips
    width = w_qkv.shape[1] * faces // 3 // strips
    units = 2 * count // SPAN
    pieces = 2
    vmem = pl.BlockSpec(memory_space=pltpu.VMEM)
    smem = pl.BlockSpec(memory_space=pltpu.SMEM)
    hbm = pl.BlockSpec(memory_space=pltpu.HBM)
    dma = pltpu.SemaphoreType.DMA
    square = (units, width, width)
    return pl.pallas_call(
        functools.partial(
            fused_kernel, (faces, strips, w_qkv.shape[1] // width, pieces, tall, wide)
        ),
        out_shape=jax.ShapeDtypeStruct((block, strips * width), bf16),
        in_specs=[hbm, hbm, hbm, smem, smem],
        out_specs=pl.BlockSpec(memory_space=pl.ANY),
        scratch_shapes=[
            pltpu.VMEM((count, features), bf16),
            pltpu.VMEM((3, features, width), bf16),
            pltpu.VMEM(w_gate_t.shape, bf16),
            pltpu.VMEM((2, 2 * features // width, width), bf16),
            pltpu.VMEM((2, 2 * features // width, width), bf16),
            pltpu.VMEM((2 * width, features), bf16),
            pltpu.VMEM((LEVELS + 3, width, width), bf16),
            pltpu.VMEM((5, count, width), f32),
            pltpu.VMEM((2, units, SPAN, width), f32),
            pltpu.VMEM((units, 1, width), f32),
            pltpu.VMEM((3,) + square, bf16),
            pltpu.VMEM(square, bf16),
            pltpu.VMEM(square, bf16),
            pltpu.VMEM(square, bf16),
            pltpu.VMEM((units, SPAN, width), bf16),
            pltpu.VMEM((units, SPAN, width), bf16),
            pltpu.VMEM(square, bf16),
            pltpu.VMEM((2, count, width), f32),
            pltpu.VMEM((strips, block, width), bf16),
            dma((strips // 2,)),
            dma((strips // 2,)),
            dma((strips,)),
            dma((3, pieces, faces)),
            dma((3, pieces)),
            dma((2, faces)),
            dma((2,)),
            dma((1,)),
            dma((strips,)),
            dma((strips,)),
        ],
        compiler_params=pltpu.CompilerParams(
            collective_id=2, has_side_effects=True, vmem_limit_bytes=20 * 2**20
        ),
        name="layer",
    )(*[
        pltpu.with_memory_space_constraint(x, pltpu.HBM)
        for x in (px, w_qkv, w_gate_t, decay_rate, beta_bias)
    ])


def fits_fused(strips, heads, dk, count, tall, wide, gate_cols, features, block):
    return (
        heads == 2 * strips
        and dk == SPAN
        and 2 * dk == 128
        and strips & (strips - 1) == 0
        and strips > 1
        and count % (4 * SPAN) == 0
        and count <= 1024
        and block % 16 == 0
        and tall % 8 == 0
        and SPAN % tall == 0
        and wide % (SPAN // tall) == 0
        and gate_cols % 8 == 0
        and features % 1024 == 0
    )


def on_device(faces, strips, pixels_in, w_qkv, w_gate, decay_rate, beta_bias):
    _, rows_here, wide, features = pixels_in.shape
    heads = decay_rate.shape[0]
    block = rows_here * wide
    count = block * strips
    tall = rows_here * strips
    model = w_qkv.shape[1] * faces // 3
    dk = model // heads
    groups = min(strips, heads)
    per_group = heads // groups
    width = per_group * dk
    n_slab = w_qkv.shape[1] // width
    gate_cols = w_gate.shape[1]
    if fits_fused(strips, heads, dk, count, tall, wide, gate_cols, features, block):
        out = fused_call(
            faces, strips, pixels_in.reshape(block, features), w_qkv, w_gate.T,
            decay_rate, beta_bias, tall, wide,
        )
        return out.reshape(1, rows_here, wide, model)
    pieces = 4
    chunk = min(128, count)
    chips = strips // 2
    vmem = pl.BlockSpec(memory_space=pltpu.VMEM)
    dma = pltpu.SemaphoreType.DMA
    if width % 128:
        w_qkv = w_qkv.reshape(features, n_slab, width).transpose(1, 0, 2)
    slabs, gates = pl.pallas_call(
        functools.partial(project_kernel, (faces, strips, groups, n_slab, pieces)),
        out_shape=(
            jax.ShapeDtypeStruct((3, count, width), bf16),
            jax.ShapeDtypeStruct((count // chunk, 2 * heads, chunk), f32),
        ),
        in_specs=[vmem, pl.BlockSpec(memory_space=pl.ANY), vmem],
        out_specs=(vmem, vmem),
        scratch_shapes=[
            pltpu.VMEM((count, features), bf16),
            pltpu.VMEM((3, features, width), bf16),
            pltpu.VMEM((gate_cols, features), f32),
            pltpu.VMEM((faces, gate_cols, features), f32),
            pltpu.VMEM((count, 3 * width), f32),
            dma((chips,)),
            dma((chips,)),
            dma((strips,)),
            dma((3, pieces, 2)),
            dma((3, pieces)),
            dma((faces,)),
            dma((faces,)),
        ],
        compiler_params=pltpu.CompilerParams(collective_id=0, has_side_effects=True),
        name="project",
    )(pixels_in.reshape(block, features), w_qkv, w_gate.T)
    group = group_of(lax.axis_index("strip"), strips, groups)
    first = (group * per_group).astype(jnp.int32).reshape(1)
    mixed = scan_call(
        first, slabs, gates, decay_rate, beta_bias, strips, per_group, tall, wide, dk
    )
    returned = pl.pallas_call(
        functools.partial(return_kernel, strips, groups),
        out_shape=jax.ShapeDtypeStruct((groups, block, width), bf16),
        in_specs=[vmem],
        out_specs=vmem,
        scratch_shapes=[dma((strips,)), dma((groups,))],
        compiler_params=pltpu.CompilerParams(collective_id=1, has_side_effects=True),
        name="give_back",
    )(mixed)
    return returned.transpose(1, 0, 2).reshape(1, rows_here, wide, model)


def solution(mesh):
    in_specs = (P("face", "strip", None, None), P(None, "face"), P(None, "face"), P(), P())
    out_specs = P("face", "strip", None, None)
    return jax.shard_map(
        functools.partial(on_device, mesh.shape["face"], mesh.shape["strip"]),
        mesh=mesh,
        in_specs=in_specs,
        out_specs=out_specs,
        check_vma=False,
    )
```

```python
import functools

import jax
import jax.numpy as jnp
from jax import lax
from jax.experimental import pallas as pl
from jax.experimental.pallas import tpu as pltpu
from jax.sharding import PartitionSpec as P

MESH = pl.DeviceIdType.MESH
f32 = jnp.float32
bf16 = jnp.bfloat16


def group_of(place, strips, groups):
    rep = strips // groups
    if rep > 1 or groups % 2:
        return place // rep
    return jnp.where(lax.rem(place, 2) == 0, place // 2, groups - 1 - place // 2)


def project_kernel(
    cfg, px_ref, wq_ref, wg_ref, slabs_ref, gates_ref,
    px_all, wbuf, wg_own, wg_all, acc, px_send, px_fwd, px_recv, w_send, w_recv, g_send, g_recv,
):
    faces, strips, groups, n_slab, pieces = cfg
    me_f, me_s = lax.axis_index("face"), lax.axis_index("strip")
    block, features = px_ref.shape
    count = strips * block
    width = wbuf.shape[2]
    chips = strips // 2
    core, chip = lax.rem(me_s, 2), me_s // 2
    partner = chip * 2 + (1 - core)
    group = group_of(me_s, strips, groups)
    depth = features // pieces

    def chip_at(step):
        return lax.rem(chip + step, chips) * 2 + core

    barrier = pltpu.get_barrier_semaphore()

    def greet(face, strip):
        pl.semaphore_signal(barrier, inc=1, device_id=(face, strip), device_id_type=MESH)

    greet(me_f, partner)
    for step in range(1, chips):
        greet(me_f, chip_at(step))
    for step in range(1, faces):
        greet(lax.rem(me_f + step, faces), me_s)

    wg_own[...] = wg_ref[...].astype(f32)

    def rows_of(strip):
        return px_all.at[pl.ds(pl.multiple_of(strip * block, block), block)]

    own_px = pltpu.make_async_copy(px_ref, rows_of(me_s), px_recv.at[me_s])
    own_px.start()
    pl.semaphore_wait(barrier, 1 + chips - 1 + faces - 1)

    def weight_from(kind):
        slab = kind * groups + group
        return slab // n_slab, lax.rem(slab, n_slab)

    def weight_src(j, p):
        rows = pl.ds(p * depth, depth)
        if len(wq_ref.shape) == 3:
            return wq_ref.at[j, rows]
        return wq_ref.at[rows, pl.ds(pl.multiple_of(j * width, width), width)]

    def weight_copy(kind, p, src, side):
        return pltpu.make_async_remote_copy(
            src_ref=src,
            dst_ref=wbuf.at[kind, pl.ds(p * depth, depth)],
            send_sem=w_send.at[kind, p, side],
            recv_sem=w_recv.at[kind, p],
            device_id=(me_f + (1 if side else -1), me_s),
            device_id_type=MESH,
        )

    def own_weight(kind, p, j):
        return pltpu.make_async_copy(
            weight_src(j, p), wbuf.at[kind, pl.ds(p * depth, depth)], w_recv.at[kind, p]
        )

    for p in range(pieces):
        for kind in range(3):
            owner, j = weight_from(kind)

            @pl.when(owner == me_f)
            def _(kind=kind, p=p, j=j):
                pl.when(me_f + 1 < faces)(weight_copy(kind, p, weight_src(j, p), 1).start)
                pl.when(me_f > 0)(weight_copy(kind, p, weight_src(j, p), 0).start)
                own_weight(kind, p, j).start()

    def px_copy(dest, sem, source, src):
        return pltpu.make_async_remote_copy(
            src_ref=src,
            dst_ref=rows_of(source),
            send_sem=sem,
            recv_sem=px_recv.at[source],
            device_id=(me_f, dest),
            device_id_type=MESH,
        )

    def px_out(step):
        return px_copy(chip_at(step), px_send.at[step], me_s, px_ref)

    def px_pass(step):
        source = chip_at(step)
        return px_copy(partner, px_fwd.at[step], source, rows_of(source))

    to_partner = px_copy(partner, px_send.at[0], me_s, px_ref)
    for step in range(1, chips):
        px_out(step).start()
    to_partner.start()

    def gate_copy(step):
        return pltpu.make_async_remote_copy(
            src_ref=wg_own,
            dst_ref=wg_all.at[me_f],
            send_sem=g_send.at[step],
            recv_sem=g_recv.at[me_f],
            device_id=(lax.rem(me_f + step, faces), me_s),
            device_id_type=MESH,
        )

    for step in range(1, faces):
        gate_copy(step).start()
    own_gate = pltpu.make_async_copy(wg_own, wg_all.at[me_f], g_recv.at[me_f])
    own_gate.start()

    def px_wait(strip):
        pltpu.make_async_copy(px_ref, rows_of(strip), px_recv.at[strip]).wait()

    def pass_pixels(step):
        px_wait(chip_at(step))
        px_pass(step).start()

    def pass_weights(p):
        for kind in range(3):
            owner, _ = weight_from(kind)
            here = wbuf.at[kind, pl.ds(p * depth, depth)]
            pltpu.make_async_copy(here, here, w_recv.at[kind, p]).wait()
            pl.when((owner < me_f) & (me_f + 1 < faces))(weight_copy(kind, p, here, 1).start)
            pl.when((owner > me_f) & (me_f > 0))(weight_copy(kind, p, here, 0).start)

    tile = min(512, count)

    def each_tile(body):
        if count == tile:
            body(pl.ds(0, tile), 0)
        else:

            def one(i, carry):
                body(pl.ds(pl.multiple_of(i * tile, tile), tile), i)
                return carry

            lax.fori_loop(0, count // tile, one, 0)

    def multiply(p):
        rows = pl.ds(p * depth, depth)
        weights = jnp.concatenate([wbuf[kind, rows, :] for kind in range(3)], axis=1)

        def body(at, _):
            term = jnp.dot(px_all[at, rows], weights, preferred_element_type=f32)
            if p > 0:
                term = term + acc[at, :]
            if p < pieces - 1:
                acc[at, :] = term
            else:
                for kind in range(3):
                    slabs_ref[kind, at, :] = term[
                        :, kind * width : (kind + 1) * width
                    ].astype(bf16)

        each_tile(body)

    for turn in range(max(pieces - 1, chips - 1)):
        if turn < pieces - 1:
            pass_weights(turn)
        if turn < chips - 1:
            pass_pixels(turn + 1)
    px_wait(me_s)
    px_wait(partner)
    for step in range(1, chips):
        px_wait(lax.rem(chip + step, chips) * 2 + (1 - core))
    for face in range(faces):
        pltpu.make_async_copy(wg_own, wg_all.at[face], g_recv.at[face]).wait()
    gate_w = jnp.concatenate([wg_all[face] for face in range(faces)], axis=0).astype(bf16)

    chunk = gates_ref.shape[2]

    def gate_body(at, i):
        logits = lax.dot_general(
            gate_w, px_all[at, :], (((1,), (1,)), ((), ())), preferred_element_type=f32
        )
        logits = logits.astype(bf16).astype(f32)
        for c in range(tile // chunk):
            gates_ref[i * (tile // chunk) + c] = logits[:, c * chunk : (c + 1) * chunk]

    each_tile(gate_body)
    for p in range(pieces - 1):
        multiply(p)
    pass_weights(pieces - 1)
    multiply(pieces - 1)

    to_partner.wait_send()
    for step in range(1, chips):
        px_out(step).wait_send()
        px_pass(step).wait_send()
    for step in range(1, faces):
        gate_copy(step).wait_send()
    for p in range(pieces):
        for kind in range(3):
            owner, _ = weight_from(kind)
            here = wbuf.at[kind, pl.ds(p * depth, depth)]
            pl.when((owner <= me_f) & (me_f + 1 < faces))(
                weight_copy(kind, p, here, 1).wait_send
            )
            pl.when((owner >= me_f) & (me_f > 0))(weight_copy(kind, p, here, 0).wait_send)


def mm(a, b, dims=((1,), (0,))):
    return lax.dot_general(
        a.astype(bf16), b.astype(bf16), (dims, ((), ())), preferred_element_type=f32
    )


def split_mm(exact, wide, pieces):
    exact = exact.astype(bf16)
    total, rest = None, wide
    for _ in range(pieces):
        piece = rest.astype(bf16)
        rest = rest - piece.astype(f32)
        term = jnp.dot(exact, piece, preferred_element_type=f32)
        total = term if total is None else total + term
    return total


def mm_split(wide, exact, pieces):
    exact = exact.astype(bf16)
    total, rest = None, wide
    for _ in range(pieces):
        piece = rest.astype(bf16)
        rest = rest - piece.astype(f32)
        term = jnp.dot(piece, exact, preferred_element_type=f32)
        total = term if total is None else total + term
    return total


def scan_kernel(
    cfg, first_ref, slabs_ref, gates_ref, rate_ref, bias_ref, out_ref,
    feats, gates, row_buf, col_buf, states,
):
    chunk, per_group, tall, wide, dk = cfg
    count, width = slabs_ref.shape[1:]
    strips, block, _ = out_ref.shape
    heads = gates_ref.shape[1] // 2
    first = first_ref[0]

    lane = lax.broadcasted_iota(jnp.int32, (width, width), 1)
    sub = lax.broadcasted_iota(jnp.int32, (width, width), 0)
    same_head = (lane // dk) == (sub // dk)
    head_ones = same_head.astype(f32)
    ti = lax.broadcasted_iota(jnp.int32, (chunk, chunk), 0)
    tj = lax.broadcasted_iota(jnp.int32, (chunk, chunk), 1)
    inclusive = ti >= tj
    tri = inclusive.astype(f32)
    eye = (ti == tj).astype(f32)

    def prepare(i, carry):
        at = pl.ds(pl.multiple_of(i * chunk, chunk), chunk)
        for kind in range(3):
            x = slabs_ref[kind, at, :].astype(f32)
            if kind < 2:
                x = x * lax.rsqrt(mm_split(x * x, head_ones, 2) + 1e-06)
            feats[kind, at, :] = x
        for a in range(per_group):
            head = first + a
            decay = -rate_ref[head] * jnp.exp(gates_ref[i, pl.ds(head, 1), :])
            strength = jax.nn.sigmoid(gates_ref[i, pl.ds(heads + head, 1), :] + bias_ref[head])
            gates[a, at, :] = jnp.broadcast_to(decay, (chunk, chunk)).T
            gates[per_group + a, at, :] = jnp.broadcast_to(strength, (chunk, chunk)).T
        return carry

    lax.fori_loop(0, count // chunk, prepare, 0, unroll=count // chunk <= 4)

    columns = chunk // tall
    flane = lax.broadcasted_iota(jnp.int32, (chunk, width), 1) // dk

    def lanes_of(parts):
        out = parts[0][:, :width]
        for a in range(1, per_group):
            out = jnp.where(flane == a, parts[a][:, :width], out)
        return out

    def stacked(x):
        if per_group == 1:
            return x
        return jnp.concatenate(
            [jnp.where(flane == a, x, jnp.zeros_like(x)) for a in range(per_group)], axis=0
        )

    def side_by_side(parts):
        return parts[0] if per_group == 1 else jnp.concatenate(parts, axis=1)

    def load(ref, which, i, by_column):
        if not by_column:
            return ref[which, pl.ds(pl.multiple_of(i * chunk, chunk), chunk), :]
        return jnp.concatenate(
            [ref[which, pl.ds(i * columns + c, tall, stride=wide), :] for c in range(columns)],
            axis=0,
        )

    states[...] = jnp.zeros_like(states)

    def advance(i, carry):
        work = []
        for order in range(2):
            q, k, v = (load(feats, kind, i, order) for kind in range(3))
            cums, betas, systems, scores = [], [], [], []
            for a in range(per_group):
                cum = split_mm(tri, load(gates, a, i, order), 3)
                beta = load(gates, per_group + a, i, order)
                gap = cum - cum.T
                within = jnp.where(inclusive, jnp.exp(jnp.where(inclusive, gap, 0.0)), 0.0)
                k_a = k if per_group == 1 else jnp.where(flane == a, k, 0.0)
                q_a = q if per_group == 1 else jnp.where(flane == a, q, 0.0)
                dots = mm(jnp.concatenate([k_a, q_a], axis=0), k, ((1,), (1,)))
                systems.append(within * dots[:chunk] * beta)
                scores.append(within * dots[chunk:])
                cums.append(cum)
                betas.append(beta)
            work.append((q, k, v, cums, betas, systems, scores))

        inverses = [[None] * per_group for _ in range(2)]
        half = 1
        while half < chunk:
            here = ((ti // (2 * half)) == (tj // (2 * half))) & (
                (lax.rem(ti, 2 * half) >= half) & (lax.rem(tj, 2 * half) < half)
            )
            lows = [
                [jnp.where(here, work[o][5][a], 0.0) for a in range(per_group)] for o in range(2)
            ]
            if half == 1:
                inverses = [[eye - low for low in row] for row in lows]
            else:
                firsts = [
                    [mm(lows[o][a], inverses[o][a]) for a in range(per_group)] for o in range(2)
                ]
                inverses = [
                    [inverses[o][a] - mm(inverses[o][a], firsts[o][a]) for a in range(per_group)]
                    for o in range(2)
                ]
            half *= 2

        for order in range(2):
            q, k, v, cums, betas, _, scores = work[order]
            beta = lanes_of(betas)
            cum = lanes_of(cums)
            scale = jnp.exp(cum)
            last = cum[chunk - 1 : chunk, :]
            tail = jnp.exp(last - cum)
            both = side_by_side(inverses[order])
            u = mm(both, stacked(v * beta))
            w = mm(both, stacked(k * (beta * scale)))
            state = states[order]
            fresh = u - mm(w, state)
            out = mm(q * scale, state) + mm(side_by_side(scores), stacked(fresh))
            grown = mm(k * tail, fresh, ((0,), (0,)))
            decayed = state * jnp.exp(last)
            states[order] = decayed + jnp.where(same_head, grown, 0.0)
            normed = out * lax.rsqrt(mm_split(out * out, head_ones, 2) * (1.0 / dk) + 1e-06)
            if order == 0:
                row_buf[pl.ds(pl.multiple_of(i * chunk, chunk), chunk), :] = normed
            else:
                normed = normed.astype(bf16).astype(f32)
                for c in range(columns):
                    col_buf[pl.ds(i * columns + c, tall, stride=wide), :] = normed[
                        c * tall : (c + 1) * tall
                    ]
        return carry

    lax.fori_loop(0, count // chunk, advance, 0)

    def finish(s, carry):
        at = pl.ds(s * block, block)
        out_ref[s] = (row_buf[at, :] + col_buf[at, :]).astype(bf16)
        return carry

    lax.fori_loop(0, strips, finish, 0)


def return_kernel(strips, groups, mixed_ref, out_ref, send_sem, recv_sem):
    me_f, me_s = lax.axis_index("face"), lax.axis_index("strip")
    rep = strips // groups
    barrier = pltpu.get_barrier_semaphore()
    for step in range(1, strips):
        pl.semaphore_signal(
            barrier, inc=1, device_id=(me_f, lax.rem(me_s + step, strips)), device_id_type=MESH
        )
    pl.semaphore_wait(barrier, strips - 1)
    mine = group_of(me_s, strips, groups)
    sends = lax.rem(me_s, rep) == 0

    def copy(step):
        dest = lax.rem(me_s + step, strips)
        return pltpu.make_async_remote_copy(
            src_ref=mixed_ref.at[dest],
            dst_ref=out_ref.at[mine],
            send_sem=send_sem.at[step],
            recv_sem=recv_sem.at[mine],
            device_id=(me_f, dest),
            device_id_type=MESH,
        )

    @pl.when(sends)
    def _():
        for step in range(1, strips):
            copy(step).start()
        pltpu.make_async_copy(mixed_ref.at[me_s], out_ref.at[mine], recv_sem.at[mine]).start()
        for step in range(1, strips):
            copy(step).wait_send()

    for group in range(groups):
        pltpu.make_async_copy(mixed_ref.at[0], out_ref.at[group], recv_sem.at[group]).wait()


def scan_call(
    first, slabs, gates, decay_rate, beta_bias, strips, per_group, tall, wide, dk
):
    count, width = slabs.shape[1:]
    block = count // strips
    chunk = min(128, count)
    vmem = pl.BlockSpec(memory_space=pltpu.VMEM)
    smem = pl.BlockSpec(memory_space=pltpu.SMEM)
    return pl.pallas_call(
        functools.partial(scan_kernel, (chunk, per_group, tall, wide, dk)),
        out_shape=jax.ShapeDtypeStruct((strips, block, width), bf16),
        in_specs=[smem, vmem, vmem, smem, smem],
        out_specs=vmem,
        scratch_shapes=[
            pltpu.VMEM((3, count, width), f32),
            pltpu.VMEM((2 * per_group, count, chunk), f32),
            pltpu.VMEM((count, width), f32),
            pltpu.VMEM((count, width), f32),
            pltpu.VMEM((2, width, width), f32),
        ],
        name="scans",
    )(first, slabs, gates, decay_rate, beta_bias)


LEVELS = 6
SPAN = 1 << LEVELS


def fused_kernel(
    cfg, px_ref, wq_ref, wg_ref, rate_ref, bias_ref, out_ref,
    px_all, wbuf, wg_own, g_out, g_in, g_rows, masks, flat, ordered, cums, sides,
    inv, into, trans, reads, asks, states, outs, mixed,
    px_send, px_fwd, px_recv, w_send, w_recv, g_send, g_recv, wg_sem, r_send, r_recv,
):
    faces, strips, n_slab, pieces, tall, wide = cfg
    me_f, me_s = lax.axis_index("face"), lax.axis_index("strip")
    block, features = px_ref.shape
    count = strips * block
    width = wbuf.shape[2]
    dk = width // 2
    heads = rate_ref.shape[0]
    gate_cols = wg_ref.shape[0]
    chips = strips // 2
    core, chip = lax.rem(me_s, 2), me_s // 2
    partner = chip * 2 + (1 - core)
    group = group_of(lax.rem(me_s + strips // 2, strips), strips, strips)
    depth = features // pieces
    spans = count // SPAN
    columns = SPAN // tall

    barrier = pltpu.get_barrier_semaphore()
    for step in range(1, strips):
        pl.semaphore_signal(
            barrier, inc=1, device_id=(me_f, lax.rem(me_s + step, strips)), device_id_type=MESH
        )
    for step in range(1, faces):
        pl.semaphore_signal(
            barrier, inc=1, device_id=(lax.rem(me_f + step, faces), me_s), device_id_type=MESH
        )

    def chip_at(step, on=None):
        other, bit = chip, 1
        while bit < chips:
            if step & bit:
                other = other + bit - 2 * bit * lax.rem(other // bit, 2)
            bit *= 2
        return other * 2 + (core if on is None else on)

    def rows_of(strip):
        return px_all.at[pl.ds(pl.multiple_of(strip * block, block), block)]

    def weight_from(kind):
        slab = kind * strips + group
        return slab // n_slab, lax.rem(slab, n_slab)

    def weight_src(j, p):
        return wq_ref.at[pl.ds(p * depth, depth), pl.ds(pl.multiple_of(j * width, width), width)]

    def weight_at(kind, p):
        return wbuf.at[kind, pl.ds(p * depth, depth)]

    def weight_copy(kind, p, src, dest):
        return pltpu.make_async_remote_copy(
            src_ref=src,
            dst_ref=weight_at(kind, p),
            send_sem=w_send.at[kind, p, dest],
            recv_sem=w_recv.at[kind, p],
            device_id=(dest, me_s),
            device_id_type=MESH,
        )

    def own_weight(kind, p, j):
        return pltpu.make_async_copy(weight_src(j, p), weight_at(kind, p), w_recv.at[kind, p])

    def weight_wait(kind, p):
        here = weight_at(kind, p)
        pltpu.make_async_copy(here, here, w_recv.at[kind, p]).wait()

    def relays(owner, dest):
        up = (dest == me_f + 1) & (owner == me_f - 1)
        return up | ((dest == me_f - 1) & (owner == me_f + 1))

    def direct(owner, dest, far):
        gap = jnp.abs(dest - me_f)
        return (owner == me_f) & ((gap > 2) if far else (gap == 1))

    def sends(owner, dest):
        return direct(owner, dest, False) | direct(owner, dest, True) | relays(owner, dest)

    def gate_from(which):
        column = which * heads + group * 2
        return column // gate_cols, lax.rem(column, gate_cols)

    def gate_copy(which, dest):
        return pltpu.make_async_remote_copy(
            src_ref=g_out.at[which],
            dst_ref=g_in.at[which],
            send_sem=g_send.at[which, dest],
            recv_sem=g_recv.at[which],
            device_id=(dest, me_s),
            device_id_type=MESH,
        )

    lines = features // width

    def pick_gates():
        here = wg_own[...].astype(f32)
        row_of = lax.broadcasted_iota(jnp.int32, here.shape, 0)
        for which in range(2):
            owner, row = gate_from(which)

            @pl.when(owner == me_f)
            def _(which=which, row=row):
                picked = [
                    jnp.sum(jnp.where(row_of == row + a, here, 0.0), axis=0, keepdims=True)
                    for a in range(2)
                ]
                parts = [
                    picked[a][:, i * width : (i + 1) * width]
                    for a in range(2)
                    for i in range(lines)
                ]
                g_out[which] = jnp.concatenate(parts, axis=0).astype(bf16)

    def send_gates():
        for which in range(2):
            owner, _ = gate_from(which)

            @pl.when(owner == me_f)
            def _(which=which):
                for dest in range(faces):
                    pl.when(dest != me_f)(gate_copy(which, dest).start)
                pltpu.make_async_copy(g_out.at[which], g_in.at[which], g_recv.at[which]).start()

    own_px = pltpu.make_async_copy(px_ref, rows_of(me_s), px_recv.at[me_s])
    own_px.start()
    own_gate = pltpu.make_async_copy(wg_ref, wg_own, wg_sem.at[0])
    own_gate.start()
    own_gate.wait()
    pick_gates()
    pl.semaphore_wait(barrier, strips - 1 + faces - 1)
    send_gates()

    def send_weights(kind, far):
        owner, j = weight_from(kind)

        @pl.when(owner == me_f)
        def _():
            for p in range(pieces):
                for dest in range(faces):
                    pl.when(direct(owner, dest, far))(
                        weight_copy(kind, p, weight_src(j, p), dest).start
                    )

    def own_weights(kind):
        owner, j = weight_from(kind)

        @pl.when(owner == me_f)
        def _():
            for p in range(pieces):
                own_weight(kind, p, j).start()

    send_weights(1, False)
    send_weights(1, True)
    def px_copy(dest, sem, source, src):
        return pltpu.make_async_remote_copy(
            src_ref=src,
            dst_ref=rows_of(source),
            send_sem=sem,
            recv_sem=px_recv.at[source],
            device_id=(me_f, dest),
            device_id_type=MESH,
        )

    def px_out(step):
        return px_copy(chip_at(step), px_send.at[step], me_s, px_ref)

    def px_pass(step):
        source = chip_at(step)
        return px_copy(partner, px_fwd.at[step], source, rows_of(source))

    to_partner = px_copy(partner, px_send.at[0], me_s, px_ref)
    for step in range(1, chips):
        px_out(step).start()
    to_partner.start()
    own_weights(1)

    ti = lax.broadcasted_iota(jnp.int32, (width, width), 0)
    tj = lax.broadcasted_iota(jnp.int32, (width, width), 1)
    for level in range(LEVELS):
        half = 1 << level
        here = (ti // (2 * half)) == (tj // (2 * half))
        here = here & (lax.rem(ti, 2 * half) >= half) & (lax.rem(tj, 2 * half) < half)
        masks[level] = here.astype(f32).astype(bf16)
    eye = (ti == tj).astype(f32)
    masks[LEVELS] = eye.astype(bf16)
    same_head = (ti // dk) == (tj // dk)
    masks[LEVELS + 1] = same_head.astype(f32).astype(bf16)
    tri = same_head & (ti >= tj)
    masks[LEVELS + 2] = tri.astype(f32).astype(bf16)

    def px_wait(strip):
        pltpu.make_async_copy(px_ref, rows_of(strip), px_recv.at[strip]).wait()

    def pass_pixels(step):
        px_wait(chip_at(step))
        px_pass(step).start()

    def relayed(owner):
        return (jnp.abs(owner - me_f) == 1) & (
            ((2 * me_f - owner) >= 0) & ((2 * me_f - owner) < faces)
        )

    def pass_weights(kind, p):
        owner, _ = weight_from(kind)

        @pl.when(relayed(owner))
        def _():
            weight_wait(kind, p)
            for dest in range(faces):
                pl.when(relays(owner, dest))(weight_copy(kind, p, weight_at(kind, p), dest).start)

    for p in range(pieces):
        pass_weights(1, p)
    for kind in (0, 2):
        send_weights(kind, False)
    for kind in (0, 2):
        own_weights(kind)
    upper = me_f * 2 >= faces

    def early(p):
        pl.when(upper)(functools.partial(pass_weights, 2, p))
        pl.when(jnp.logical_not(upper))(functools.partial(pass_weights, 0, p))

    def late(p):
        pl.when(upper)(functools.partial(pass_weights, 0, p))
        pl.when(jnp.logical_not(upper))(functools.partial(pass_weights, 2, p))

    for p in range(pieces):
        early(p)
    for step in range(1, chips):
        pass_pixels(step)
    for which in range(2):
        pltpu.make_async_copy(g_in.at[which], g_in.at[which], g_recv.at[which]).wait()
        got = g_in[which].astype(f32)
        for a in range(2):
            for i in range(lines):
                line = got[a * lines + i : a * lines + i + 1, :]
                at = which * width + a * dk
                g_rows[at : at + dk, i * width : (i + 1) * width] = jnp.broadcast_to(
                    line, (dk, width)
                ).astype(bf16)
    px_wait(me_s)
    px_wait(partner)
    for step in range(1, chips):
        px_wait(chip_at(step, 1 - core))

    lane = lax.broadcasted_iota(jnp.int32, (1, width), 1) // dk
    first = group * 2

    def by_head(ref):
        return jnp.where(lane == 0, ref[first], ref[first + 1])

    logits = lax.dot_general(
        px_all[...], g_rows[...], (((1,), (1,)), ((), ())), preferred_element_type=f32
    )
    logits = logits.astype(bf16).astype(f32)
    flat[0] = -by_head(rate_ref) * jnp.exp(logits[:, :width])
    flat[1] = jax.nn.sigmoid(logits[:, width:] + by_head(bias_ref))

    head_ones = masks[LEVELS + 1]

    def features_of(kind):
        owner, _ = weight_from(kind)
        for p in range(pieces):
            pl.when(jnp.logical_not(relayed(owner)))(functools.partial(weight_wait, kind, p))
        if kind == 1:
            for late in (0, 2):
                send_weights(late, True)
        x = jnp.dot(px_all[...], wbuf[kind], preferred_element_type=f32)
        x = x.astype(bf16).astype(f32)
        if kind < 2:
            x = x * lax.rsqrt(mm(x * x, head_ones) + 1e-06)
        flat[2 + kind] = x

    def rows_at(i):
        return pl.ds(i * SPAN if isinstance(i, int) else pl.multiple_of(i * SPAN, SPAN), SPAN)

    def load(which, i, by_column):
        if not by_column:
            return flat[which, rows_at(i), :]
        return jnp.concatenate(
            [flat[which, pl.ds(i * columns + c, tall, stride=wide), :] for c in range(columns)],
            axis=0,
        )

    half_masks = [(lane == a).astype(f32).astype(bf16) for a in range(2)]

    def stacked(x):
        x = x.astype(bf16)
        return jnp.concatenate([x * half_masks[0], x * half_masks[1]], axis=0)

    def twice(x):
        return jnp.concatenate([x, x], axis=0)

    def slot(i, o):
        return i * 2 + o

    ri = lax.broadcasted_iota(jnp.int32, (SPAN, width), 0)
    rj = lax.rem(lax.broadcasted_iota(jnp.int32, (SPAN, width), 1), dk)
    inclusive = ri >= rj

    units_all = [(i, o) for i in range(spans) for o in range(2)]

    def each_span(body, per_turn):
        def turn(t, carry):
            body([(t * per_turn + u, o) for u in range(per_turn) for o in range(2)])
            return carry

        lax.fori_loop(0, spans // per_turn, turn, 0)

    def key_stage(units):
        lows, tails, kbs = [], [], []
        for i, o in units:
            decay, beta, k = load(0, i, o), load(1, i, o), load(3, i, o)
            cum = split_mm(masks[LEVELS + 2], twice(decay), 3)[:SPAN]
            turned = twice(cum).T
            across = jnp.where(lane == 0, turned[0:1, :], turned[dk : dk + 1, :])
            gap = cum - across
            within = jnp.exp(jnp.where(inclusive, gap, -1e30))
            ks = stacked(k)
            gram = mm(k, ks, ((1,), (1,)))
            lows.append(twice((within * gram * beta).astype(bf16)))
            scale = jnp.exp(cum)
            last = cum[SPAN - 1 : SPAN, :]
            tails.append(stacked(k * jnp.exp(last - cum)))
            kb = stacked(k * (beta * scale))
            kbs.append(kb)
            at = slot(i, o)
            cums[at] = jnp.exp(last)
            ordered[0, at] = scale
            ordered[1, at] = within
            sides[0, at] = ks
            sides[1, at] = kb
        xs = [masks[LEVELS] - low * masks[0] for low in lows]
        for level in range(1, LEVELS):
            mids = [mm(low * masks[level], x) for low, x in zip(lows, xs)]
            ends = [mm(x, mid) for x, mid in zip(xs, mids)]
            xs = [x - end.astype(bf16) for x, end in zip(xs, ends)]
        hs = [mm(tail, x, ((0,), (0,))).astype(bf16) for tail, x in zip(tails, xs)]
        ms = [mm(h, kb).astype(bf16) for h, kb in zip(hs, kbs)]
        for (i, o), x, h, m in zip(units, xs, hs, ms):
            at = slot(i, o)
            inv[at] = x
            into[at] = h
            trans[at] = m

    def query_stage(units):
        for i, o in units:
            at = slot(i, o)
            q = load(2, i, o)
            scores = ordered[1, at] * mm(q, sides[0, at], ((1,), (1,)))
            g = mm(scores, inv[at]).astype(bf16)
            reads[at] = g
            asks[at] = (q * ordered[0, at] - mm(g, sides[1, at])).astype(bf16)

    def output_stage(units):
        for i, o in units:
            at = slot(i, o)
            out = mm(reads[at], sides[2, at]) + mm(asks[at], states[at])
            if o == 0:
                outs[0, rows_at(i), :] = out
            else:
                for c in range(columns):
                    outs[1, pl.ds(i * columns + c, tall, stride=wide), :] = out[
                        c * tall : (c + 1) * tall
                    ]

    def value_scan(finish):
        features_of(2)
        state = [jnp.zeros((width, width), f32) for _ in range(2)]
        for i in range(spans):
            for o in range(2):
                at = slot(i, o)
                vb = stacked(load(4, i, o) * load(1, i, o))
                sides[2, at] = vb
                held = state[o].astype(bf16)
                states[at] = held
                if i < spans - 1:
                    wrote = mm(into[at], vb)
                    state[o] = state[o] * cums[at] + (wrote - mm(trans[at], held))
                if finish:
                    output_stage([(i, o)])

    queries_last = me_f * 2 >= faces
    features_of(1)
    for p in range(pieces):
        late(p)
    key_stage(units_all)
    pl.when(queries_last)(functools.partial(value_scan, False))
    features_of(0)
    each_span(query_stage, 4)
    pl.when(jnp.logical_not(queries_last))(functools.partial(value_scan, True))

    pl.when(queries_last)(functools.partial(each_span, output_stage, 8))
    def lanes_of(owner):
        return out_ref.at[:, pl.ds(pl.multiple_of(owner * width, width), width)]

    def give(step):
        return give_to(lax.rem(me_s + step, strips))

    def give_to(dest):
        return pltpu.make_async_remote_copy(
            src_ref=mixed.at[dest],
            dst_ref=lanes_of(group),
            send_sem=r_send.at[dest],
            recv_sem=r_recv.at[group],
            device_id=(me_f, dest),
            device_id_type=MESH,
        )

    squares = [outs[o] * outs[o] for o in range(2)]
    scales = [lax.rsqrt(mm(x, head_ones) * (1.0 / dk) + 1e-06) for x in squares]
    for s in range(strips):
        at = slice(s * block, (s + 1) * block)
        across = (outs[0, at, :] * scales[0][at], outs[1, at, :] * scales[1][at])
        mixed[s] = (across[0] + across[1].astype(bf16).astype(f32)).astype(bf16)
        pl.when(s != me_s)(give_to(s).start)
    pltpu.make_async_copy(mixed.at[me_s], lanes_of(group), r_recv.at[group]).start()

    to_partner.wait_send()
    for step in range(1, chips):
        px_out(step).wait_send()
        px_pass(step).wait_send()
    for which in range(2):
        owner, _ = gate_from(which)
        for dest in range(faces):
            pl.when((owner == me_f) & (dest != me_f))(gate_copy(which, dest).wait_send)
    for p in range(pieces):
        for kind in range(3):
            owner, _ = weight_from(kind)
            for dest in range(faces):
                pl.when(sends(owner, dest))(
                    weight_copy(kind, p, weight_at(kind, p), dest).wait_send
                )
    for owner in range(strips):
        pltpu.make_async_copy(mixed.at[0], lanes_of(owner), r_recv.at[owner]).wait()
    for step in range(1, strips):
        give(step).wait_send()


def fused_call(faces, strips, px, w_qkv, w_gate_t, decay_rate, beta_bias, tall, wide):
    block, features = px.shape
    count = block * strips
    width = w_qkv.shape[1] * faces // 3 // strips
    units = 2 * count // SPAN
    pieces = 2
    vmem = pl.BlockSpec(memory_space=pltpu.VMEM)
    smem = pl.BlockSpec(memory_space=pltpu.SMEM)
    hbm = pl.BlockSpec(memory_space=pltpu.HBM)
    dma = pltpu.SemaphoreType.DMA
    square = (units, width, width)
    return pl.pallas_call(
        functools.partial(
            fused_kernel, (faces, strips, w_qkv.shape[1] // width, pieces, tall, wide)
        ),
        out_shape=jax.ShapeDtypeStruct((block, strips * width), bf16),
        in_specs=[hbm, hbm, hbm, smem, smem],
        out_specs=pl.BlockSpec(memory_space=pl.ANY),
        scratch_shapes=[
            pltpu.VMEM((count, features), bf16),
            pltpu.VMEM((3, features, width), bf16),
            pltpu.VMEM(w_gate_t.shape, bf16),
            pltpu.VMEM((2, 2 * features // width, width), bf16),
            pltpu.VMEM((2, 2 * features // width, width), bf16),
            pltpu.VMEM((2 * width, features), bf16),
            pltpu.VMEM((LEVELS + 3, width, width), bf16),
            pltpu.VMEM((5, count, width), f32),
            pltpu.VMEM((2, units, SPAN, width), f32),
            pltpu.VMEM((units, 1, width), f32),
            pltpu.VMEM((3,) + square, bf16),
            pltpu.VMEM(square, bf16),
            pltpu.VMEM(square, bf16),
            pltpu.VMEM(square, bf16),
            pltpu.VMEM((units, SPAN, width), bf16),
            pltpu.VMEM((units, SPAN, width), bf16),
            pltpu.VMEM(square, bf16),
            pltpu.VMEM((2, count, width), f32),
            pltpu.VMEM((strips, block, width), bf16),
            dma((strips // 2,)),
            dma((strips // 2,)),
            dma((strips,)),
            dma((3, pieces, faces)),
            dma((3, pieces)),
            dma((2, faces)),
            dma((2,)),
            dma((1,)),
            dma((strips,)),
            dma((strips,)),
        ],
        compiler_params=pltpu.CompilerParams(
            collective_id=2, has_side_effects=True, vmem_limit_bytes=20 * 2**20
        ),
        name="layer",
    )(*[
        pltpu.with_memory_space_constraint(x, pltpu.HBM)
        for x in (px, w_qkv, w_gate_t, decay_rate, beta_bias)
    ])


def fits_fused(strips, heads, dk, count, tall, wide, gate_cols, features, block):
    return (
        heads == 2 * strips
        and dk == SPAN
        and 2 * dk == 128
        and strips & (strips - 1) == 0
        and strips > 1
        and count % (4 * SPAN) == 0
        and count <= 1024
        and block % 16 == 0
        and tall % 8 == 0
        and SPAN % tall == 0
        and wide % (SPAN // tall) == 0
        and gate_cols % 8 == 0
        and features % 1024 == 0
    )


def on_device(faces, strips, pixels_in, w_qkv, w_gate, decay_rate, beta_bias):
    _, rows_here, wide, features = pixels_in.shape
    heads = decay_rate.shape[0]
    block = rows_here * wide
    count = block * strips
    tall = rows_here * strips
    model = w_qkv.shape[1] * faces // 3
    dk = model // heads
    groups = min(strips, heads)
    per_group = heads // groups
    width = per_group * dk
    n_slab = w_qkv.shape[1] // width
    gate_cols = w_gate.shape[1]
    if fits_fused(strips, heads, dk, count, tall, wide, gate_cols, features, block):
        out = fused_call(
            faces, strips, pixels_in.reshape(block, features), w_qkv, w_gate.T,
            decay_rate, beta_bias, tall, wide,
        )
        return out.reshape(1, rows_here, wide, model)
    pieces = 4
    chunk = min(128, count)
    chips = strips // 2
    vmem = pl.BlockSpec(memory_space=pltpu.VMEM)
    dma = pltpu.SemaphoreType.DMA
    if width % 128:
        w_qkv = w_qkv.reshape(features, n_slab, width).transpose(1, 0, 2)
    slabs, gates = pl.pallas_call(
        functools.partial(project_kernel, (faces, strips, groups, n_slab, pieces)),
        out_shape=(
            jax.ShapeDtypeStruct((3, count, width), bf16),
            jax.ShapeDtypeStruct((count // chunk, 2 * heads, chunk), f32),
        ),
        in_specs=[vmem, pl.BlockSpec(memory_space=pl.ANY), vmem],
        out_specs=(vmem, vmem),
        scratch_shapes=[
            pltpu.VMEM((count, features), bf16),
            pltpu.VMEM((3, features, width), bf16),
            pltpu.VMEM((gate_cols, features), f32),
            pltpu.VMEM((faces, gate_cols, features), f32),
            pltpu.VMEM((count, 3 * width), f32),
            dma((chips,)),
            dma((chips,)),
            dma((strips,)),
            dma((3, pieces, 2)),
            dma((3, pieces)),
            dma((faces,)),
            dma((faces,)),
        ],
        compiler_params=pltpu.CompilerParams(collective_id=0, has_side_effects=True),
        name="project",
    )(pixels_in.reshape(block, features), w_qkv, w_gate.T)
    group = group_of(lax.axis_index("strip"), strips, groups)
    first = (group * per_group).astype(jnp.int32).reshape(1)
    mixed = scan_call(
        first, slabs, gates, decay_rate, beta_bias, strips, per_group, tall, wide, dk
    )
    returned = pl.pallas_call(
        functools.partial(return_kernel, strips, groups),
        out_shape=jax.ShapeDtypeStruct((groups, block, width), bf16),
        in_specs=[vmem],
        out_specs=vmem,
        scratch_shapes=[dma((strips,)), dma((groups,))],
        compiler_params=pltpu.CompilerParams(collective_id=1, has_side_effects=True),
        name="give_back",
    )(mixed)
    return returned.transpose(1, 0, 2).reshape(1, rows_here, wide, model)


def solution(mesh):
    in_specs = (P("face", "strip", None, None), P(None, "face"), P(None, "face"), P(), P())
    out_specs = P("face", "strip", None, None)
    return jax.shard_map(
        functools.partial(on_device, mesh.shape["face"], mesh.shape["strip"]),
        mesh=mesh,
        in_specs=in_specs,
        out_specs=out_specs,
        check_vma=False,
    )
```
